32 devices in a mesh: section: 4 (over y, x), coil: 4 (over z), cuts: 2 (over core).
Axes of the slice: x: 2, y: 2, z: 4, core: 2. Of those that a mesh axis runs over, the one named last changes fastest.
Arguments:
- initial: bfloat16 [2, 32, 80, 2, 128], P(None, 'coil', 'cuts'), may hold values from -6 to 6
- sens: bfloat16 [2, 8, 32, 80, 2, 128], P(None, ('coil', 'cuts')), may hold values from -2.5 to 2.5
- kspace: bfloat16 [2, 8, 32, 80, 2, 128], P(None, ('coil', 'cuts')), may hold values from -6 to 6
- mask: int32 [2, 80, 128], replicated, may hold values 0 or 1
- step_sizes: float32 [4], P('section'), may hold values from 0.3 to 1.5
- conv_in: bfloat16 [4, 128, 18], P('section'), may hold values from -1.5 to 1.5
- bias_in: float32 [4, 128], P('section'), may hold values from -3 to 3
- conv_out: bfloat16 [4, 18, 128], P('section'), may hold values from -0.1875 to 0.1875
Outputs:
- cascade_images: bfloat16 [4, 2, 32, 80, 2, 128], P('section', None, 'coil', 'cuts')
The draws below stay inside these ranges and needn't reach their ends.
Inputs may be any that keep to these rules, and one draw needn't show every extreme that they name: `mask`: 1 marks a sampled phase-encoding line of the slab, 0 one that was not measured.
All inputs are finite; a program needn't handle non-finite values.
Results may differ from the reference program's by a relative error of at most 0.028.
Values may be sent and summed in bfloat16 or wider, within the bound.
No kernel may reach another device: no remote copies, remote signals or barrier semaphores. Data moves between devices by JAX's collectives and lax.ppermute only.
A program may use at most 128 MiB of HBM per device.

```python
import math
import jax
import jax.numpy as jnp
from jax import lax

X = 32
Y = 80
Z = 128
HID = 128
SLABS = 2
COILS = 8
CASCADES = 4


def set_ends(drawn, rng, smallest, largest):
    longest = drawn.shape.index(max(drawn.shape))
    spots = []
    for shift in (0, 1):
        where = [jax.random.randint(jax.random.fold_in(rng, axis), (), 0, length) for axis, length in enumerate(drawn.shape)]
        where[longest] = (where[longest] + shift) % drawn.shape[longest]
        spots.append(tuple(where))
    return drawn.at[spots[0]].set(smallest).at[spots[1]].set(largest)


def with_spikes(drawn, rng, source, target, blocks, factor):
    def block_of(axis_at):
        return (jnp.arange(drawn.shape[axis_at]) // (drawn.shape[axis_at] // blocks)).reshape((-1,) + (1,) * (drawn.ndim - 1 - axis_at))

    one_side = jax.random.permutation(rng, blocks)[block_of(target)]
    second = (block_of(target) + blocks // 2) % blocks
    return jnp.where((block_of(source) == one_side) | (block_of(source) == second), factor * drawn, drawn)


def block_levels(stream_key, shape, cuts, smallest, largest):
    factor_of, own = 1.0, jax.random.fold_in(stream_key, 6)
    for dim, parts in cuts:
        heights = jnp.exp(jax.random.uniform(jax.random.fold_in(own, dim), (parts,), jnp.float32, smallest / len(cuts), largest / len(cuts)))
        factor_of = factor_of * jnp.repeat(heights, shape[dim] // parts).reshape([-1 if axis == dim else 1 for axis in range(len(shape))])
    return factor_of


def centred(own_key, extent, scale, bound, cuts=(), held_as=jnp.bfloat16):
    loudness = block_levels(own_key, extent, cuts, -0.22, 0.18) if cuts else 1.0
    drawn = jax.random.normal(own_key, extent, jnp.float32) * scale * loudness
    return jnp.minimum(jnp.maximum(drawn, -bound), bound).astype(held_as)


def heavy_noise(stream_key, extent, scale, bound, pieces, heavy, kind=jnp.bfloat16):
    entries = scale * jax.random.normal(stream_key, extent, jnp.float32)
    if pieces:
        entries = entries * block_levels(stream_key, extent, pieces, -0.22, 0.18)
    return jnp.clip(with_spikes(entries, jax.random.fold_in(stream_key, 3), *heavy), -bound, bound).astype(kind)


def setup_inputs(seed: int = 0) -> dict:
    key_of = jax.random.split(jax.random.key(seed), 9)
    return {
        "initial": centred(key_of[0], (SLABS, X, Y, 2, Z), 1.0, 6.0, ((1, 4), (2, 2))),
        "sens": heavy_noise(key_of[1], (SLABS, COILS, X, Y, 2, Z), 0.12, 2.5, ((1, 8),), (1, 2, 8, 2.0)),
        "kspace": centred(key_of[2], (SLABS, COILS, X, Y, 2, Z), 1.0, 6.0, ((1, 8),)),
        "mask": set_ends((jax.random.randint(key_of[3], (SLABS, Y, Z), 0, 3) < 1).astype(jnp.int32), jax.random.fold_in(key_of[3], 1), 0, 1),
        "step_sizes": jnp.clip(jnp.exp(math.log(1.5) - 1.60943787 * jax.random.uniform(key_of[4], (CASCADES,), jnp.float32) ** block_levels(key_of[4], (CASCADES,), ((0, 4),), -0.2, 0.2)), 0.3, 1.5),
        "conv_in": centred(key_of[5], (CASCADES, HID, 18), 18 ** -0.5, 1.5, ((0, 4),)),
        "bias_in": centred(key_of[6], (CASCADES, HID), 0.5, 3.0, ((0, 4),), jnp.float32),
        "conv_out": centred(key_of[7], (CASCADES, 18, HID), (9 * HID) ** -0.5, 0.1875, ((0, 4),)),
    }


def dft_table(length, sign):
    ramp = jnp.arange(length, dtype=jnp.int32)
    phase = ramp[:, None] * ramp[None, :] % length
    angle = phase.astype(jnp.float32) * (2.0 * math.pi / length)
    scale = 1.0 / math.sqrt(length)
    cosine = jnp.cos(angle) * scale
    sine = jnp.sin(angle) * (scale * sign)
    upper = jnp.concatenate([cosine, -sine], axis=1)
    lower = jnp.concatenate([sine, cosine], axis=1)
    return jnp.concatenate([upper, lower], axis=0).astype(jnp.bfloat16)

def pass_last(volume, table):
    shape = volume.shape
    flat = volume.reshape(-1, shape[-2] * shape[-1])
    return jnp.dot(flat, table, preferred_element_type=jnp.float32).astype(jnp.bfloat16).reshape(shape)

def pass_middle(volume, table):
    length = volume.shape[1]
    split = table.reshape(2, length, 2, length).astype(jnp.float32)
    return jnp.einsum('pjcz,cjdk->pkdz', volume.astype(jnp.float32), split).astype(jnp.bfloat16)

def pass_first(volume, table):
    length = volume.shape[0]
    split = table.reshape(2, length, 2, length).astype(jnp.float32)
    return jnp.einsum('jycz,cjdk->kydz', volume.astype(jnp.float32), split).astype(jnp.bfloat16)

def complex_product(sens, image):
    sens_real = sens[:, :, 0].astype(jnp.float32)
    sens_imag = sens[:, :, 1].astype(jnp.float32)
    image_real = image[:, :, 0].astype(jnp.float32)
    image_imag = image[:, :, 1].astype(jnp.float32)
    return jnp.stack([sens_real * image_real - sens_imag * image_imag, sens_real * image_imag + sens_imag * image_real], axis=2)

def conj_product(sens, back):
    sens_real = sens[:, :, 0].astype(jnp.float32)
    sens_imag = sens[:, :, 1].astype(jnp.float32)
    back_real = back[:, :, 0].astype(jnp.float32)
    back_imag = back[:, :, 1].astype(jnp.float32)
    return jnp.stack([sens_real * back_real + sens_imag * back_imag, sens_real * back_imag - sens_imag * back_real], axis=2)

def refine_block(image, weights_in, bias, weights_out):
    rows = image.shape[1]
    width = image.shape[3]
    padded = jnp.pad(image, ((0, 0), (1, 1), (0, 0), (1, 1)))
    taps = jnp.stack([padded[:, shift_row:shift_row + rows, :, shift_col:shift_col + width] for shift_row in range(3) for shift_col in range(3)], axis=2)
    taps = taps.reshape(image.shape[0], rows, 18, width)
    summed = jnp.einsum('hf,xyfz->xyhz', weights_in.astype(jnp.float32), taps.astype(jnp.float32))
    hidden = jax.nn.silu(summed + bias[None, None, :, None]).astype(jnp.bfloat16)
    product = jnp.einsum('fh,xyhz->xyfz', weights_out.astype(jnp.float32), hidden.astype(jnp.float32))
    beside_all = jnp.pad(product, ((0, 0), (1, 1), (0, 0), (1, 1)))
    total = jnp.zeros(image.shape, jnp.float32)
    for shift_row in range(3):
        for shift_col in range(3):
            first = (3 * shift_row + shift_col) * 2
            total = total + beside_all[:, shift_row:shift_row + rows, first:first + 2, shift_col:shift_col + width]
    return total

def cascade_step(image, sens_slab, kspace_slab, mask_slab, step, weights_in, bias, weights_out):
    size_x, size_y, _, size_z = image.shape
    forward_x, forward_y, forward_z = (dft_table(size_x, 1.0), dft_table(size_y, 1.0), dft_table(size_z, 1.0))
    back_x, back_y, back_z = (dft_table(size_x, -1.0), dft_table(size_y, -1.0), dft_table(size_z, -1.0))
    weight_mask = mask_slab.astype(jnp.float32)[None, :, None, :]

    def one_coil(grad, pair):
        sens_one, data_one = pair
        coil_image = complex_product(sens_one, image).astype(jnp.bfloat16)
        predicted = pass_first(pass_middle(pass_last(coil_image, forward_z), forward_y), forward_x)
        resid = (weight_mask * (data_one.astype(jnp.float32) - predicted.astype(jnp.float32))).astype(jnp.bfloat16)
        back = pass_last(pass_middle(pass_first(resid, back_x), back_y), back_z)
        return (grad + conj_product(sens_one, back), None)
    grad, _ = lax.scan(one_coil, jnp.zeros(image.shape, jnp.float32), (sens_slab, kspace_slab))
    refine = refine_block(image, weights_in, bias, weights_out)
    return (image.astype(jnp.float32) - step * grad + refine).astype(jnp.bfloat16)

def reference(initial, sens, kspace, mask, step_sizes, conv_in, bias_in, conv_out):
    images = [initial[slab] for slab in range(SLABS)]
    stacked = []
    for cascade in range(CASCADES):
        images = [cascade_step(images[slab], sens[slab], kspace[slab], mask[slab], step_sizes[cascade], conv_in[cascade], bias_in[cascade], conv_out[cascade]) for slab in range(SLABS)]
        stacked.append(jnp.stack(images, axis=0))
    return jnp.stack(stacked, axis=0)
```

```python
import math

import jax
import jax.numpy as jnp
from jax import lax
from jax.sharding import PartitionSpec as P


def dft_table(length, sign):
    ramp = jnp.arange(length, dtype=jnp.int32)
    phase = ramp[:, None] * ramp[None, :] % length
    angle = phase.astype(jnp.float32) * (2.0 * math.pi / length)
    scale = 1.0 / math.sqrt(length)
    cosine = jnp.cos(angle) * scale
    sine = jnp.sin(angle) * (scale * sign)
    upper = jnp.concatenate([cosine, -sine], axis=1)
    lower = jnp.concatenate([sine, cosine], axis=1)
    return jnp.concatenate([upper, lower], axis=0).astype(jnp.bfloat16)


def peers(axis):
    count = lax.axis_size(axis)
    me = lax.axis_index(axis)
    for k in range(1, count):
        if count & (count - 1) == 0:
            yield [(j, j ^ k) for j in range(count)], jnp.bitwise_xor(me, k), jnp.bitwise_xor(me, k)
        else:
            route = [(j, (j + k) % count) for j in range(count)]
            yield route, (me + k) % count, (me - k) % count


def exchange(piece_for, axis):
    arrived = [piece_for(lax.axis_index(axis))]
    for route, target, _ in peers(axis):
        arrived.append(lax.ppermute(piece_for(target), axis, route))
    return arrived


def step_to(index, axis):
    count = lax.axis_size(axis)
    me = lax.axis_index(axis)
    if count & (count - 1) == 0:
        return jnp.bitwise_xor(me, index)
    return (me - index) % count


def complex_product(a, b):
    ar, ai = a[..., 0, :, :].astype(jnp.float32), a[..., 1, :, :].astype(jnp.float32)
    br, bi = b[..., 0, :, :].astype(jnp.float32), b[..., 1, :, :].astype(jnp.float32)
    return jnp.stack([ar * br - ai * bi, ar * bi + ai * br], axis=-3)


def conj_product(a, b):
    ar, ai = a[..., 0, :, :].astype(jnp.float32), a[..., 1, :, :].astype(jnp.float32)
    br, bi = b[..., 0, :, :].astype(jnp.float32), b[..., 1, :, :].astype(jnp.float32)
    return jnp.stack([ar * br + ai * bi, ar * bi - ai * br], axis=-3)


def pass_z(v, table):
    length = v.shape[-1]
    split = table.reshape(2, length, 2, length)
    return jnp.einsum("...cyz,czdw->...dyw", v, split, preferred_element_type=jnp.float32).astype(jnp.bfloat16)


def pass_y(v, table):
    length = v.shape[-2]
    split = table.reshape(2, length, 2, length)
    return jnp.einsum("...cyz,cydk->...dkz", v, split, preferred_element_type=jnp.float32).astype(jnp.bfloat16)


def refine(image, weights_in, bias, weights_out):
    rows, width = image.shape[-2:]
    padded = jnp.pad(image, ((0, 0), (0, 0), (1, 1), (1, 1)))
    taps = jnp.concatenate(
        [padded[:, :, dy : dy + rows, dz : dz + width] for dy in range(3) for dz in range(3)], axis=1
    )
    summed = jnp.einsum("hf,pfyz->phyz", weights_in, taps, preferred_element_type=jnp.float32)
    hidden = jax.nn.silu(summed + bias[None, :, None, None]).astype(jnp.bfloat16)
    product = jnp.einsum("fh,phyz->pfyz", weights_out, hidden, preferred_element_type=jnp.float32)
    beside = jnp.pad(product, ((0, 0), (0, 0), (1, 1), (1, 1)))
    total = jnp.zeros(image.shape, jnp.float32)
    for dy in range(3):
        for dz in range(3):
            first = (3 * dy + dz) * 2
            total = total + beside[:, first : first + 2, dy : dy + rows, dz : dz + width]
    return total


def body(initial, sens, kspace, mask, step_sizes, conv_in, bias_in, conv_out):
    bf16 = jnp.bfloat16
    slabs, _, size_x, size_y, _, size_z = sens.shape
    sections, cuts, coils = lax.axis_size("section"), lax.axis_size("cuts"), lax.axis_size("coil")
    section, cut = lax.axis_index("section"), lax.axis_index("cuts")
    halves = sections // slabs
    slab, half = section // halves, section % halves
    owned = size_x // coils
    by_half = math.gcd(owned, halves)
    by_cut = math.gcd(owned // by_half, cuts)
    per = owned // (by_half * by_cut)
    run = by_cut * per
    half_block = half * by_half // halves
    rows = size_y // cuts

    def cut_block(which):
        return which * by_cut // cuts

    hid = bias_in.shape[1]
    packed = jnp.concatenate(
        [
            conv_in[0].astype(jnp.float32).T,
            conv_out[0].astype(jnp.float32),
            bias_in,
            jnp.broadcast_to(step_sizes[:, None], (1, hid)),
        ],
        axis=0,
    )
    params = jnp.stack(exchange(lambda _: packed, "section"), axis=0)

    mine = lax.dynamic_index_in_dim(initial, slab, 0, keepdims=False)
    mine = lax.dynamic_slice_in_dim(mine, half_block * run, run, 0)
    mine = jnp.swapaxes(mine, 1, 2)

    halves_of_rows = exchange(
        lambda to: lax.dynamic_slice_in_dim(mine, cut_block(to) * per, per, 0), "cuts"
    )
    order = [step_to(jnp.int32(i), "cuts") for i in range(cuts)]
    stacked_rows = jnp.stack(halves_of_rows, axis=0)
    image = jnp.concatenate(
        [lax.dynamic_index_in_dim(stacked_rows, at, 0, keepdims=False) for at in order], axis=2
    )

    def over_coils(array):
        def for_coil(to):
            return lax.dynamic_slice_in_dim(array, to * run, run, 0)

        columns = jnp.stack(exchange(for_coil, "coil"), axis=0)
        return exchange(
            lambda to: lax.dynamic_slice_in_dim(columns, cut_block(to) * per, per, 1), "cuts"
        )

    def half_slices(array, dim):
        shape = array.shape
        split = array.reshape(shape[:dim] + (coils, by_half, run) + shape[dim + 1 :])
        part = lax.dynamic_index_in_dim(split, half_block, dim + 1, keepdims=False)
        return part.reshape(shape[:dim] + (coils * run,) + shape[dim + 1 :])

    sens_one = lax.dynamic_index_in_dim(sens, slab, 0, keepdims=False)[0]
    sens_half = jnp.swapaxes(half_slices(sens_one, 0), 1, 2)
    sens_mine = jnp.concatenate(over_coils(sens_half), axis=0)

    data_one = lax.dynamic_index_in_dim(kspace, slab, 0, keepdims=False)[0]
    mask_one = lax.dynamic_index_in_dim(mask, slab, 0, keepdims=False).astype(bf16)
    back_x = half_slices(dft_table(size_x, -1.0).reshape(2, size_x, 2, size_x), 3)
    forward_y, forward_z = dft_table(size_y, 1.0), dft_table(size_z, 1.0)
    back_y, back_z = dft_table(size_y, -1.0), dft_table(size_z, -1.0)
    spectrum = jnp.einsum("jycz,cjdk->kdyz", data_one, back_x, preferred_element_type=jnp.float32)
    spectrum = spectrum.astype(bf16) * mask_one
    back = pass_z(pass_y(spectrum, back_y), back_z)
    term = conj_product(sens_half, back).reshape((coils, by_cut, per, 2, size_y, size_z))
    pair = exchange(
        lambda to: lax.dynamic_index_in_dim(term, cut_block(to), 1, keepdims=False).astype(bf16), "cuts"
    )
    pair = sum(p.astype(jnp.float32) for p in pair)
    data_term = sum(
        p.astype(jnp.float32)
        for p in exchange(
            lambda to: lax.dynamic_index_in_dim(pair, to, 0, keepdims=False).astype(bf16), "coil"
        )
    )

    images = []
    for cascade in range(sections):
        own = lax.dynamic_index_in_dim(params, step_to(jnp.int32(cascade), "section"), 0, keepdims=False)
        weights_in, weights_out = own[:18].T.astype(bf16), own[18:36].astype(bf16)
        bias, step = own[36], own[37, 0]
        coil_image = complex_product(sens_mine, image[None]).astype(bf16)
        predicted = pass_y(pass_z(coil_image, forward_z), forward_y) * mask_one
        back = pass_z(pass_y(predicted, back_y), back_z)
        normal = conj_product(sens_mine, back).sum(axis=0)
        grad = data_term - normal
        image = (
            image.astype(jnp.float32) - step * grad + refine(image, weights_in, bias, weights_out)
        ).astype(bf16)
        images.append(image)

    out = jnp.stack(images, axis=0).reshape(sections, per, 2, cuts, rows, size_z)
    out = jnp.transpose(out, (0, 3, 1, 4, 2, 5)).reshape(sections * cuts, per, rows, 2, size_z)
    out = lax.all_to_all(out, ("section", "cuts"), 0, 0, tiled=True)
    out = out.reshape(slabs, halves, cuts, per, rows, 2, size_z)[:, :: halves // by_half, :: cuts // by_cut]
    return out.reshape(1, slabs, owned, rows, 2, size_z)


def solution(mesh):
    return jax.shard_map(
        body,
        mesh=mesh,
        in_specs=(
            P(None, "coil", "cuts", None, None),
            P(None, ("coil", "cuts"), None, None, None, None),
            P(None, ("coil", "cuts"), None, None, None, None),
            P(),
            P("section"),
            P("section", None, None),
            P("section", None),
            P("section", None, None),
        ),
        out_specs=P("section", None, "coil", "cuts", None, None),
        check_vma=False,
    )
```

```python
import functools
import math

import jax
import jax.numpy as jnp
import ml_dtypes
import numpy as np
from jax import lax
from jax.experimental import pallas as pl
from jax.experimental.pallas import tpu as pltpu
from jax.sharding import PartitionSpec as P

INTERPRET = False
BF16, F32 = jnp.bfloat16, jnp.float32
TILE = 8


def dft_table(length, sign):
    ramp = np.arange(length)
    angle = (ramp[:, None] * ramp[None, :] % length) * (2.0 * math.pi / length)
    cosine = np.cos(angle) / math.sqrt(length)
    sine = sign * np.sin(angle) / math.sqrt(length)
    return np.block([[cosine, -sine], [sine, cosine]]).astype(ml_dtypes.bfloat16)


def peers(axis):
    count = lax.axis_size(axis)
    me = lax.axis_index(axis)
    for k in range(1, count):
        if count & (count - 1) == 0:
            yield [(j, j ^ k) for j in range(count)], jnp.bitwise_xor(me, k), jnp.bitwise_xor(me, k)
        else:
            route = [(j, (j + k) % count) for j in range(count)]
            yield route, (me + k) % count, (me - k) % count


def exchange(piece_for, axis):
    arrived = [piece_for(lax.axis_index(axis))]
    for route, target, _ in peers(axis):
        arrived.append(lax.ppermute(piece_for(target), axis, route))
    return arrived


def step_to(index, axis):
    count = lax.axis_size(axis)
    me = lax.axis_index(axis)
    if count & (count - 1) == 0:
        return jnp.bitwise_xor(me, index)
    return (me - index) % count


def conj_product(a, b):
    ar, ai = a[..., 0, :, :].astype(jnp.float32), a[..., 1, :, :].astype(jnp.float32)
    br, bi = b[..., 0, :, :].astype(jnp.float32), b[..., 1, :, :].astype(jnp.float32)
    return jnp.stack([ar * br + ai * bi, ar * bi - ai * br], axis=-3)


def pass_z(v, table):
    length = v.shape[-1]
    split = table.reshape(2, length, 2, length)
    return jnp.einsum("...cyz,czdw->...dyw", v, split, preferred_element_type=jnp.float32).astype(jnp.bfloat16)


def pass_y(v, table):
    length = v.shape[-2]
    split = table.reshape(2, length, 2, length)
    return jnp.einsum("...cyz,cydk->...dkz", v, split, preferred_element_type=jnp.float32).astype(jnp.bfloat16)


def selections():
    chosen = np.zeros((4 * 4 * TILE + TILE, 42), np.float32)
    for dy in range(3):
        for dz in range(3):
            for part in range(2):
                tap = (3 * dy + dz) * 2 + part
                for row in range(2):
                    chosen[row * 32 + (row + dy) * TILE + dz * 2 + part, tap] = 0.5
                    chosen[64 + row * 32 + (row + 2 - dy) * TILE + dz * 2 + part, 21 + tap] = 1.0
    for row in range(2):
        for piece, at in enumerate((TILE + 6, TILE + 7, 2 * TILE + 6)):
            chosen[row * 32 + at, 18 + piece] = 0.5
    for piece in range(3):
        chosen[128 + piece, 39 + piece] = 1.0
    return chosen.astype(ml_dtypes.bfloat16)


def in_three(x):
    high = lax.reduce_precision(x, 8, 7)
    rest = x - high
    mid = lax.reduce_precision(rest, 8, 7)
    return [high, mid, rest - mid]


def pack_weights(conv_in, bias, conv_out, step):
    rows = [conv_in.astype(F32).T] + in_three(bias[None]) + [conv_out.astype(F32)]
    rows += in_three(jnp.broadcast_to(step[None], (1, bias.shape[0])))
    operand = jnp.concatenate(rows, axis=0).astype(BF16)
    return jnp.dot(jnp.asarray(selections()), operand, preferred_element_type=F32).astype(BF16)


def shifted(plane, by, width):
    lane = lax.broadcasted_iota(jnp.int32, (plane.shape[0], width), 1)
    parts = []
    for at in range(0, plane.shape[1], width):
        moved = pltpu.roll(plane[:, at : at + width], (-by) % width, 1)
        parts.append(jnp.where((lane + by >= 0) & (lane + by < width), moved, 0.0))
    return jnp.concatenate(parts, axis=1)


def refine_into(planes, weights, taps_f32, taps, products, result, width):
    rows, lanes = planes[0].shape
    for dz in range(3):
        for part in range(2):
            plane = planes[part] if dz == 1 else shifted(planes[part], dz - 1, width)
            for s in range(lanes // width):
                place = pl.ds(TILE + dz * 2 + part, rows, stride=TILE)
                taps_f32.at[s][place, :] = plane[:, s * width : (s + 1) * width]
    for s in range(lanes // width):
        taps[:, s * width : (s + 1) * width] = taps_f32[s].astype(BF16)
    packed = weights.astype(F32)
    first = jnp.concatenate([packed[0:32].T, packed[32:64].T], axis=0).astype(BF16)
    second = jnp.concatenate([weights[64:96], weights[96:128]], axis=1)

    def pair(i, carry):
        start = pl.multiple_of(i * 2 * TILE, 2 * TILE)
        half = jnp.dot(first, taps[pl.ds(start, 4 * TILE), :], preferred_element_type=F32)
        hidden = (half + half * jnp.tanh(half)).astype(BF16)
        out = jnp.dot(second, hidden, preferred_element_type=F32)
        done = out[: 2 * TILE] + carry
        for s in range(lanes // width):
            products.at[s][pl.ds(start, 2 * TILE), :] = done[:, s * width : (s + 1) * width]
        return out[2 * TILE :]

    last = lax.fori_loop(0, rows // 2, pair, jnp.zeros((2 * TILE, lanes), F32), unroll=4)
    for s in range(lanes // width):
        own = slice(s * width, (s + 1) * width)
        products.at[s][rows * TILE : (rows + 2) * TILE, :] = last[:, own]
        for part in range(2):
            total = products.at[s][pl.ds(TILE + 2 + part, rows, stride=TILE), :]
            for dz in (0, 2):
                total += shifted(products.at[s][pl.ds(TILE + dz * 2 + part, rows, stride=TILE), :], dz - 1, width)
            result[part, :, own] = total


def fill_ones(taps_f32):
    taps_f32[...] = jnp.zeros(taps_f32.shape, F32)
    slices, rows, width = taps_f32.shape
    for s in range(slices):
        for at in (6, 7):
            taps_f32.at[s][pl.ds(at, rows // TILE, stride=TILE), :] = jnp.ones((rows // TILE, width), F32)


def load_planes(image, per):
    return [jnp.concatenate([image[s, part].astype(F32) for s in range(per)], axis=1) for part in range(2)]


def first_refine_kernel(order, image, weights, result, taps_f32, taps, products):
    per, _, _, width = image.shape
    fill_ones(taps_f32)
    refine_into(load_planes(image, per), weights[order[0]], taps_f32, taps, products, result, width)


def cascades_kernel(n_sens, n_data, order, *refs):
    image, first, mask, weights, forward_z, back_z, forward_y, back_y = refs[:8]
    senses, datas = refs[8 : 8 + n_sens], refs[8 + n_sens : 8 + n_sens + n_data]
    out = refs[8 + n_sens + n_data]
    taps_f32, taps, products, refined, planes, gradient, rows_z, rows_y = refs[9 + n_sens + n_data :]
    per, _, height, width = image.shape
    cascades = out.shape[0]
    fill_ones(taps_f32)
    refined[...] = first[...]
    for part, plane in enumerate(load_planes(image, per)):
        planes[part] = plane
    weight_mask = jnp.concatenate([mask[...]] * 2, axis=0)

    def place(piece, q, s):
        before = sum(r.shape[0] for r in senses[:piece])
        return (before + q) * per + s

    def each_coil(step):
        for piece, ref in enumerate(senses):
            if ref.shape[0] <= 8:
                for q in range(ref.shape[0]):
                    step(piece, ref, q)
            else:
                lax.fori_loop(0, ref.shape[0], lambda q, _: step(piece, ref, q), None)

    def aligned(start):
        return start if isinstance(start, int) else pl.multiple_of(start, 16)

    def cascade(c, _):
        def product(piece, ref, q):
            for s in range(per):
                lanes = slice(s * width, (s + 1) * width)
                sr, si = ref[q, s, 0].astype(F32), ref[q, s, 1].astype(F32)
                ir, ii = planes[0, :, lanes], planes[1, :, lanes]
                coil = jnp.concatenate([sr * ir - si * ii, sr * ii + si * ir], axis=1).astype(BF16)
                w = jnp.dot(coil, forward_z[...], preferred_element_type=F32).astype(BF16)
                w = jnp.concatenate([w[:, :width], w[:, width:]], axis=0)
                rows_y[place(piece, q, s)] = w

        each_coil(product)
        planes_count = rows_y.shape[0]

        def line(b, _):
            w = jnp.dot(forward_y[...], rows_y[b], preferred_element_type=F32)
            w = (w * weight_mask).astype(BF16)
            w = jnp.dot(back_y[...], w, preferred_element_type=F32).astype(BF16)
            rows_z[b] = jnp.concatenate([w[:height], w[height:]], axis=1)

        lax.fori_loop(0, planes_count, line, None, unroll=4)
        for s in range(per):
            lanes = slice(s * width, (s + 1) * width)
            for part in range(2):
                gradient[part, :, lanes] = sum(d[s, part].astype(F32) for d in datas)

        def gather(piece, ref, q):
            for s in range(per):
                lanes = slice(s * width, (s + 1) * width)
                sr, si = ref[q, s, 0].astype(F32), ref[q, s, 1].astype(F32)
                w = jnp.dot(rows_z[place(piece, q, s)], back_z[...], preferred_element_type=F32)
                br, bi = w[:, :width], w[:, width:]
                gradient[0, :, lanes] -= sr * br + si * bi
                gradient[1, :, lanes] -= sr * bi - si * br

        each_coil(gather)
        now = weights[order[c]]
        step = sum(now[128 + piece : 129 + piece, 0:1].astype(F32) for piece in range(3))
        for part in range(2):
            new = (planes[part] - step * gradient[part] + refined[part]).astype(BF16)
            for s in range(per):
                out[c, s, part] = new[:, s * width : (s + 1) * width]
            planes[part] = new.astype(F32)

        @pl.when(c + 1 < cascades)
        def _():
            refine_into(
                [planes[0], planes[1]], weights[order[c + 1]], taps_f32, taps, products, refined, width
            )

    lax.fori_loop(0, cascades, cascade, None)


def refine_scratch(height, per, width):
    rows = (height + 2) * TILE
    return [
        pltpu.VMEM((per, rows, width), F32),
        pltpu.VMEM((rows, per * width), BF16),
        pltpu.VMEM((per, rows, width), F32),
    ]


SMEM = pl.BlockSpec(memory_space=pltpu.SMEM)
VMEM = pl.BlockSpec(memory_space=pltpu.VMEM)


def first_refine(order, image, weights):
    per, _, height, width = image.shape
    return pl.pallas_call(
        first_refine_kernel,
        out_shape=jax.ShapeDtypeStruct((2, height, per * width), F32),
        in_specs=[SMEM, VMEM, VMEM],
        out_specs=VMEM,
        scratch_shapes=refine_scratch(height, per, width),
        interpret=INTERPRET,
    )(order, image, weights)


def run_cascades(order, image, first, mask, weights, senses, datas, cascades):
    per, _, height, width = image.shape
    lanes = per * width
    count = sum(s.shape[0] for s in senses) * per
    tables = [
        dft_table(width, 1.0),
        dft_table(width, -1.0),
        dft_table(height, 1.0).T.copy(),
        dft_table(height, -1.0).T.copy(),
    ]
    args = [image, first, mask, weights] + [jnp.asarray(t) for t in tables] + list(senses) + list(datas)
    return pl.pallas_call(
        functools.partial(cascades_kernel, len(senses), len(datas)),
        out_shape=jax.ShapeDtypeStruct((cascades, per, 2, height, width), BF16),
        in_specs=[SMEM] + [VMEM] * len(args),
        out_specs=VMEM,
        scratch_shapes=refine_scratch(height, per, width)
        + [
            pltpu.VMEM((2, height, lanes), F32),
            pltpu.VMEM((2, height, lanes), F32),
            pltpu.VMEM((2, height, lanes), F32),
            pltpu.VMEM((count, height, 2 * width), BF16),
            pltpu.VMEM((count, 2 * height, width), BF16),
        ],
        interpret=INTERPRET,
    )(order, *args)


def body(initial, sens, kspace, mask, step_sizes, conv_in, bias_in, conv_out):
    bf16 = BF16
    slabs, _, size_x, size_y, _, size_z = sens.shape
    sections, cuts, coils = lax.axis_size("section"), lax.axis_size("cuts"), lax.axis_size("coil")
    section, cut = lax.axis_index("section"), lax.axis_index("cuts")
    halves = sections // slabs
    slab, half = section // halves, section % halves
    owned = size_x // coils
    by_half = math.gcd(owned, halves)
    by_cut = math.gcd(owned // by_half, cuts)
    per = owned // (by_half * by_cut)
    run = by_cut * per
    half_block = half * by_half // halves
    rows = size_y // cuts

    def cut_block(which):
        return which * by_cut // cuts

    packed = pack_weights(conv_in[0], bias_in[0], conv_out[0], step_sizes)
    params = jnp.stack(exchange(lambda _: packed, "section"), axis=0)

    cascade_order = jnp.stack([step_to(jnp.int32(c), "section") for c in range(sections)])

    mine = lax.dynamic_index_in_dim(initial, slab, 0, keepdims=False)
    mine = lax.dynamic_slice_in_dim(mine, half_block * run, run, 0)
    mine = jnp.swapaxes(mine, 1, 2)

    halves_of_rows = exchange(
        lambda to: lax.dynamic_slice_in_dim(mine, cut_block(to) * per, per, 0), "cuts"
    )
    order = [step_to(jnp.int32(i), "cuts") for i in range(cuts)]
    stacked_rows = jnp.stack(halves_of_rows, axis=0)
    image = jnp.concatenate(
        [lax.dynamic_index_in_dim(stacked_rows, at, 0, keepdims=False) for at in order], axis=2
    )

    def over_coils(array):
        def for_coil(to):
            return lax.dynamic_slice_in_dim(array, to * run, run, 0)

        columns = jnp.stack(exchange(for_coil, "coil"), axis=0)
        return exchange(
            lambda to: lax.dynamic_slice_in_dim(columns, cut_block(to) * per, per, 1), "cuts"
        )

    def half_slices(array, dim):
        shape = array.shape
        split = array.reshape(shape[:dim] + (coils, by_half, run) + shape[dim + 1 :])
        part = lax.dynamic_index_in_dim(split, half_block, dim + 1, keepdims=False)
        return part.reshape(shape[:dim] + (coils * run,) + shape[dim + 1 :])

    sens_one = lax.dynamic_index_in_dim(sens, slab, 0, keepdims=False)[0]
    sens_half = jnp.swapaxes(half_slices(sens_one, 0), 1, 2)
    senses = over_coils(sens_half)

    data_one = lax.dynamic_index_in_dim(kspace, slab, 0, keepdims=False)[0]
    mask_one = lax.dynamic_index_in_dim(mask, slab, 0, keepdims=False).astype(bf16)
    back_x = half_slices(jnp.asarray(dft_table(size_x, -1.0)).reshape(2, size_x, 2, size_x), 3)
    back_y, back_z = jnp.asarray(dft_table(size_y, -1.0)), jnp.asarray(dft_table(size_z, -1.0))
    spectrum = jnp.einsum("jycz,cjdk->kdyz", data_one, back_x, preferred_element_type=jnp.float32)
    spectrum = spectrum.astype(bf16) * mask_one
    back = pass_z(pass_y(spectrum, back_y), back_z)
    term = conj_product(sens_half, back).reshape((coils, by_cut, per, 2, size_y, size_z))
    pair = exchange(
        lambda to: lax.dynamic_index_in_dim(term, cut_block(to), 1, keepdims=False).astype(bf16), "cuts"
    )
    pair = sum(p.astype(jnp.float32) for p in pair)
    datas = exchange(lambda to: lax.dynamic_index_in_dim(pair, to, 0, keepdims=False).astype(bf16), "coil")

    first = first_refine(cascade_order, image, params)
    images = run_cascades(
        cascade_order, image, first, mask_one.astype(F32), params, senses, datas, sections
    )
    out = images.reshape(sections, per, 2, cuts, rows, size_z)
    out = jnp.transpose(out, (0, 3, 1, 4, 2, 5)).reshape(sections * cuts, per, rows, 2, size_z)
    out = lax.all_to_all(out, ("section", "cuts"), 0, 0, tiled=True)
    out = out.reshape(slabs, halves, cuts, per, rows, 2, size_z)[:, :: halves // by_half, :: cuts // by_cut]
    return out.reshape(1, slabs, owned, rows, 2, size_z)


def solution(mesh):
    return jax.shard_map(
        body,
        mesh=mesh,
        in_specs=(
            P(None, "coil", "cuts", None, None),
            P(None, ("coil", "cuts"), None, None, None, None),
            P(None, ("coil", "cuts"), None, None, None, None),
            P(),
            P("section"),
            P("section", None, None),
            P("section", None),
            P("section", None, None),
        ),
        out_specs=P("section", None, "coil", "cuts", None, None),
        check_vma=False,
    )
```

```python
import functools
import math

import jax
import jax.numpy as jnp
import ml_dtypes
import numpy as np
from jax import lax
from jax.experimental import pallas as pl
from jax.experimental.pallas import tpu as pltpu
from jax.sharding import PartitionSpec as P

INTERPRET = False
BF16, F32 = jnp.bfloat16, jnp.float32
ACT = F32
GROUP = 4
TILE = 8


def dft_table(length, sign):
    ramp = np.arange(length)
    angle = (ramp[:, None] * ramp[None, :] % length) * (2.0 * math.pi / length)
    cosine = np.cos(angle) / math.sqrt(length)
    sine = sign * np.sin(angle) / math.sqrt(length)
    return np.block([[cosine, -sine], [sine, cosine]]).astype(ml_dtypes.bfloat16)


def peers(axis):
    count = lax.axis_size(axis)
    me = lax.axis_index(axis)
    for k in range(1, count):
        if count & (count - 1) == 0:
            yield [(j, j ^ k) for j in range(count)], jnp.bitwise_xor(me, k), jnp.bitwise_xor(me, k)
        else:
            route = [(j, (j + k) % count) for j in range(count)]
            yield route, (me + k) % count, (me - k) % count


def own_and_peers(axis):
    me = lax.axis_index(axis)
    yield None, me, me
    yield from peers(axis)


def step_to(index, axis):
    count = lax.axis_size(axis)
    me = lax.axis_index(axis)
    if count & (count - 1) == 0:
        return jnp.bitwise_xor(me, index)
    return (me - index) % count


SMEM = pl.BlockSpec(memory_space=pltpu.SMEM)
VMEM = pl.BlockSpec(memory_space=pltpu.VMEM)
ANY = pl.BlockSpec(memory_space=pl.ANY)


def selections():
    chosen = np.zeros((4 * 4 * TILE + TILE, 42), np.float32)
    for dy in range(3):
        for dz in range(3):
            for part in range(2):
                tap = (3 * dy + dz) * 2 + part
                for row in range(2):
                    chosen[row * 32 + (row + dy) * TILE + dz * 2 + part, tap] = 0.5
                    chosen[64 + row * 32 + (row + 2 - dy) * TILE + dz * 2 + part, 21 + tap] = 1.0
    for row in range(2):
        for piece, at in enumerate((TILE + 6, TILE + 7, 2 * TILE + 6)):
            chosen[row * 32 + at, 18 + piece] = 0.5
    for piece in range(3):
        chosen[128 + piece, 39 + piece] = 1.0
    return chosen.astype(ml_dtypes.bfloat16)


def in_three(x):
    high = x.astype(BF16)
    rest = x - high.astype(F32)
    mid = rest.astype(BF16)
    return [high, mid, (rest - mid.astype(F32)).astype(BF16)]


def pack_kernel(chosen, conv_in, bias, conv_out, step, packed):
    def picked(rows, lanes):
        return jnp.dot(chosen[:, lanes], rows, preferred_element_type=F32)

    total = picked(conv_in[...], slice(0, 18)) + picked(conv_out[...], slice(21, 39))
    steps = jnp.full(bias.shape, step[0], F32)
    for at, split in ((18, in_three(bias[...])), (39, in_three(steps))):
        for piece, row in enumerate(split):
            column = chosen[:, at + piece : at + piece + 1].astype(F32)
            total += column * row.astype(F32)
    packed[...] = total.astype(BF16)


def pack_weights(conv_in, bias, conv_out, step):
    chosen = jnp.asarray(selections())
    return pl.pallas_call(
        pack_kernel,
        out_shape=jax.ShapeDtypeStruct((chosen.shape[0], bias.shape[1]), BF16),
        in_specs=[VMEM, VMEM, VMEM, VMEM, SMEM],
        out_specs=VMEM,
        interpret=INTERPRET,
    )(chosen, conv_in.T, bias, conv_out, step)


def shifted(plane, by, width):
    lane = lax.broadcasted_iota(jnp.int32, (plane.shape[0], width), 1)
    parts = []
    for at in range(0, plane.shape[1], width):
        moved = pltpu.roll(plane[:, at : at + width], (-by) % width, 1)
        parts.append(jnp.where((lane + by >= 0) & (lane + by < width), moved, 0.0))
    return jnp.concatenate(parts, axis=1)


def refine_into(planes, weights, scratch, result, width):
    rows, lanes = planes[0].shape
    taps_f32, taps, products, halves, hidden = scratch
    for dz in range(3):
        for part in range(2):
            plane = planes[part] if dz == 1 else shifted(planes[part], dz - 1, width)
            for s in range(lanes // width):
                place = pl.ds(TILE + dz * 2 + part, rows, stride=TILE)
                taps_f32.at[s][place, :] = plane[:, s * width : (s + 1) * width]
    for s in range(lanes // width):
        taps[:, s * width : (s + 1) * width] = taps_f32[s].astype(BF16)
    packed = weights.astype(F32)
    first = jnp.concatenate([packed[0:32].T, packed[32:64].T], axis=0).astype(BF16)
    second = jnp.concatenate([weights[64:96], weights[96:128]], axis=1)

    def start_of(j, g):
        start = (j * GROUP + g) * 2 * TILE
        return start if isinstance(start, int) else pl.multiple_of(start, 2 * TILE)

    def before(j, slot, g):
        window = taps[pl.ds(start_of(j, g), 4 * TILE), :]
        halves[slot, g] = jnp.dot(first, window, preferred_element_type=F32).astype(halves.dtype)

    def activate(slot, g):
        half = halves[slot, g]
        hidden[slot, g] = (half + half * jnp.tanh(half)).astype(BF16)

    def after(j, slot, g, carry):
        out = jnp.dot(second, hidden[slot, g], preferred_element_type=F32)
        done = out[: 2 * TILE] + carry
        for s in range(lanes // width):
            products.at[s][pl.ds(start_of(j, g), 2 * TILE), :] = done[:, s * width : (s + 1) * width]
        return out[2 * TILE :]

    blocks = rows // (2 * GROUP)
    for g in range(GROUP):
        before(0, 0, g)
    for g in range(GROUP):
        activate(0, g)
        before(1, 1, g)

    def two(i, carry):
        for j, slot in ((2 * i + 1, 1), (2 * i + 2, 0)):
            for g in range(GROUP):
                carry = after(j - 1, 1 - slot, g, carry)
                activate(slot, g)
                before(j + 1, 1 - slot, g)
        return carry

    carry = lax.fori_loop(0, (blocks - 2) // 2, two, jnp.zeros((2 * TILE, lanes), F32))
    for g in range(GROUP):
        carry = after(blocks - 2, 0, g, carry)
        activate(1, g)
    for g in range(GROUP):
        carry = after(blocks - 1, 1, g, carry)
    last = carry
    for s in range(lanes // width):
        own = slice(s * width, (s + 1) * width)
        products.at[s][rows * TILE : (rows + 2) * TILE, :] = last[:, own]
        for part in range(2):
            total = products.at[s][pl.ds(TILE + 2 + part, rows, stride=TILE), :]
            for dz in (0, 2):
                total += shifted(products.at[s][pl.ds(TILE + dz * 2 + part, rows, stride=TILE), :], dz - 1, width)
            result[part, :, own] = total


def fill_ones(taps_f32):
    taps_f32[...] = jnp.zeros(taps_f32.shape, F32)
    slices, rows, width = taps_f32.shape
    for s in range(slices):
        for at in (6, 7):
            taps_f32.at[s][pl.ds(at, rows // TILE, stride=TILE), :] = jnp.ones((rows // TILE, width), F32)


def first_refine_kernel(n_rows, n_weights, *refs):
    pieces, weights = refs[:n_rows], refs[n_rows : n_rows + n_weights]
    refined, planes, stage = refs[n_rows + n_weights : n_rows + n_weights + 3]
    scratch = refs[n_rows + n_weights + 3 :]
    per, _, width = pieces[0].shape
    fill_ones(scratch[0])
    for k, (_, _, source) in enumerate(own_and_peers("cuts")):
        block = pieces[k].shape[1]
        for s in range(per):
            stage.at[s][pl.ds(pl.multiple_of(source * block, 16), block), :] = pieces[k][s].astype(F32)
    height = stage.shape[1] // 2
    for s in range(per):
        for part in range(2):
            planes[part, :, s * width : (s + 1) * width] = stage.at[s][pl.ds(part, height, stride=2), :]
    refine_into([planes[0], planes[1]], of_cascade(weights, 0), scratch, refined, width)


def of_cascade(weights, cascade):
    at = step_to(cascade, "section")
    chosen = weights[0][...]
    for k in range(1, len(weights)):
        chosen = jnp.where(at == k, weights[k][...], chosen)
    return chosen


def cascades_kernel(n_weights, n_sens, n_more, n_data, by_cut, *refs):
    planes_in, first, mask, forward_z, back_z, forward_y, back_y = refs[:7]
    at = 7
    weights, at = refs[at : at + n_weights], at + n_weights
    senses, at = refs[at : at + n_sens], at + n_sens
    more, at = refs[at : at + n_more], at + n_more
    datas, at = refs[at : at + n_data], at + n_data
    out = refs[at]
    scratch = refs[at + 1 : -8]
    refined, planes, gradient, coil_planes, rows_z, rows_y, stage, all_weights = refs[-8:]
    per, _, height, width = datas[0].shape
    cascades = len(weights)
    cuts = out.shape[0] // cascades
    slab = lax.axis_index("section") // (lax.axis_size("section") // mask.shape[0])
    fill_ones(scratch[0])
    refined[...] = first[...]
    planes[...] = planes_in[...]
    for k in range(cascades):
        all_weights[k] = weights[k][...]
    weight_mask = mask[slab].astype(F32)
    weight_mask = jnp.concatenate([weight_mask] * 2, axis=0)

    def keep(n, rows):
        stage[n % stage.shape[0]] = rows.astype(F32)
        for part in range(2):
            plane = stage.at[n % stage.shape[0]][pl.ds(part, height, stride=2), :]
            coil_planes[n, part] = plane.astype(BF16)

    run_start = (lax.axis_index("cuts") * by_cut // cuts) * per
    n = 0
    for ref in senses:
        for s in range(per):
            keep(n, ref[run_start + s])
            n += 1
    for ref in more:
        for q in range(ref.shape[0]):
            for s in range(per):
                keep(n, ref[q, s])
                n += 1
    coils = n // per
    unroll = coils <= 8

    def each_coil(step):
        if unroll:
            for q in range(coils):
                step(q)
        else:
            lax.fori_loop(0, coils, lambda q, _: step(q), None)

    def cascade(c, _):
        def product(q):
            for s in range(per):
                lanes = slice(s * width, (s + 1) * width)
                sr, si = coil_planes[q * per + s, 0].astype(F32), coil_planes[q * per + s, 1].astype(F32)
                ir, ii = planes[0, :, lanes], planes[1, :, lanes]
                coil = jnp.concatenate([sr * ir - si * ii, sr * ii + si * ir], axis=1).astype(BF16)
                w = jnp.dot(coil, forward_z[...], preferred_element_type=F32).astype(BF16)
                rows_y[q * per + s] = jnp.concatenate([w[:, :width], w[:, width:]], axis=0)

        each_coil(product)

        def line(b, _):
            w = jnp.dot(forward_y[...], rows_y[b], preferred_element_type=F32)
            w = (w * weight_mask).astype(BF16)
            w = jnp.dot(back_y[...], w, preferred_element_type=F32).astype(BF16)
            rows_z[b] = jnp.concatenate([w[:height], w[height:]], axis=1)

        lax.fori_loop(0, coils * per, line, None, unroll=4)
        for s in range(per):
            lanes = slice(s * width, (s + 1) * width)
            for part in range(2):
                gradient[part, :, lanes] = sum(d[s, part].astype(F32) for d in datas)

        def gather(q):
            for s in range(per):
                lanes = slice(s * width, (s + 1) * width)
                sr, si = coil_planes[q * per + s, 0].astype(F32), coil_planes[q * per + s, 1].astype(F32)
                w = jnp.dot(rows_z[q * per + s], back_z[...], preferred_element_type=F32)
                br, bi = w[:, :width], w[:, width:]
                gradient[0, :, lanes] -= sr * br + si * bi
                gradient[1, :, lanes] -= sr * bi - si * br

        each_coil(gather)
        now = all_weights.at[step_to(c, "section")]
        step = sum(now[128 + piece : 129 + piece, 0:1].astype(F32) for piece in range(3))
        for part in range(2):
            new = (planes[part] - step * gradient[part] + refined[part]).astype(BF16).astype(F32)
            planes[part] = new
            for s in range(per):
                stage.at[s][pl.ds(part, height, stride=2), :] = new[:, s * width : (s + 1) * width]
        block = 2 * height // cuts
        for s in range(per):
            for cut in range(cuts):
                out[c * cuts + cut, s] = stage[s, cut * block : (cut + 1) * block].astype(BF16)

        @pl.when(c + 1 < cascades)
        def _():
            refine_into(
                [planes[0], planes[1]], all_weights[step_to(c + 1, "section")], scratch, refined, width
            )

    lax.fori_loop(0, cascades, cascade, None)


def refine_scratch(height, per, width, hid):
    rows, lanes = (height + 2) * TILE, per * width
    assert height % (4 * GROUP) == 0
    return [
        pltpu.VMEM((per, rows, width), F32),
        pltpu.VMEM((rows, lanes), BF16),
        pltpu.VMEM((per, rows, width), F32),
        pltpu.VMEM((2, GROUP, 2 * hid, lanes), ACT),
        pltpu.VMEM((2, GROUP, 2 * hid, lanes), BF16),
    ]


def first_refine(pieces, weights):
    per, block, width = pieces[0].shape
    rows = block * len(pieces)
    plane = jax.ShapeDtypeStruct((2, rows // 2, per * width), F32)
    return pl.pallas_call(
        functools.partial(first_refine_kernel, len(pieces), len(weights)),
        out_shape=(plane, plane),
        in_specs=[VMEM] * (len(pieces) + len(weights)),
        out_specs=(VMEM, VMEM),
        scratch_shapes=[pltpu.VMEM((per, rows, width), F32)]
        + refine_scratch(rows // 2, per, width, weights[0].shape[-1]),
        interpret=INTERPRET,
    )(*pieces, *weights)


def run_cascades(planes, first, mask, weights, senses, more, datas, cuts, by_cut):
    per, _, height, width = datas[0].shape
    lanes = per * width
    count = per * (len(senses) + sum(m.shape[0] for m in more))
    tables = [
        dft_table(width, 1.0),
        dft_table(width, -1.0),
        dft_table(height, 1.0).T.copy(),
        dft_table(height, -1.0).T.copy(),
    ]
    args = [planes, first, mask] + [jnp.asarray(t) for t in tables]
    args += list(weights) + list(senses) + list(more) + list(datas)
    return pl.pallas_call(
        functools.partial(
            cascades_kernel, len(weights), len(senses), len(more), len(datas), by_cut
        ),
        out_shape=jax.ShapeDtypeStruct((len(weights) * cuts, per, 2 * height // cuts, width), BF16),
        in_specs=[VMEM] * len(args),
        out_specs=VMEM,
        scratch_shapes=refine_scratch(height, per, width, weights[0].shape[-1])
        + [
            pltpu.VMEM((2, height, lanes), F32),
            pltpu.VMEM((2, height, lanes), F32),
            pltpu.VMEM((2, height, lanes), F32),
            pltpu.VMEM((count, 2, height, width), BF16),
            pltpu.VMEM((count, height, 2 * width), BF16),
            pltpu.VMEM((count, 2 * height, width), BF16),
            pltpu.VMEM((max(per, 4), 2 * height, width), F32),
            pltpu.VMEM((len(weights),) + weights[0].shape, BF16),
        ],
        interpret=INTERPRET,
    )(*args)


def copy_all(copies):
    for copy in copies:
        copy.start()
    for copy in copies:
        copy.wait()


def split_kernel(place, sens, initial, *refs):
    coils, cuts = lax.axis_size("coil"), lax.axis_size("cuts")
    sens_out, initial_out, sems = refs[:coils], refs[coils : coils + cuts], refs[-1]
    slab, block = place.slab(), place.half_block()
    copies = []
    for k, (_, target, _) in enumerate(own_and_peers("coil")):
        source = sens.at[slab, 0, pl.ds(target * place.owned + block * place.run, place.run)]
        copies.append(pltpu.make_async_copy(source, sens_out[k], sems.at[k]))
    for k, (_, target, _) in enumerate(own_and_peers("cuts")):
        start = block * place.run + place.cut_block(target) * place.per
        source = initial.at[slab, pl.ds(start, place.per)]
        copies.append(pltpu.make_async_copy(source, initial_out[k], sems.at[coils + k]))
    copy_all(copies)


def split(place, sens, initial):
    coils, cuts = lax.axis_size("coil"), lax.axis_size("cuts")
    outs = [jax.ShapeDtypeStruct((place.run,) + sens.shape[-2:], BF16)] * coils
    outs += [jax.ShapeDtypeStruct((place.per,) + initial.shape[-2:], BF16)] * cuts
    made = pl.pallas_call(
        functools.partial(split_kernel, place),
        out_shape=outs,
        in_specs=[ANY, ANY],
        out_specs=[ANY] * len(outs),
        scratch_shapes=[pltpu.SemaphoreType.DMA((len(outs),))],
        interpret=INTERPRET,
    )(sens, initial)
    return made[:coils], made[coils:]


def partners_kernel(place, *refs):
    coils, cuts = lax.axis_size("coil"), lax.axis_size("cuts")
    senses, outs, sems = refs[:coils], refs[coils : coils + cuts - 1], refs[-1]
    copies = []
    for k, (_, target, _) in enumerate(own_and_peers("cuts")):
        if k:
            for q in range(coils):
                source = senses[q].at[pl.ds(place.cut_block(target) * place.per, place.per)]
                copies.append(pltpu.make_async_copy(source, outs[k - 1].at[q], sems.at[k - 1, q]))
    copy_all(copies)


def for_partners(place, senses):
    coils, cuts = lax.axis_size("coil"), lax.axis_size("cuts")
    outs = [jax.ShapeDtypeStruct((coils, place.per) + senses[0].shape[-2:], BF16)] * (cuts - 1)
    return pl.pallas_call(
        functools.partial(partners_kernel, place),
        out_shape=outs,
        in_specs=[ANY] * coils,
        out_specs=[ANY] * len(outs),
        scratch_shapes=[pltpu.SemaphoreType.DMA((cuts - 1, coils))],
        interpret=INTERPRET,
    )(*senses)


CHUNKS = 4


def adjoint_kernel(place, kspace, sens, mask, table_x, back_y, back_z, *refs):
    coils, cuts = lax.axis_size("coil"), lax.axis_size("cuts")
    outs = refs[:cuts]
    data, own_sens, by_row, by_slice, stage, sems = refs[cuts:]
    size_x, rows, width = data.shape
    height = rows // 2
    kept = coils * place.run
    slab, block = place.slab(), place.half_block()
    chunk = size_x // CHUNKS
    copies = []
    for i in range(CHUNKS):
        at = pl.ds(i * chunk, chunk)
        copies.append(pltpu.make_async_copy(kspace.at[slab, 0, at], data.at[at], sems.at[i]))
    for q in range(coils):
        source = sens.at[slab, 0, pl.ds(q * place.owned + block * place.run, place.run)]
        target = own_sens.at[pl.ds(q * place.run, place.run)]
        copies.append(pltpu.make_async_copy(source, target, sems.at[CHUNKS + q]))
    for copy in copies:
        copy.start()
    for i in range(CHUNKS):
        copies[i].wait()
        for x in range(i * chunk, (i + 1) * chunk):
            by_row[pl.ds(x, rows, stride=size_x), :] = data[x].astype(F32)
    selected = table_x[block]

    def along_x(y, _):
        operand = by_row[pl.ds(pl.multiple_of(y * 2 * size_x, 2 * size_x), 2 * size_x), :].astype(BF16)
        w = jnp.dot(selected, operand, preferred_element_type=F32)
        by_slice[pl.ds(y, 2 * kept, stride=height), :] = w

    lax.fori_loop(0, height, along_x, None, unroll=8)
    for copy in copies[CHUNKS:]:
        copy.wait()
    weight_mask = mask[slab].astype(F32)
    for k, (_, target, _) in enumerate(own_and_peers("cuts")):

        def one(q, _, k=k, target=target):
            for s in range(place.per):
                n = q * place.run + place.cut_block(target) * place.per + s
                parts = []
                for part in range(2):
                    start = pl.multiple_of((part * kept + n) * height, 16)
                    w = by_slice[pl.ds(start, height), :]
                    parts.append((w.astype(BF16).astype(F32) * weight_mask).astype(BF16))
                w = jnp.concatenate(parts, axis=0)
                w = jnp.dot(back_y[...], w, preferred_element_type=F32).astype(BF16)
                w = jnp.concatenate([w[:height], w[height:]], axis=1)
                w = jnp.dot(w, back_z[...], preferred_element_type=F32)
                br, bi = w[:, :width], w[:, width:]
                stage[s] = own_sens[n].astype(F32)
                sr, si = (stage.at[s][pl.ds(part, height, stride=2), :] for part in range(2))
                outs[k][q, s, 0] = (sr * br + si * bi).astype(BF16)
                outs[k][q, s, 1] = (sr * bi - si * br).astype(BF16)

        lax.fori_loop(0, coils, one, None, unroll=4)


def adjoint(place, kspace, sens, mask):
    coils, cuts = lax.axis_size("coil"), lax.axis_size("cuts")
    size_x, rows, width = kspace.shape[-3:]
    height = rows // 2
    kept = coils * place.run
    table = dft_table(size_x, -1.0).reshape(2, size_x, 2, coils, place.by_half, place.run)
    table = table.transpose(4, 2, 3, 5, 0, 1).reshape(place.by_half, 2 * kept, 2 * size_x)
    tables = [table, dft_table(height, -1.0).T.copy(), dft_table(width, -1.0)]
    return pl.pallas_call(
        functools.partial(adjoint_kernel, place),
        out_shape=[jax.ShapeDtypeStruct((coils, place.per, 2, height, width), BF16)] * cuts,
        in_specs=[ANY, ANY] + [VMEM] * 4,
        out_specs=[VMEM] * cuts,
        scratch_shapes=[
            pltpu.VMEM((size_x, rows, width), BF16),
            pltpu.VMEM((kept, rows, width), BF16),
            pltpu.VMEM((rows * size_x, width), F32),
            pltpu.VMEM((2 * kept * height, width), F32),
            pltpu.VMEM((place.per, rows, width), F32),
            pltpu.SemaphoreType.DMA((CHUNKS + coils,)),
        ],
        interpret=INTERPRET,
    )(kspace, sens, mask, *[jnp.asarray(t) for t in tables])


def pair_sum_kernel(n_in, *refs):
    terms, outs = refs[:n_in], refs[n_in:]
    for k, (_, target, _) in enumerate(own_and_peers("coil")):
        outs[k][...] = sum(t[target].astype(F32) for t in terms).astype(BF16)


def pair_sum(terms):
    coils = lax.axis_size("coil")
    return pl.pallas_call(
        functools.partial(pair_sum_kernel, len(terms)),
        out_shape=[jax.ShapeDtypeStruct(terms[0].shape[1:], BF16)] * coils,
        in_specs=[VMEM] * len(terms),
        out_specs=[VMEM] * coils,
        interpret=INTERPRET,
    )(*terms)


class Place:
    def __init__(self, slabs, size_x):
        sections, coils, cuts = (lax.axis_size(a) for a in ("section", "coil", "cuts"))
        self.slabs, self.cuts, self.halves = slabs, cuts, sections // slabs
        self.owned = size_x // coils
        self.by_half = math.gcd(self.owned, self.halves)
        self.by_cut = math.gcd(self.owned // self.by_half, cuts)
        self.per = self.owned // (self.by_half * self.by_cut)
        self.run = self.by_cut * self.per

    def slab(self):
        return lax.axis_index("section") // self.halves

    def half_block(self):
        return lax.axis_index("section") % self.halves * self.by_half // self.halves

    def cut_block(self, cut):
        return cut * self.by_cut // self.cuts


def sent(pieces, axis):
    arrived = [pieces[0]]
    for k, (route, _, _) in enumerate(peers(axis)):
        arrived.append(lax.ppermute(pieces[k + 1], axis, route))
    return arrived


def body(initial, sens, kspace, mask, step_sizes, conv_in, bias_in, conv_out):
    slabs, _, size_x, size_y, _, size_z = sens.shape
    sections, cuts = lax.axis_size("section"), lax.axis_size("cuts")
    place = Place(slabs, size_x)
    rows = size_y // cuts

    def joined(array):
        return array.reshape(array.shape[:-3] + (array.shape[-3] * 2, size_z))

    initial, sens, kspace = joined(initial), joined(sens), joined(kspace)
    sens_pieces, image_pieces = split(place, sens, initial)
    senses = sent(sens_pieces, "coil")

    terms = adjoint(place, kspace, sens, mask)
    terms = [terms[0]] + [
        lax.ppermute(terms[k + 1], "cuts", route) for k, (route, _, _) in enumerate(peers("cuts"))
    ]
    datas = sent(pair_sum(terms), "coil")

    packed = pack_weights(conv_in[0], bias_in, conv_out[0], step_sizes)
    weights = sent([packed] * sections, "section")
    first, planes = first_refine(sent(image_pieces, "cuts"), weights)

    more = [
        lax.ppermute(piece, "cuts", route)
        for piece, (route, _, _) in zip(for_partners(place, senses), peers("cuts"))
    ]
    out = run_cascades(planes, first, mask, weights, senses, more, datas, cuts, place.by_cut)
    out = lax.all_to_all(out, ("section", "cuts"), 0, 0, tiled=True)
    out = out.reshape(slabs, place.halves, cuts, place.per, rows, 2, size_z)
    out = out[:, :: place.halves // place.by_half, :: cuts // place.by_cut]
    return out.reshape(1, slabs, place.owned, rows, 2, size_z)


def solution(mesh):
    return jax.shard_map(
        body,
        mesh=mesh,
        in_specs=(
            P(None, "coil", "cuts", None, None),
            P(None, ("coil", "cuts"), None, None, None, None),
            P(None, ("coil", "cuts"), None, None, None, None),
            P(),
            P("section"),
            P("section", None, None),
            P("section", None),
            P("section", None, None),
        ),
        out_specs=P("section", None, "coil", "cuts", None, None),
        check_vma=False,
    )
```

```python
import functools
import math

import jax
import jax.numpy as jnp
import ml_dtypes
import numpy as np
from jax import lax
from jax.experimental import pallas as pl
from jax.experimental.pallas import tpu as pltpu
from jax.sharding import PartitionSpec as P


INTERPRET = False
BF16, F32 = jnp.bfloat16, jnp.float32
ACT = F32
GROUP = 4
TILE = 8


def dft_table(length, sign):
    ramp = np.arange(length)
    angle = (ramp[:, None] * ramp[None, :] % length) * (2.0 * math.pi / length)
    cosine = np.cos(angle) / math.sqrt(length)
    sine = sign * np.sin(angle) / math.sqrt(length)
    return np.block([[cosine, -sine], [sine, cosine]]).astype(ml_dtypes.bfloat16)


def peers(axis):
    count = lax.axis_size(axis)
    me = lax.axis_index(axis)
    for k in range(1, count):
        if count & (count - 1) == 0:
            yield [(j, j ^ k) for j in range(count)], jnp.bitwise_xor(me, k), jnp.bitwise_xor(me, k)
        else:
            route = [(j, (j + k) % count) for j in range(count)]
            yield route, (me + k) % count, (me - k) % count


def own_and_peers(axis):
    me = lax.axis_index(axis)
    yield None, me, me
    yield from peers(axis)


def step_to(index, axis):
    count = lax.axis_size(axis)
    me = lax.axis_index(axis)
    if count & (count - 1) == 0:
        return jnp.bitwise_xor(me, index)
    return (me - index) % count


SMEM = pl.BlockSpec(memory_space=pltpu.SMEM)
VMEM = pl.BlockSpec(memory_space=pltpu.VMEM)
ANY = pl.BlockSpec(memory_space=pl.ANY)


def far():
    return INTERPRET or lax.axis_size("coil") > 8


def near(x):
    return x if far() else pltpu.with_memory_space_constraint(x, pltpu.VMEM)


def near_out(shape, dtype):
    return jax.ShapeDtypeStruct(shape, dtype) if far() else pltpu.VMEM(shape, dtype)


def selections():
    chosen = np.zeros((4 * 4 * TILE + TILE, 42), np.float32)
    for dy in range(3):
        for dz in range(3):
            for part in range(2):
                tap = (3 * dy + dz) * 2 + part
                for row in range(2):
                    chosen[row * 32 + (row + dy) * TILE + dz * 2 + part, tap] = 0.5
                    chosen[64 + row * 32 + (row + 2 - dy) * TILE + dz * 2 + part, 21 + tap] = 1.0
    for row in range(2):
        for piece, at in enumerate((TILE + 6, TILE + 7, 2 * TILE + 6)):
            chosen[row * 32 + at, 18 + piece] = 0.5
    for piece in range(3):
        chosen[128 + piece, 39 + piece] = 1.0
    return chosen.astype(ml_dtypes.bfloat16)


def in_three(x):
    high = x.astype(BF16)
    rest = x - high.astype(F32)
    mid = rest.astype(BF16)
    return [high, mid, (rest - mid.astype(F32)).astype(BF16)]


def pack_into(packed, chosen, conv_in, bias, conv_out, step):
    def picked(rows, lanes):
        return jnp.dot(chosen[:, lanes], rows, preferred_element_type=F32)

    total = picked(conv_in[...], slice(0, 18)) + picked(conv_out[...], slice(21, 39))
    steps = jnp.full(bias.shape, step[0], F32)
    for at, split in ((18, in_three(bias[...])), (39, in_three(steps))):
        for piece, row in enumerate(split):
            column = chosen[:, at + piece : at + piece + 1].astype(F32)
            total += column * row.astype(F32)
    packed[...] = total.astype(BF16)


def shifted(plane, by, width):
    lane = lax.broadcasted_iota(jnp.int32, (plane.shape[0], width), 1)
    parts = []
    for at in range(0, plane.shape[1], width):
        moved = pltpu.roll(plane[:, at : at + width], (-by) % width, 1)
        parts.append(jnp.where((lane + by >= 0) & (lane + by < width), moved, 0.0))
    return jnp.concatenate(parts, axis=1)


def refine_into(planes, weights, scratch, result, width):
    rows, lanes = planes[0].shape
    taps_f32, taps, products, halves, hidden = scratch
    for dz in range(3):
        for part in range(2):
            plane = planes[part] if dz == 1 else shifted(planes[part], dz - 1, width)
            for s in range(lanes // width):
                place = pl.ds(TILE + dz * 2 + part, rows, stride=TILE)
                taps_f32.at[s][place, :] = plane[:, s * width : (s + 1) * width]
    for s in range(lanes // width):
        taps[:, s * width : (s + 1) * width] = taps_f32[s].astype(BF16)
    packed = weights.astype(F32)
    first = jnp.concatenate([packed[0:32].T, packed[32:64].T], axis=0).astype(BF16)
    second = jnp.concatenate([weights[64:96], weights[96:128]], axis=1)

    def start_of(j, g):
        start = (j * GROUP + g) * 2 * TILE
        return start if isinstance(start, int) else pl.multiple_of(start, 2 * TILE)

    def before(j, slot, g):
        window = taps[pl.ds(start_of(j, g), 4 * TILE), :]
        halves[slot, g] = jnp.dot(first, window, preferred_element_type=F32).astype(halves.dtype)

    def activate(slot, g):
        half = halves[slot, g]
        hidden[slot, g] = (half + half * jnp.tanh(half)).astype(BF16)

    def after(j, slot, g, carry):
        out = jnp.dot(second, hidden[slot, g], preferred_element_type=F32)
        done = out[: 2 * TILE] + carry
        for s in range(lanes // width):
            products.at[s][pl.ds(start_of(j, g), 2 * TILE), :] = done[:, s * width : (s + 1) * width]
        return out[2 * TILE :]

    blocks = rows // (2 * GROUP)
    for g in range(GROUP):
        before(0, 0, g)
    for g in range(GROUP):
        activate(0, g)
        before(1, 1, g)

    def two(i, carry):
        for j, slot in ((2 * i + 1, 1), (2 * i + 2, 0)):
            for g in range(GROUP):
                carry = after(j - 1, 1 - slot, g, carry)
                activate(slot, g)
                before(j + 1, 1 - slot, g)
        return carry

    carry = lax.fori_loop(0, (blocks - 2) // 2, two, jnp.zeros((2 * TILE, lanes), F32))
    for g in range(GROUP):
        carry = after(blocks - 2, 0, g, carry)
        activate(1, g)
    for g in range(GROUP):
        carry = after(blocks - 1, 1, g, carry)
    last = carry
    for s in range(lanes // width):
        own = slice(s * width, (s + 1) * width)
        products.at[s][rows * TILE : (rows + 2) * TILE, :] = last[:, own]
        for part in range(2):
            total = products.at[s][pl.ds(TILE + 2 + part, rows, stride=TILE), :]
            for dz in (0, 2):
                total += shifted(products.at[s][pl.ds(TILE + dz * 2 + part, rows, stride=TILE), :], dz - 1, width)
            result[part, :, own] = total


def fill_ones(taps_f32):
    taps_f32[...] = jnp.zeros(taps_f32.shape, F32)
    slices, rows, width = taps_f32.shape
    for s in range(slices):
        for at in (6, 7):
            taps_f32.at[s][pl.ds(at, rows // TILE, stride=TILE), :] = jnp.ones((rows // TILE, width), F32)


def first_refine_kernel(n_rows, n_weights, *refs):
    pieces, weights = refs[:n_rows], refs[n_rows : n_rows + n_weights]
    refined, planes, stage = refs[n_rows + n_weights : n_rows + n_weights + 3]
    scratch = refs[n_rows + n_weights + 3 :]
    per, _, width = pieces[0].shape
    fill_ones(scratch[0])
    for k, (_, _, source) in enumerate(own_and_peers("cuts")):
        block = pieces[k].shape[1]
        for s in range(per):
            stage.at[s][pl.ds(pl.multiple_of(source * block, 16), block), :] = pieces[k][s].astype(F32)
    height = stage.shape[1] // 2
    for s in range(per):
        for part in range(2):
            planes[part, :, s * width : (s + 1) * width] = stage.at[s][pl.ds(part, height, stride=2), :]
    refine_into([planes[0], planes[1]], of_cascade(weights, 0), scratch, refined, width)


def of_cascade(weights, cascade):
    at = step_to(cascade, "section")
    chosen = weights[0][...]
    for k in range(1, len(weights)):
        chosen = jnp.where(at == k, weights[k][...], chosen)
    return chosen


def cascades_kernel(n_weights, n_sens, n_more, n_data, by_cut, *refs):
    planes_in, first, mask, forward_z, back_z, forward_y, back_y = refs[:7]
    at = 7
    weights, at = refs[at : at + n_weights], at + n_weights
    senses, at = refs[at : at + n_sens], at + n_sens
    more, at = refs[at : at + n_more], at + n_more
    datas, at = refs[at : at + n_data], at + n_data
    out = refs[at]
    scratch = refs[at + 1 : -8]
    refined, planes, gradient, coil_planes, rows_z, rows_y, stage, all_weights = refs[-8:]
    per, _, height, width = datas[0].shape
    cascades = len(weights)
    cuts = out.shape[0] // cascades
    slab = lax.axis_index("section") // (lax.axis_size("section") // mask.shape[0])
    fill_ones(scratch[0])
    refined[...] = first[...]
    planes[...] = planes_in[...]
    for k in range(cascades):
        all_weights[k] = weights[k][...]
    weight_mask = mask[slab].astype(F32)
    weight_mask = jnp.concatenate([weight_mask] * 2, axis=0)

    def keep(n, rows):
        stage[n % stage.shape[0]] = rows.astype(F32)
        for part in range(2):
            plane = stage.at[n % stage.shape[0]][pl.ds(part, height, stride=2), :]
            coil_planes[n, part] = plane.astype(BF16)

    run_start = (lax.axis_index("cuts") * by_cut // cuts) * per
    n = 0
    for ref in senses:
        for s in range(per):
            keep(n, ref[run_start + s])
            n += 1
    for ref in more:
        for q in range(ref.shape[0]):
            for s in range(per):
                keep(n, ref[q, s])
                n += 1
    coils = n // per
    unroll = coils <= 8

    def each_coil(step):
        if unroll:
            for q in range(coils):
                step(q)
        else:
            lax.fori_loop(0, coils, lambda q, _: step(q), None)

    def cascade(c, _):
        def product(q):
            for s in range(per):
                lanes = slice(s * width, (s + 1) * width)
                sr, si = coil_planes[q * per + s, 0].astype(F32), coil_planes[q * per + s, 1].astype(F32)
                ir, ii = planes[0, :, lanes], planes[1, :, lanes]
                coil = jnp.concatenate([sr * ir - si * ii, sr * ii + si * ir], axis=1).astype(BF16)
                w = jnp.dot(coil, forward_z[...], preferred_element_type=F32).astype(BF16)
                rows_y[q * per + s] = jnp.concatenate([w[:, :width], w[:, width:]], axis=0)

        each_coil(product)

        def line(b, _):
            w = jnp.dot(forward_y[...], rows_y[b], preferred_element_type=F32)
            w = (w * weight_mask).astype(BF16)
            w = jnp.dot(back_y[...], w, preferred_element_type=F32).astype(BF16)
            rows_z[b] = jnp.concatenate([w[:height], w[height:]], axis=1)

        lax.fori_loop(0, coils * per, line, None, unroll=4)
        for s in range(per):
            lanes = slice(s * width, (s + 1) * width)
            for part in range(2):
                gradient[part, :, lanes] = sum(d[s, part].astype(F32) for d in datas)

        def gather(q):
            for s in range(per):
                lanes = slice(s * width, (s + 1) * width)
                sr, si = coil_planes[q * per + s, 0].astype(F32), coil_planes[q * per + s, 1].astype(F32)
                w = jnp.dot(rows_z[q * per + s], back_z[...], preferred_element_type=F32)
                br, bi = w[:, :width], w[:, width:]
                gradient[0, :, lanes] -= sr * br + si * bi
                gradient[1, :, lanes] -= sr * bi - si * br

        each_coil(gather)
        now = all_weights.at[step_to(c, "section")]
        step = sum(now[128 + piece : 129 + piece, 0:1].astype(F32) for piece in range(3))
        for part in range(2):
            new = (planes[part] - step * gradient[part] + refined[part]).astype(BF16).astype(F32)
            planes[part] = new
            for s in range(per):
                stage.at[s][pl.ds(part, height, stride=2), :] = new[:, s * width : (s + 1) * width]
        block = 2 * height // cuts
        for s in range(per):
            for cut in range(cuts):
                out[c * cuts + cut, s] = stage[s, cut * block : (cut + 1) * block].astype(BF16)

        @pl.when(c + 1 < cascades)
        def _():
            refine_into(
                [planes[0], planes[1]], all_weights[step_to(c + 1, "section")], scratch, refined, width
            )

    lax.fori_loop(0, cascades, cascade, None)


def refine_scratch(height, per, width, hid):
    rows, lanes = (height + 2) * TILE, per * width
    assert height % (4 * GROUP) == 0
    return [
        pltpu.VMEM((per, rows, width), F32),
        pltpu.VMEM((rows, lanes), BF16),
        pltpu.VMEM((per, rows, width), F32),
        pltpu.VMEM((2, GROUP, 2 * hid, lanes), ACT),
        pltpu.VMEM((2, GROUP, 2 * hid, lanes), BF16),
    ]


def first_refine(pieces, weights):
    per, block, width = pieces[0].shape
    rows = block * len(pieces)
    plane = near_out((2, rows // 2, per * width), F32)
    return pl.pallas_call(
        functools.partial(first_refine_kernel, len(pieces), len(weights)),
        out_shape=(plane, plane),
        in_specs=[VMEM] * (len(pieces) + len(weights)),
        out_specs=(VMEM, VMEM),
        scratch_shapes=[pltpu.VMEM((per, rows, width), F32)]
        + refine_scratch(rows // 2, per, width, weights[0].shape[-1]),
        interpret=INTERPRET,
    )(*[near(x) for x in [*pieces, *weights]])


def run_cascades(planes, first, mask, weights, senses, more, datas, cuts, by_cut):
    per, _, height, width = datas[0].shape
    lanes = per * width
    count = per * (len(senses) + sum(m.shape[0] for m in more))
    tables = [
        dft_table(width, 1.0),
        dft_table(width, -1.0),
        dft_table(height, 1.0).T.copy(),
        dft_table(height, -1.0).T.copy(),
    ]
    args = [planes, first, mask] + [jnp.asarray(t) for t in tables]
    args += list(weights) + list(senses) + list(more) + list(datas)
    return pl.pallas_call(
        functools.partial(
            cascades_kernel, len(weights), len(senses), len(more), len(datas), by_cut
        ),
        out_shape=jax.ShapeDtypeStruct((len(weights) * cuts, per, 2 * height // cuts, width), BF16),
        in_specs=[VMEM] * len(args),
        out_specs=VMEM,
        scratch_shapes=refine_scratch(height, per, width, weights[0].shape[-1])
        + [
            pltpu.VMEM((2, height, lanes), F32),
            pltpu.VMEM((2, height, lanes), F32),
            pltpu.VMEM((2, height, lanes), F32),
            pltpu.VMEM((count, 2, height, width), BF16),
            pltpu.VMEM((count, height, 2 * width), BF16),
            pltpu.VMEM((count, 2 * height, width), BF16),
            pltpu.VMEM((max(per, 4), 2 * height, width), F32),
            pltpu.VMEM((len(weights),) + weights[0].shape, BF16),
        ],
        interpret=INTERPRET,
    )(*[near(x) for x in args])


def split_kernel(place, sens, initial, chosen, conv_in, bias, conv_out, step, *refs):
    coils, cuts = lax.axis_size("coil"), lax.axis_size("cuts")
    sens_out, initial_out, packed, sems = refs[:coils], refs[coils : coils + cuts], refs[-2], refs[-1]
    slab, block = place.slab(), place.half_block()
    copies = []
    for k, (_, target, _) in enumerate(own_and_peers("coil")):
        source = sens.at[slab, 0, pl.ds(target * place.owned + block * place.run, place.run)]
        copies.append(pltpu.make_async_copy(source, sens_out[k], sems.at[k]))
    for k, (_, target, _) in enumerate(own_and_peers("cuts")):
        start = block * place.run + place.cut_block(target) * place.per
        source = initial.at[slab, pl.ds(start, place.per)]
        copies.append(pltpu.make_async_copy(source, initial_out[k], sems.at[coils + k]))
    for copy in copies:
        copy.start()
    pack_into(packed, chosen, conv_in, bias, conv_out, step)
    for copy in copies:
        copy.wait()


def split(place, sens, initial, conv_in, bias, conv_out, step):
    coils, cuts = lax.axis_size("coil"), lax.axis_size("cuts")
    chosen = jnp.asarray(selections())
    outs = [near_out((place.run,) + sens.shape[-2:], BF16)] * coils
    outs += [near_out((place.per,) + initial.shape[-2:], BF16)] * cuts
    outs += [near_out((chosen.shape[0], bias.shape[1]), BF16)]
    made = pl.pallas_call(
        functools.partial(split_kernel, place),
        out_shape=outs,
        in_specs=[ANY, ANY, VMEM, VMEM, VMEM, VMEM, SMEM],
        out_specs=[VMEM] * len(outs),
        scratch_shapes=[pltpu.SemaphoreType.DMA((coils + cuts,))],
        interpret=INTERPRET,
    )(sens, initial, chosen, conv_in.T, bias, conv_out, step)
    return made[:coils], made[coils:-1], made[-1]


def partners_kernel(place, *refs):
    coils = lax.axis_size("coil")
    senses, outs = refs[:coils], refs[coils:]
    for k, (_, target, _) in enumerate(peers("cuts")):
        for q in range(coils):
            outs[k][q] = senses[q][pl.ds(place.cut_block(target) * place.per, place.per)]


def for_partners(place, senses):
    coils, cuts = lax.axis_size("coil"), lax.axis_size("cuts")
    outs = [near_out((coils, place.per) + senses[0].shape[-2:], BF16)] * (cuts - 1)
    return pl.pallas_call(
        functools.partial(partners_kernel, place),
        out_shape=outs,
        in_specs=[VMEM] * coils,
        out_specs=[VMEM] * len(outs),
        interpret=INTERPRET,
    )(*[near(x) for x in senses])


CHUNKS = 4


def adjoint_kernel(place, kspace, sens, mask, tables_x, back_y, back_z, *refs):
    coils, cuts = lax.axis_size("coil"), lax.axis_size("cuts")
    outs = refs[:cuts]
    data, own_sens, table_x, planes, rows_z, stage, sems = refs[cuts:]
    size_x, rows, width = data.shape
    height = rows // 2
    kept = coils * place.run
    slab, block = place.slab(), place.half_block()
    chunk = size_x // CHUNKS
    copies = [pltpu.make_async_copy(tables_x.at[block], table_x, sems.at[0])]
    for i in range(CHUNKS):
        at = pl.ds(i * chunk, chunk)
        copies.append(pltpu.make_async_copy(kspace.at[slab, 0, at], data.at[at], sems.at[1 + i]))
    first_sens = len(copies)
    for q in range(coils):
        source = sens.at[slab, 0, pl.ds(q * place.owned + block * place.run, place.run)]
        target = own_sens.at[pl.ds(q * place.run, place.run)]
        copies.append(pltpu.make_async_copy(source, target, sems.at[first_sens + q]))
    for copy in copies:
        copy.start()
    for copy in copies[:first_sens]:
        copy.wait()
    weight_mask = mask[slab].astype(F32)
    groups = rows // (2 * TILE)
    for g in range(0, groups, 2):
        both = [
            data[:, (g + i) * 2 * TILE : (g + i + 1) * 2 * TILE, :].reshape(size_x * 2 * TILE, width)
            for i in range(2)
        ]
        w = jnp.dot(table_x[...], jnp.concatenate(both, axis=1), preferred_element_type=F32)
        for i in range(2):
            at = slice((g + i) * TILE, (g + i + 1) * TILE)
            part = w[:, i * width : (i + 1) * width].reshape(2 * kept, TILE, width)
            planes[:, at, :] = part * weight_mask[at][None]
    for n in range(0, kept, 2):
        pair = [
            jnp.concatenate([planes[2 * (n + i)], planes[2 * (n + i) + 1]], axis=0).astype(BF16)
            for i in range(2)
        ]
        w = jnp.dot(back_y[...], jnp.concatenate(pair, axis=1), preferred_element_type=F32).astype(BF16)
        for i in range(2):
            lanes = slice(i * width, (i + 1) * width)
            rows_z[n + i] = jnp.concatenate([w[:height, lanes], w[height:, lanes]], axis=1)
    for copy in copies[first_sens:]:
        copy.wait()
    for k, (_, target, _) in enumerate(own_and_peers("cuts")):
        for q in range(coils):
            for s in range(place.per):
                n = q * place.run + place.cut_block(target) * place.per + s
                w = jnp.dot(rows_z[n], back_z[...], preferred_element_type=F32)
                br, bi = w[:, :width], w[:, width:]
                slot = stage.at[(q * place.per + s) % stage.shape[0]]
                slot[...] = own_sens[n].astype(F32)
                sr, si = (slot[pl.ds(part, height, stride=2), :] for part in range(2))
                outs[k][q, s, 0] = (sr * br + si * bi).astype(BF16)
                outs[k][q, s, 1] = (sr * bi - si * br).astype(BF16)


def adjoint(place, kspace, sens, mask):
    coils, cuts = lax.axis_size("coil"), lax.axis_size("cuts")
    size_x, rows, width = kspace.shape[-3:]
    height = rows // 2
    kept = coils * place.run
    table = dft_table(size_x, -1.0).reshape(2, size_x, 2, coils, place.by_half, place.run)
    table = np.einsum("cxdqbr,uv->bqrduxvc", table.astype(np.float32), np.eye(TILE, dtype=np.float32))
    table = table.reshape(place.by_half, 2 * kept * TILE, 2 * size_x * TILE).astype(ml_dtypes.bfloat16)
    tables = [jnp.asarray(t) for t in (table, dft_table(height, -1.0).T.copy(), dft_table(width, -1.0))]
    return pl.pallas_call(
        functools.partial(adjoint_kernel, place),
        out_shape=[near_out((coils, place.per, 2, height, width), BF16)] * cuts,
        in_specs=[ANY, ANY, VMEM, ANY, VMEM, VMEM],
        out_specs=[VMEM] * cuts,
        scratch_shapes=[
            pltpu.VMEM((size_x, rows, width), BF16),
            pltpu.VMEM((kept, rows, width), BF16),
            pltpu.VMEM(table.shape[1:], BF16),
            pltpu.VMEM((2 * kept, height, width), F32),
            pltpu.VMEM((kept, height, 2 * width), BF16),
            pltpu.VMEM((4, rows, width), F32),
            pltpu.SemaphoreType.DMA((1 + CHUNKS + coils,)),
        ],
        interpret=INTERPRET,
    )(kspace, sens, near(mask), tables[0], near(tables[1]), near(tables[2]))


def pair_sum_kernel(n_in, *refs):
    terms, outs = refs[:n_in], refs[n_in:]
    for k, (_, target, _) in enumerate(own_and_peers("coil")):
        outs[k][...] = sum(t[target].astype(F32) for t in terms).astype(BF16)


def pair_sum(terms):
    coils = lax.axis_size("coil")
    return pl.pallas_call(
        functools.partial(pair_sum_kernel, len(terms)),
        out_shape=[near_out(terms[0].shape[1:], BF16)] * coils,
        in_specs=[VMEM] * len(terms),
        out_specs=[VMEM] * coils,
        interpret=INTERPRET,
    )(*[near(t) for t in terms])


class Place:
    def __init__(self, slabs, size_x):
        sections, coils, cuts = (lax.axis_size(a) for a in ("section", "coil", "cuts"))
        self.slabs, self.cuts, self.halves = slabs, cuts, sections // slabs
        self.owned = size_x // coils
        self.by_half = math.gcd(self.owned, self.halves)
        self.by_cut = math.gcd(self.owned // self.by_half, cuts)
        self.per = self.owned // (self.by_half * self.by_cut)
        self.run = self.by_cut * self.per

    def slab(self):
        return lax.axis_index("section") // self.halves

    def half_block(self):
        return lax.axis_index("section") % self.halves * self.by_half // self.halves

    def cut_block(self, cut):
        return cut * self.by_cut // self.cuts


def sent(pieces, axis):
    arrived = [pieces[0]]
    for k, (route, _, _) in enumerate(peers(axis)):
        arrived.append(lax.ppermute(pieces[k + 1], axis, route))
    return arrived


def body(initial, sens, kspace, mask, step_sizes, conv_in, bias_in, conv_out):
    slabs, _, size_x, size_y, _, size_z = sens.shape
    sections, cuts = lax.axis_size("section"), lax.axis_size("cuts")
    place = Place(slabs, size_x)
    rows = size_y // cuts

    def joined(array):
        return array.reshape(array.shape[:-3] + (array.shape[-3] * 2, size_z))

    initial, sens, kspace = joined(initial), joined(sens), joined(kspace)
    sens_pieces, image_pieces, packed = split(place, sens, initial, conv_in[0], bias_in, conv_out[0], step_sizes)
    senses = sent(sens_pieces, "coil")
    weights = sent([packed] * sections, "section")
    image_pieces = sent(image_pieces, "cuts")
    terms = adjoint(place, kspace, sens, mask)
    terms = sent(terms, "cuts")
    sums = pair_sum(terms)
    datas = sent(sums, "coil")
    given = for_partners(place, senses)
    more = sent([None] + list(given), "cuts")[1:]
    first, planes = first_refine(image_pieces, weights)
    out = run_cascades(planes, first, mask, weights, senses, more, datas, cuts, place.by_cut)
    out = lax.all_to_all(out, ("section", "cuts"), 0, 0, tiled=True)
    out = out.reshape(slabs, place.halves, cuts, place.per, rows, 2, size_z)
    out = out[:, :: place.halves // place.by_half, :: cuts // place.by_cut]
    return out.reshape(1, slabs, place.owned, rows, 2, size_z)


def solution(mesh):
    return jax.shard_map(
        body,
        mesh=mesh,
        in_specs=(
            P(None, "coil", "cuts", None, None),
            P(None, ("coil", "cuts"), None, None, None, None),
            P(None, ("coil", "cuts"), None, None, None, None),
            P(),
            P("section"),
            P("section", None, None),
            P("section", None),
            P("section", None, None),
        ),
        out_specs=P("section", None, "coil", "cuts", None, None),
        check_vma=False,
    )
```

```python
import functools
import math

import jax
import jax.numpy as jnp
import ml_dtypes
import numpy as np
from jax import lax
from jax.experimental import pallas as pl
from jax.experimental.pallas import tpu as pltpu
from jax.sharding import PartitionSpec as P


INTERPRET = False
BF16, F32 = jnp.bfloat16, jnp.float32
ACT = F32
GROUP = 4
TILE = 8


def dft_table(length, sign):
    ramp = np.arange(length)
    angle = (ramp[:, None] * ramp[None, :] % length) * (2.0 * math.pi / length)
    cosine = np.cos(angle) / math.sqrt(length)
    sine = sign * np.sin(angle) / math.sqrt(length)
    return np.block([[cosine, -sine], [sine, cosine]]).astype(ml_dtypes.bfloat16)


def peers(axis):
    count = lax.axis_size(axis)
    me = lax.axis_index(axis)
    for k in range(1, count):
        if count & (count - 1) == 0:
            yield [(j, j ^ k) for j in range(count)], jnp.bitwise_xor(me, k), jnp.bitwise_xor(me, k)
        else:
            route = [(j, (j + k) % count) for j in range(count)]
            yield route, (me + k) % count, (me - k) % count


def own_and_peers(axis):
    me = lax.axis_index(axis)
    yield None, me, me
    yield from peers(axis)


def step_to(index, axis):
    count = lax.axis_size(axis)
    me = lax.axis_index(axis)
    if count & (count - 1) == 0:
        return jnp.bitwise_xor(me, index)
    return (me - index) % count


SMEM = pl.BlockSpec(memory_space=pltpu.SMEM)
VMEM = pl.BlockSpec(memory_space=pltpu.VMEM)
ANY = pl.BlockSpec(memory_space=pl.ANY)


def far():
    return INTERPRET or lax.axis_size("coil") > 8


def near(x):
    return x if far() else pltpu.with_memory_space_constraint(x, pltpu.VMEM)


def away(x):
    return x if INTERPRET else pltpu.with_memory_space_constraint(x, pltpu.HBM)


def near_out(shape, dtype):
    return jax.ShapeDtypeStruct(shape, dtype) if far() else pltpu.VMEM(shape, dtype)


def kernel_params():
    return None if far() else pltpu.CompilerParams(vmem_limit_bytes=20 << 20)


def selections():
    chosen = np.zeros((4 * 4 * TILE + TILE, 42), np.float32)
    for dy in range(3):
        for dz in range(3):
            for part in range(2):
                tap = (3 * dy + dz) * 2 + part
                for row in range(2):
                    chosen[row * 32 + (row + dy) * TILE + dz * 2 + part, tap] = 0.5
                    chosen[64 + row * 32 + (row + 2 - dy) * TILE + dz * 2 + part, 21 + tap] = 1.0
    for row in range(2):
        for piece, at in enumerate((TILE + 6, TILE + 7, 2 * TILE + 6)):
            chosen[row * 32 + at, 18 + piece] = 0.5
    for piece in range(3):
        chosen[128 + piece, 39 + piece] = 1.0
    return chosen.astype(ml_dtypes.bfloat16)


def in_three(x):
    high = x.astype(BF16)
    rest = x - high.astype(F32)
    mid = rest.astype(BF16)
    return [high, mid, (rest - mid.astype(F32)).astype(BF16)]


def pack_into(packed, chosen, conv_in, bias, conv_out, step):
    def picked(rows, lanes):
        return jnp.dot(chosen[:, lanes], rows, preferred_element_type=F32)

    total = picked(conv_in[...], slice(0, 18)) + picked(conv_out[...], slice(21, 39))
    steps = jnp.full(bias.shape, step[0], F32)
    for at, split in ((18, in_three(bias[...])), (39, in_three(steps))):
        for piece, row in enumerate(split):
            column = chosen[:, at + piece : at + piece + 1].astype(F32)
            total += column * row.astype(F32)
    packed[...] = total.astype(BF16)


def shifted(plane, by, width):
    lane = lax.broadcasted_iota(jnp.int32, (plane.shape[0], width), 1)
    parts = []
    for at in range(0, plane.shape[1], width):
        moved = pltpu.roll(plane[:, at : at + width], (-by) % width, 1)
        parts.append(jnp.where((lane + by >= 0) & (lane + by < width), moved, 0.0))
    return jnp.concatenate(parts, axis=1)


def refine_into(planes, weights, scratch, result, width):
    rows, lanes = planes[0].shape
    taps_f32, taps, products, halves, hidden = scratch
    for dz in range(3):
        for part in range(2):
            plane = planes[part] if dz == 1 else shifted(planes[part], dz - 1, width)
            for s in range(lanes // width):
                place = pl.ds(TILE + dz * 2 + part, rows, stride=TILE)
                taps_f32.at[s][place, :] = plane[:, s * width : (s + 1) * width]
    for s in range(lanes // width):
        taps[:, s * width : (s + 1) * width] = taps_f32[s].astype(BF16)
    packed = weights.astype(F32)
    first = jnp.concatenate([packed[0:32].T, packed[32:64].T], axis=0).astype(BF16)
    second = jnp.concatenate([weights[64:96], weights[96:128]], axis=1)

    def start_of(j, g):
        start = (j * GROUP + g) * 2 * TILE
        return start if isinstance(start, int) else pl.multiple_of(start, 2 * TILE)

    def before(j, slot, g):
        window = taps[pl.ds(start_of(j, g), 4 * TILE), :]
        halves[slot, g] = jnp.dot(first, window, preferred_element_type=F32).astype(halves.dtype)

    def activate(slot, g):
        half = halves[slot, g]
        hidden[slot, g] = (half + half * jnp.tanh(half)).astype(BF16)

    def after(j, slot, g, carry):
        out = jnp.dot(second, hidden[slot, g], preferred_element_type=F32)
        done = out[: 2 * TILE] + carry
        for s in range(lanes // width):
            products.at[s][pl.ds(start_of(j, g), 2 * TILE), :] = done[:, s * width : (s + 1) * width]
        return out[2 * TILE :]

    blocks = rows // (2 * GROUP)
    for g in range(GROUP):
        before(0, 0, g)
    for g in range(GROUP):
        activate(0, g)
        before(1, 1, g)

    def two(i, carry):
        for j, slot in ((2 * i + 1, 1), (2 * i + 2, 0)):
            for g in range(GROUP):
                carry = after(j - 1, 1 - slot, g, carry)
                activate(slot, g)
                before(j + 1, 1 - slot, g)
        return carry

    carry = lax.fori_loop(0, (blocks - 2) // 2, two, jnp.zeros((2 * TILE, lanes), F32))
    for g in range(GROUP):
        carry = after(blocks - 2, 0, g, carry)
        activate(1, g)
    for g in range(GROUP):
        carry = after(blocks - 1, 1, g, carry)
    last = carry
    for s in range(lanes // width):
        own = slice(s * width, (s + 1) * width)
        products.at[s][rows * TILE : (rows + 2) * TILE, :] = last[:, own]
        for part in range(2):
            total = products.at[s][pl.ds(TILE + 2 + part, rows, stride=TILE), :]
            for dz in (0, 2):
                total += shifted(products.at[s][pl.ds(TILE + dz * 2 + part, rows, stride=TILE), :], dz - 1, width)
            result[part, :, own] = total


def fill_ones(taps_f32):
    taps_f32[...] = jnp.zeros(taps_f32.shape, F32)
    slices, rows, width = taps_f32.shape
    for s in range(slices):
        for at in (6, 7):
            taps_f32.at[s][pl.ds(at, rows // TILE, stride=TILE), :] = jnp.ones((rows // TILE, width), F32)


def first_refine_kernel(n_rows, n_weights, *refs):
    pieces, weights = refs[:n_rows], refs[n_rows : n_rows + n_weights]
    refined, planes, stage = refs[n_rows + n_weights : n_rows + n_weights + 3]
    scratch = refs[n_rows + n_weights + 3 :]
    per, _, width = pieces[0].shape
    fill_ones(scratch[0])
    for k, (_, _, source) in enumerate(own_and_peers("cuts")):
        block = pieces[k].shape[1]
        for s in range(per):
            stage.at[s][pl.ds(pl.multiple_of(source * block, 16), block), :] = pieces[k][s].astype(F32)
    height = stage.shape[1] // 2
    for s in range(per):
        for part in range(2):
            planes[part, :, s * width : (s + 1) * width] = stage.at[s][pl.ds(part, height, stride=2), :]
    refine_into([planes[0], planes[1]], of_cascade(weights, 0), scratch, refined, width)


def of_cascade(weights, cascade):
    at = step_to(cascade, "section")
    chosen = weights[0][...]
    for k in range(1, len(weights)):
        chosen = jnp.where(at == k, weights[k][...], chosen)
    return chosen


def subtract_normal(planes, coil_planes, weight_mask, tables, gradient, rows_y, rows_z):
    forward_z, back_z, forward_y, back_y = tables
    count, _, height, width = coil_planes.shape
    per = planes.shape[2] // width
    assert per <= 2
    pairs = count // 2

    def each_pair(step):
        if pairs <= 8:
            for m in range(pairs):
                step(m)
        else:
            lax.fori_loop(0, pairs, lambda m, _: step(m), None)

    def sens_and_lanes(m, i):
        n, s = 2 * m + i, i % per
        sens = coil_planes[n, 0].astype(F32), coil_planes[n, 1].astype(F32)
        return *sens, slice(s * width, (s + 1) * width)

    def product(m):
        coils = []
        for i in range(2):
            sr, si, lanes = sens_and_lanes(m, i)
            ir, ii = planes[0, :, lanes], planes[1, :, lanes]
            coils.append(jnp.concatenate([sr * ir - si * ii, sr * ii + si * ir], axis=1).astype(BF16))
        w = jnp.dot(jnp.concatenate(coils, axis=0), forward_z[...], preferred_element_type=F32)
        w = w.astype(BF16)
        for i in range(2):
            for part in range(2):
                block = w[i * height : (i + 1) * height, part * width : (part + 1) * width]
                rows_y[m, part * height : (part + 1) * height, i * width : (i + 1) * width] = block

    def forward(m):
        w = jnp.dot(forward_y[...], rows_y[m], preferred_element_type=F32)
        for i in range(2):
            lanes = slice(i * width, (i + 1) * width)
            rows_y[m, :, lanes] = (w[:, lanes] * weight_mask).astype(BF16)

    def back(m):
        w = jnp.dot(back_y[...], rows_y[m], preferred_element_type=F32).astype(BF16)
        for i in range(2):
            for part in range(2):
                block = w[part * height : (part + 1) * height, i * width : (i + 1) * width]
                rows_z[m, i * height : (i + 1) * height, part * width : (part + 1) * width] = block

    def gather(m):
        w = jnp.dot(rows_z[m], back_z[...], preferred_element_type=F32)
        for i in range(2):
            sr, si, lanes = sens_and_lanes(m, i)
            br = w[i * height : (i + 1) * height, :width]
            bi = w[i * height : (i + 1) * height, width:]
            gradient[0, :, lanes] -= sr * br + si * bi
            gradient[1, :, lanes] -= sr * bi - si * br

    for stage in (product, forward, back, gather):
        each_pair(stage)


def mask_of(place, mask):
    weight_mask = mask[place.slab()].astype(F32)
    return jnp.concatenate([weight_mask] * 2, axis=0)


def first_normal_kernel(place, n_sens, planes, mask, *refs):
    tables, senses, more = refs[:4], refs[4 : 4 + n_sens], refs[4 + n_sens : -5]
    coil_planes, normal, rows_y, rows_z, stage = refs[-5:]
    height = coil_planes.shape[2]

    def keep(n, rows):
        slot = stage.at[n % stage.shape[0]]
        slot[...] = rows.astype(F32)
        for part in range(2):
            coil_planes[n, part] = slot[pl.ds(part, height, stride=2), :].astype(BF16)

    start = place.cut_block(lax.axis_index("cuts")) * place.per
    n = 0
    for ref in senses:
        for s in range(place.per):
            keep(n, ref[start + s])
            n += 1
    for ref in more:
        for q in range(ref.shape[0]):
            for s in range(place.per):
                keep(n, ref[q, s])
                n += 1
    normal[...] = jnp.zeros(normal.shape, F32)
    subtract_normal(planes, coil_planes, mask_of(place, mask), tables, normal, rows_y, rows_z)


def cascades_kernel(place, n_weights, n_data, *refs):
    planes_in, first, normal, coil_planes, mask = refs[:5]
    tables, at = refs[5:9], 9
    weights, at = refs[at : at + n_weights], at + n_weights
    datas, at = refs[at : at + n_data], at + n_data
    out = refs[at]
    scratch = refs[at + 1 : -8]
    refined, planes, data, gradient, rows_y, rows_z, stage, all_weights = refs[-8:]
    per, _, height, width = datas[0].shape
    cascades = len(weights)
    cuts = out.shape[0] // cascades
    fill_ones(scratch[0])
    refined[...] = first[...]
    planes[...] = planes_in[...]
    for k in range(cascades):
        all_weights[k] = weights[k][...]
    for s in range(per):
        for part in range(2):
            data[part, :, s * width : (s + 1) * width] = sum(d[s, part].astype(F32) for d in datas)
    gradient[...] = data[...] + normal[...]
    weight_mask = mask_of(place, mask)

    def cascade(c, _):
        now = all_weights.at[step_to(c, "section")]
        step = sum(now[128 + piece : 129 + piece, 0:1].astype(F32) for piece in range(3))
        for part in range(2):
            new = (planes[part] - step * gradient[part] + refined[part]).astype(BF16).astype(F32)
            planes[part] = new
            for s in range(per):
                stage.at[s][pl.ds(part, height, stride=2), :] = new[:, s * width : (s + 1) * width]
        block = 2 * height // cuts
        for s in range(per):
            for cut in range(cuts):
                out[c * cuts + cut, s] = stage[s, cut * block : (cut + 1) * block].astype(BF16)

        @pl.when(c + 1 < cascades)
        def _():
            refine_into(
                [planes[0], planes[1]], all_weights[step_to(c + 1, "section")], scratch, refined, width
            )
            gradient[...] = data[...]
            subtract_normal(planes, coil_planes, weight_mask, tables, gradient, rows_y, rows_z)

    lax.fori_loop(0, cascades, cascade, None)


def refine_scratch(height, per, width, hid):
    rows, lanes = (height + 2) * TILE, per * width
    assert height % (4 * GROUP) == 0
    return [
        pltpu.VMEM((per, rows, width), F32),
        pltpu.VMEM((rows, lanes), BF16),
        pltpu.VMEM((per, rows, width), F32),
        pltpu.VMEM((2, GROUP, 2 * hid, lanes), ACT),
        pltpu.VMEM((2, GROUP, 2 * hid, lanes), BF16),
    ]


def first_refine(pieces, weights):
    per, block, width = pieces[0].shape
    rows = block * len(pieces)
    plane = near_out((2, rows // 2, per * width), F32)
    return pl.pallas_call(
        functools.partial(first_refine_kernel, len(pieces), len(weights)),
        out_shape=(plane, plane),
        in_specs=[VMEM] * (len(pieces) + len(weights)),
        out_specs=(VMEM, VMEM),
        scratch_shapes=[pltpu.VMEM((per, rows, width), F32)]
        + refine_scratch(rows // 2, per, width, weights[0].shape[-1]),
        compiler_params=kernel_params(),
        interpret=INTERPRET,
    )(*[near(x) for x in [*pieces, *weights]])


def pass_tables(height, width):
    tables = [
        dft_table(width, 1.0),
        dft_table(width, -1.0),
        dft_table(height, 1.0).T.copy(),
        dft_table(height, -1.0).T.copy(),
    ]
    return [near(jnp.asarray(t)) for t in tables]


def pass_scratch(count, height, width):
    return [
        pltpu.VMEM((count // 2, 2 * height, 2 * width), BF16),
        pltpu.VMEM((count // 2, 2 * height, 2 * width), BF16),
    ]


def first_normal(place, planes, mask, senses, more):
    _, height, lanes = planes.shape
    width = senses[0].shape[-1]
    count = place.per * (len(senses) + sum(m.shape[0] for m in more))
    args = [planes, mask] + pass_tables(height, width) + list(senses) + list(more)
    return pl.pallas_call(
        functools.partial(first_normal_kernel, place, len(senses)),
        out_shape=[near_out((count, 2, height, width), BF16), near_out((2, height, lanes), F32)],
        in_specs=[VMEM] * len(args),
        out_specs=[VMEM] * 2,
        scratch_shapes=pass_scratch(count, height, width) + [pltpu.VMEM((4, 2 * height, width), F32)],
        compiler_params=kernel_params(),
        interpret=INTERPRET,
    )(*[near(x) for x in args])


def run_cascades(place, planes, first, normal, coil_planes, mask, weights, datas, cuts):
    per, _, height, width = datas[0].shape
    lanes = per * width
    count = coil_planes.shape[0]
    args = [planes, first, normal, coil_planes, mask] + pass_tables(height, width)
    args += list(weights) + list(datas)
    return pl.pallas_call(
        functools.partial(cascades_kernel, place, len(weights), len(datas)),
        out_shape=jax.ShapeDtypeStruct((len(weights) * cuts, per, 2 * height // cuts, width), BF16),
        in_specs=[VMEM] * len(args),
        out_specs=VMEM,
        scratch_shapes=refine_scratch(height, per, width, weights[0].shape[-1])
        + [pltpu.VMEM((2, height, lanes), F32)] * 4
        + pass_scratch(count, height, width)
        + [
            pltpu.VMEM((per, 2 * height, width), F32),
            pltpu.VMEM((len(weights),) + weights[0].shape, BF16),
        ],
        compiler_params=kernel_params(),
        interpret=INTERPRET,
    )(*[near(x) for x in args])


def split_kernel(place, sens, initial, *refs):
    coils, cuts = lax.axis_size("coil"), lax.axis_size("cuts")
    small, step, refs = refs[:4], refs[4], refs[5:]
    sens_out, initial_out, packed = refs[:coils], refs[coils : coils + cuts], refs[coils + cuts]
    held, sems = refs[coils + cuts + 1 : -1], refs[-1]
    slab, block = place.slab(), place.half_block()
    copies = []
    for k, (_, target, _) in enumerate(own_and_peers("coil")):
        source = sens.at[slab, 0, pl.ds(target * place.owned + block * place.run, place.run)]
        copies.append(pltpu.make_async_copy(source, sens_out[k], sems.at[k]))
    for k, (_, target, _) in enumerate(own_and_peers("cuts")):
        start = block * place.run + place.cut_block(target) * place.per
        source = initial.at[slab, pl.ds(start, place.per)]
        copies.append(pltpu.make_async_copy(source, initial_out[k], sems.at[coils + k]))
    for k, (source, target) in enumerate(zip(small, held)):
        copies.append(pltpu.make_async_copy(source, target, sems.at[coils + cuts + k]))
    for copy in copies:
        copy.start()
    for copy in copies[coils + cuts :]:
        copy.wait()
    pack_into(packed, *held, step)
    for copy in copies[: coils + cuts]:
        copy.wait()


def split(place, sens, initial, conv_in, bias, conv_out, step):
    coils, cuts = lax.axis_size("coil"), lax.axis_size("cuts")
    chosen = jnp.asarray(selections())
    small = [chosen, conv_in.T, bias, conv_out]
    outs = [near_out((place.run,) + sens.shape[-2:], BF16)] * coils
    outs += [near_out((place.per,) + initial.shape[-2:], BF16)] * cuts
    outs += [near_out((chosen.shape[0], bias.shape[1]), BF16)]
    made = pl.pallas_call(
        functools.partial(split_kernel, place),
        out_shape=outs,
        in_specs=[ANY] * 6 + [SMEM],
        out_specs=[VMEM] * len(outs),
        scratch_shapes=[pltpu.VMEM(x.shape, x.dtype) for x in small]
        + [pltpu.SemaphoreType.DMA((coils + cuts + len(small),))],
        compiler_params=kernel_params(),
        interpret=INTERPRET,
    )(*[away(x) for x in [sens, initial] + small], step)
    return made[:coils], made[coils:-1], made[-1]


def partners_kernel(place, *refs):
    coils = lax.axis_size("coil")
    senses, outs = refs[:coils], refs[coils:]
    for k, (_, target, _) in enumerate(peers("cuts")):
        for q in range(coils):
            outs[k][q] = senses[q][pl.ds(place.cut_block(target) * place.per, place.per)]


def for_partners(place, senses):
    coils, cuts = lax.axis_size("coil"), lax.axis_size("cuts")
    outs = [near_out((coils, place.per) + senses[0].shape[-2:], BF16)] * (cuts - 1)
    return pl.pallas_call(
        functools.partial(partners_kernel, place),
        out_shape=outs,
        in_specs=[VMEM] * coils,
        out_specs=[VMEM] * len(outs),
        compiler_params=kernel_params(),
        interpret=INTERPRET,
    )(*[near(x) for x in senses])


CHUNKS = 4


def adjoint_kernel(place, kspace, sens, mask, tables_x, back_y, back_z, *refs):
    coils, cuts = lax.axis_size("coil"), lax.axis_size("cuts")
    outs = refs[:cuts]
    data, own_sens, table_x, planes, rows_z, stage, sems = refs[cuts:]
    size_x, rows, width = data.shape
    height = rows // 2
    kept = coils * place.run
    slab, block = place.slab(), place.half_block()
    chunk = size_x // CHUNKS
    copies = [pltpu.make_async_copy(tables_x.at[block], table_x, sems.at[0])]
    for i in range(CHUNKS):
        at = pl.ds(i * chunk, chunk)
        copies.append(pltpu.make_async_copy(kspace.at[slab, 0, at], data.at[at], sems.at[1 + i]))
    first_sens = len(copies)
    for q in range(coils):
        source = sens.at[slab, 0, pl.ds(q * place.owned + block * place.run, place.run)]
        target = own_sens.at[pl.ds(q * place.run, place.run)]
        copies.append(pltpu.make_async_copy(source, target, sems.at[first_sens + q]))
    for copy in copies:
        copy.start()
    for copy in copies[:first_sens]:
        copy.wait()
    weight_mask = mask[slab].astype(F32)
    groups = rows // (2 * TILE)
    for g in range(0, groups, 2):
        both = [
            data[:, (g + i) * 2 * TILE : (g + i + 1) * 2 * TILE, :].reshape(size_x * 2 * TILE, width)
            for i in range(2)
        ]
        w = jnp.dot(table_x[...], jnp.concatenate(both, axis=1), preferred_element_type=F32)
        for i in range(2):
            at = slice((g + i) * TILE, (g + i + 1) * TILE)
            part = w[:, i * width : (i + 1) * width].reshape(2 * kept, TILE, width)
            planes[:, at, :] = part * weight_mask[at][None]
    for n in range(0, kept, 2):
        pair = [
            jnp.concatenate([planes[2 * (n + i)], planes[2 * (n + i) + 1]], axis=0).astype(BF16)
            for i in range(2)
        ]
        w = jnp.dot(back_y[...], jnp.concatenate(pair, axis=1), preferred_element_type=F32).astype(BF16)
        for i in range(2):
            lanes = slice(i * width, (i + 1) * width)
            rows_z[n + i] = jnp.concatenate([w[:height, lanes], w[height:, lanes]], axis=1)
    for copy in copies[first_sens:]:
        copy.wait()
    for k, (_, target, _) in enumerate(own_and_peers("cuts")):
        for q in range(coils):
            for s in range(place.per):
                n = q * place.run + place.cut_block(target) * place.per + s
                w = jnp.dot(rows_z[n], back_z[...], preferred_element_type=F32)
                br, bi = w[:, :width], w[:, width:]
                slot = stage.at[(q * place.per + s) % stage.shape[0]]
                slot[...] = own_sens[n].astype(F32)
                sr, si = (slot[pl.ds(part, height, stride=2), :] for part in range(2))
                outs[k][q, s, 0] = (sr * br + si * bi).astype(BF16)
                outs[k][q, s, 1] = (sr * bi - si * br).astype(BF16)


def adjoint(place, kspace, sens, mask):
    coils, cuts = lax.axis_size("coil"), lax.axis_size("cuts")
    size_x, rows, width = kspace.shape[-3:]
    height = rows // 2
    kept = coils * place.run
    table = dft_table(size_x, -1.0).reshape(2, size_x, 2, coils, place.by_half, place.run)
    table = np.einsum("cxdqbr,uv->bqrduxvc", table.astype(np.float32), np.eye(TILE, dtype=np.float32))
    table = table.reshape(place.by_half, 2 * kept * TILE, 2 * size_x * TILE).astype(ml_dtypes.bfloat16)
    tables = [jnp.asarray(t) for t in (table, dft_table(height, -1.0).T.copy(), dft_table(width, -1.0))]
    return pl.pallas_call(
        functools.partial(adjoint_kernel, place),
        out_shape=[near_out((coils, place.per, 2, height, width), BF16)] * cuts,
        in_specs=[ANY, ANY, VMEM, ANY, VMEM, VMEM],
        out_specs=[VMEM] * cuts,
        scratch_shapes=[
            pltpu.VMEM((size_x, rows, width), BF16),
            pltpu.VMEM((kept, rows, width), BF16),
            pltpu.VMEM(table.shape[1:], BF16),
            pltpu.VMEM((2 * kept, height, width), F32),
            pltpu.VMEM((kept, height, 2 * width), BF16),
            pltpu.VMEM((4, rows, width), F32),
            pltpu.SemaphoreType.DMA((1 + CHUNKS + coils,)),
        ],
        compiler_params=kernel_params(),
        interpret=INTERPRET,
    )(away(kspace), away(sens), near(mask), away(tables[0]), near(tables[1]), near(tables[2]))


def pair_sum_kernel(n_in, *refs):
    terms, outs = refs[:n_in], refs[n_in:]
    for k, (_, target, _) in enumerate(own_and_peers("coil")):
        outs[k][...] = sum(t[target].astype(F32) for t in terms).astype(BF16)


def pair_sum(terms):
    coils = lax.axis_size("coil")
    return pl.pallas_call(
        functools.partial(pair_sum_kernel, len(terms)),
        out_shape=[near_out(terms[0].shape[1:], BF16)] * coils,
        in_specs=[VMEM] * len(terms),
        out_specs=[VMEM] * coils,
        compiler_params=kernel_params(),
        interpret=INTERPRET,
    )(*[near(t) for t in terms])


class Place:
    def __init__(self, slabs, size_x):
        sections, coils, cuts = (lax.axis_size(a) for a in ("section", "coil", "cuts"))
        self.slabs, self.cuts, self.halves = slabs, cuts, sections // slabs
        self.owned = size_x // coils
        self.by_half = math.gcd(self.owned, self.halves)
        self.by_cut = math.gcd(self.owned // self.by_half, cuts)
        self.per = self.owned // (self.by_half * self.by_cut)
        self.run = self.by_cut * self.per

    def slab(self):
        return lax.axis_index("section") // self.halves

    def half_block(self):
        return lax.axis_index("section") % self.halves * self.by_half // self.halves

    def cut_block(self, cut):
        return cut * self.by_cut // self.cuts


def sent(pieces, axis):
    arrived = [pieces[0]]
    for k, (route, _, _) in enumerate(peers(axis)):
        arrived.append(lax.ppermute(pieces[k + 1], axis, route))
    return arrived


def body(initial, sens, kspace, mask, step_sizes, conv_in, bias_in, conv_out):
    slabs, _, size_x, size_y, _, size_z = sens.shape
    sections, cuts = lax.axis_size("section"), lax.axis_size("cuts")
    place = Place(slabs, size_x)
    rows = size_y // cuts

    def joined(array):
        return array.reshape(array.shape[:-3] + (array.shape[-3] * 2, size_z))

    initial, sens, kspace = joined(initial), joined(sens), joined(kspace)
    sens_pieces, image_pieces, packed = split(place, sens, initial, conv_in[0], bias_in, conv_out[0], step_sizes)
    senses = sent(sens_pieces, "coil")
    weights = sent([packed] * sections, "section")
    image_pieces = sent(image_pieces, "cuts")
    terms = adjoint(place, kspace, sens, mask)
    terms = sent(terms, "cuts")
    sums = pair_sum(terms)
    datas = sent(sums, "coil")
    given = for_partners(place, senses)
    more = sent([None] + list(given), "cuts")[1:]
    first, planes = first_refine(image_pieces, weights)
    coil_planes, normal = first_normal(place, planes, mask, senses, more)
    out = run_cascades(place, planes, first, normal, coil_planes, mask, weights, datas, cuts)
    out = lax.all_to_all(out, ("section", "cuts"), 0, 0, tiled=True)
    out = out.reshape(slabs, place.halves, cuts, place.per, rows, 2, size_z)
    out = out[:, :: place.halves // place.by_half, :: cuts // place.by_cut]
    return out.reshape(1, slabs, place.owned, rows, 2, size_z)


def solution(mesh):
    return jax.shard_map(
        body,
        mesh=mesh,
        in_specs=(
            P(None, "coil", "cuts", None, None),
            P(None, ("coil", "cuts"), None, None, None, None),
            P(None, ("coil", "cuts"), None, None, None, None),
            P(),
            P("section"),
            P("section", None, None),
            P("section", None),
            P("section", None, None),
        ),
        out_specs=P("section", None, "coil", "cuts", None, None),
        check_vma=False,
    )
```

```python
import functools
import math

import jax
import jax.numpy as jnp
import ml_dtypes
import numpy as np
from jax import lax
from jax.experimental import pallas as pl
from jax.experimental.pallas import tpu as pltpu
from jax.sharding import PartitionSpec as P


INTERPRET = False
BF16, F32 = jnp.bfloat16, jnp.float32
ACT = F32
GROUP = 4
TILE = 8


def dft_table(length, sign):
    ramp = np.arange(length)
    angle = (ramp[:, None] * ramp[None, :] % length) * (2.0 * math.pi / length)
    cosine = np.cos(angle) / math.sqrt(length)
    sine = sign * np.sin(angle) / math.sqrt(length)
    return np.block([[cosine, -sine], [sine, cosine]]).astype(ml_dtypes.bfloat16)


def peers(axis):
    count = lax.axis_size(axis)
    me = lax.axis_index(axis)
    for k in range(1, count):
        if count & (count - 1) == 0:
            yield [(j, j ^ k) for j in range(count)], jnp.bitwise_xor(me, k), jnp.bitwise_xor(me, k)
        else:
            route = [(j, (j + k) % count) for j in range(count)]
            yield route, (me + k) % count, (me - k) % count


def own_and_peers(axis):
    me = lax.axis_index(axis)
    yield None, me, me
    yield from peers(axis)


def step_to(index, axis):
    count = lax.axis_size(axis)
    me = lax.axis_index(axis)
    if count & (count - 1) == 0:
        return jnp.bitwise_xor(me, index)
    return (me - index) % count


SMEM = pl.BlockSpec(memory_space=pltpu.SMEM)
VMEM = pl.BlockSpec(memory_space=pltpu.VMEM)
ANY = pl.BlockSpec(memory_space=pl.ANY)


def far():
    return INTERPRET or lax.axis_size("coil") > 8


def near(x):
    return x if far() else pltpu.with_memory_space_constraint(x, pltpu.VMEM)


def away(x):
    return x if INTERPRET else pltpu.with_memory_space_constraint(x, pltpu.HBM)


def near_out(shape, dtype):
    return jax.ShapeDtypeStruct(shape, dtype) if far() else pltpu.VMEM(shape, dtype)


def kernel_params():
    return None if far() else pltpu.CompilerParams(vmem_limit_bytes=20 << 20)


def selections():
    chosen = np.zeros((4 * 4 * TILE + TILE, 42), np.float32)
    for dy in range(3):
        for dz in range(3):
            for part in range(2):
                tap = (3 * dy + dz) * 2 + part
                for row in range(2):
                    chosen[row * 32 + (row + dy) * TILE + dz * 2 + part, tap] = 0.5
                    chosen[64 + row * 32 + (row + 2 - dy) * TILE + dz * 2 + part, 21 + tap] = 1.0
    for row in range(2):
        for piece, at in enumerate((TILE + 6, TILE + 7, 2 * TILE + 6)):
            chosen[row * 32 + at, 18 + piece] = 0.5
    for piece in range(3):
        chosen[128 + piece, 39 + piece] = 1.0
    return chosen.astype(ml_dtypes.bfloat16)


def in_three(x):
    high = x.astype(BF16)
    rest = x - high.astype(F32)
    mid = rest.astype(BF16)
    return [high, mid, (rest - mid.astype(F32)).astype(BF16)]


def pack_into(packed, chosen, conv_in, bias, conv_out, step):
    def picked(rows, lanes):
        return jnp.dot(chosen[:, lanes], rows, preferred_element_type=F32)

    total = picked(conv_in[...], slice(0, 18)) + picked(conv_out[...], slice(21, 39))
    steps = jnp.full(bias.shape, step[0], F32)
    for at, split in ((18, in_three(bias[...])), (39, in_three(steps))):
        for piece, row in enumerate(split):
            column = chosen[:, at + piece : at + piece + 1].astype(F32)
            total += column * row.astype(F32)
    packed[...] = total.astype(BF16)


def shifted(plane, by, width):
    lane = lax.broadcasted_iota(jnp.int32, (plane.shape[0], width), 1)
    parts = []
    for at in range(0, plane.shape[1], width):
        moved = pltpu.roll(plane[:, at : at + width], (-by) % width, 1)
        parts.append(jnp.where((lane + by >= 0) & (lane + by < width), moved, 0.0))
    return jnp.concatenate(parts, axis=1)


def refine_into(planes, weights, scratch, result, width):
    rows, lanes = planes[0].shape
    taps_f32, taps, products, halves, hidden = scratch
    for dz in range(3):
        for part in range(2):
            plane = planes[part] if dz == 1 else shifted(planes[part], dz - 1, width)
            for s in range(lanes // width):
                place = pl.ds(TILE + dz * 2 + part, rows, stride=TILE)
                taps_f32.at[s][place, :] = plane[:, s * width : (s + 1) * width]
    for s in range(lanes // width):
        taps[:, s * width : (s + 1) * width] = taps_f32[s].astype(BF16)
    packed = weights.astype(F32)
    first = jnp.concatenate([packed[0:32].T, packed[32:64].T], axis=0).astype(BF16)
    second = jnp.concatenate([weights[64:96], weights[96:128]], axis=1)

    def start_of(j, g):
        start = (j * GROUP + g) * 2 * TILE
        return start if isinstance(start, int) else pl.multiple_of(start, 2 * TILE)

    def before(j, slot, g):
        window = taps[pl.ds(start_of(j, g), 4 * TILE), :]
        halves[slot, g] = jnp.dot(first, window, preferred_element_type=F32).astype(halves.dtype)

    def activate(slot, g):
        half = halves[slot, g]
        hidden[slot, g] = (half + half * jnp.tanh(half)).astype(BF16)

    def after(j, slot, g, carry):
        out = jnp.dot(second, hidden[slot, g], preferred_element_type=F32)
        done = out[: 2 * TILE] + carry
        for s in range(lanes // width):
            products.at[s][pl.ds(start_of(j, g), 2 * TILE), :] = done[:, s * width : (s + 1) * width]
        return out[2 * TILE :]

    blocks = rows // (2 * GROUP)
    for g in range(GROUP):
        before(0, 0, g)
    for g in range(GROUP):
        activate(0, g)
        before(1, 1, g)

    carry = jnp.zeros((2 * TILE, lanes), F32)
    for j in range(1, blocks + 1):
        for g in range(GROUP):
            carry = after(j - 1, (j - 1) % 2, g, carry)
            if j < blocks:
                activate(j % 2, g)
            if j + 1 < blocks:
                before(j + 1, (j + 1) % 2, g)
    last = carry
    for s in range(lanes // width):
        own = slice(s * width, (s + 1) * width)
        products.at[s][rows * TILE : (rows + 2) * TILE, :] = last[:, own]
        for part in range(2):
            total = products.at[s][pl.ds(TILE + 2 + part, rows, stride=TILE), :]
            for dz in (0, 2):
                total += shifted(products.at[s][pl.ds(TILE + dz * 2 + part, rows, stride=TILE), :], dz - 1, width)
            result[part, :, own] = total


def fill_ones(taps_f32):
    taps_f32[...] = jnp.zeros(taps_f32.shape, F32)
    slices, rows, width = taps_f32.shape
    for s in range(slices):
        for at in (6, 7):
            taps_f32.at[s][pl.ds(at, rows // TILE, stride=TILE), :] = jnp.ones((rows // TILE, width), F32)


def first_refine_kernel(n_rows, n_weights, *refs):
    pieces, weights = refs[:n_rows], refs[n_rows : n_rows + n_weights]
    refined, planes, stage = refs[n_rows + n_weights : n_rows + n_weights + 3]
    scratch = refs[n_rows + n_weights + 3 :]
    last, (per, _, block, width) = pieces[0].shape[0] - 1, pieces[0].shape[1:]
    fill_ones(scratch[0])
    for k, (_, _, source) in enumerate(own_and_peers("cuts")):
        for s in range(per):
            rows = pl.ds(pl.multiple_of(source * block, 16), block)
            stage.at[s][rows, :] = pieces[k][last, s, 0].astype(F32)
    height = stage.shape[1] // 2
    for s in range(per):
        for part in range(2):
            planes[part, :, s * width : (s + 1) * width] = stage.at[s][pl.ds(part, height, stride=2), :]
    refine_into([planes[0], planes[1]], of_cascade(weights, 0), scratch, refined, width)


def of_cascade(weights, cascade):
    at = step_to(cascade, "section")
    chosen = weights[0][...]
    for k in range(1, len(weights)):
        chosen = jnp.where(at == k, weights[k][...], chosen)
    return chosen


def subtract_normal(planes, coil_planes, weight_mask, tables, gradient, rows_y, rows_z):
    forward_z, back_z, forward_y, back_y = tables
    count, _, height, width = coil_planes.shape
    per = planes.shape[2] // width
    assert per <= 2
    pairs = count // 2

    def each_pair(step):
        if pairs <= 8:
            for m in range(pairs):
                step(m)
        else:
            lax.fori_loop(0, pairs, lambda m, _: step(m), None)

    def sens_and_lanes(m, i):
        n, s = 2 * m + i, i % per
        sens = coil_planes[n, 0].astype(F32), coil_planes[n, 1].astype(F32)
        return *sens, slice(s * width, (s + 1) * width)

    def product(m):
        coils = []
        for i in range(2):
            sr, si, lanes = sens_and_lanes(m, i)
            ir, ii = planes[0, :, lanes], planes[1, :, lanes]
            coils.append(jnp.concatenate([sr * ir - si * ii, sr * ii + si * ir], axis=1).astype(BF16))
        w = jnp.dot(jnp.concatenate(coils, axis=0), forward_z[...], preferred_element_type=F32)
        w = w.astype(BF16)
        for i in range(2):
            for part in range(2):
                block = w[i * height : (i + 1) * height, part * width : (part + 1) * width]
                rows_y[m, part * height : (part + 1) * height, i * width : (i + 1) * width] = block

    def forward(m):
        w = jnp.dot(forward_y[...], rows_y[m], preferred_element_type=F32)
        for i in range(2):
            lanes = slice(i * width, (i + 1) * width)
            rows_y[m, :, lanes] = (w[:, lanes] * weight_mask).astype(BF16)

    def back(m):
        w = jnp.dot(back_y[...], rows_y[m], preferred_element_type=F32).astype(BF16)
        for i in range(2):
            for part in range(2):
                block = w[part * height : (part + 1) * height, i * width : (i + 1) * width]
                rows_z[m, i * height : (i + 1) * height, part * width : (part + 1) * width] = block

    def gather(m):
        w = jnp.dot(rows_z[m], back_z[...], preferred_element_type=F32)
        for i in range(2):
            sr, si, lanes = sens_and_lanes(m, i)
            br = w[i * height : (i + 1) * height, :width]
            bi = w[i * height : (i + 1) * height, width:]
            gradient[0, :, lanes] -= sr * br + si * bi
            gradient[1, :, lanes] -= sr * bi - si * br

    for stage in (product, forward, back, gather):
        each_pair(stage)


def mask_of(place, mask):
    weight_mask = mask[place.slab()].astype(F32)
    return jnp.concatenate([weight_mask] * 2, axis=0)


def first_normal_kernel(place, n_sens, planes, mask, *refs):
    tables, senses, more = refs[:4], refs[4 : 4 + n_sens], refs[4 + n_sens : -5]
    coil_planes, normal, rows_y, rows_z, stage = refs[-5:]
    height = coil_planes.shape[2]

    def keep(n, rows):
        slot = stage.at[n % stage.shape[0]]
        slot[...] = rows.astype(F32)
        for part in range(2):
            coil_planes[n, part] = slot[pl.ds(part, height, stride=2), :].astype(BF16)

    start = place.cut_block(lax.axis_index("cuts")) * place.per
    n = 0
    for ref in senses:
        for s in range(place.per):
            keep(n, ref[start + s])
            n += 1
    for ref in more:
        for q in range(ref.shape[0]):
            for s in range(place.per):
                keep(n, ref[q, s])
                n += 1
    normal[...] = jnp.zeros(normal.shape, F32)
    subtract_normal(planes, coil_planes, mask_of(place, mask), tables, normal, rows_y, rows_z)


def cascades_kernel(place, n_weights, n_data, *refs):
    planes_in, first, normal, coil_planes, mask = refs[:5]
    tables, at = refs[5:9], 9
    weights, at = refs[at : at + n_weights], at + n_weights
    datas, at = refs[at : at + n_data], at + n_data
    out = refs[at]
    scratch = refs[at + 1 : -8]
    refined, planes, data, gradient, rows_y, rows_z, stage, all_weights = refs[-8:]
    per, _, height, width = datas[0].shape
    cascades = len(weights)
    cuts = out.shape[0] // cascades
    fill_ones(scratch[0])
    refined[...] = first[...]
    planes[...] = planes_in[...]
    for k in range(cascades):
        all_weights[k] = weights[k][...]
    for s in range(per):
        for part in range(2):
            data[part, :, s * width : (s + 1) * width] = sum(d[s, part].astype(F32) for d in datas)
    gradient[...] = data[...] + normal[...]
    weight_mask = mask_of(place, mask)

    def cascade(c, _):
        now = all_weights.at[step_to(c, "section")]
        step = sum(now[128 + piece : 129 + piece, 0:1].astype(F32) for piece in range(3))
        for part in range(2):
            new = (planes[part] - step * gradient[part] + refined[part]).astype(BF16).astype(F32)
            planes[part] = new
            for s in range(per):
                stage.at[s][pl.ds(part, height, stride=2), :] = new[:, s * width : (s + 1) * width]
        block = 2 * height // cuts
        for s in range(per):
            for cut in range(cuts):
                out[c * cuts + cut, s] = stage[s, cut * block : (cut + 1) * block].astype(BF16)

        @pl.when(c + 1 < cascades)
        def _():
            refine_into(
                [planes[0], planes[1]], all_weights[step_to(c + 1, "section")], scratch, refined, width
            )
            gradient[...] = data[...]
            subtract_normal(planes, coil_planes, weight_mask, tables, gradient, rows_y, rows_z)

    lax.fori_loop(0, cascades, cascade, None)


def refine_scratch(height, per, width, hid):
    rows, lanes = (height + 2) * TILE, per * width
    assert height % (4 * GROUP) == 0
    return [
        pltpu.VMEM((per, rows, width), F32),
        pltpu.VMEM((rows, lanes), BF16),
        pltpu.VMEM((per, rows, width), F32),
        pltpu.VMEM((2, GROUP, 2 * hid, lanes), ACT),
        pltpu.VMEM((2, GROUP, 2 * hid, lanes), BF16),
    ]


def first_refine(pieces, weights):
    per, _, block, width = pieces[0].shape[1:]
    rows = block * len(pieces)
    plane = near_out((2, rows // 2, per * width), F32)
    return pl.pallas_call(
        functools.partial(first_refine_kernel, len(pieces), len(weights)),
        out_shape=(plane, plane),
        in_specs=[VMEM] * (len(pieces) + len(weights)),
        out_specs=(VMEM, VMEM),
        scratch_shapes=[pltpu.VMEM((per, rows, width), F32)]
        + refine_scratch(rows // 2, per, width, weights[0].shape[-1]),
        compiler_params=kernel_params(),
        interpret=INTERPRET,
    )(*[near(x) for x in [*pieces, *weights]])


def pass_tables(height, width):
    tables = [
        dft_table(width, 1.0),
        dft_table(width, -1.0),
        dft_table(height, 1.0).T.copy(),
        dft_table(height, -1.0).T.copy(),
    ]
    return [near(jnp.asarray(t)) for t in tables]


def pass_scratch(count, height, width):
    return [
        pltpu.VMEM((count // 2, 2 * height, 2 * width), BF16),
        pltpu.VMEM((count // 2, 2 * height, 2 * width), BF16),
    ]


def first_normal(place, planes, mask, senses, more):
    _, height, lanes = planes.shape
    width = senses[0].shape[-1]
    count = place.per * (len(senses) + sum(m.shape[0] for m in more))
    args = [planes, mask] + pass_tables(height, width) + list(senses) + list(more)
    return pl.pallas_call(
        functools.partial(first_normal_kernel, place, len(senses)),
        out_shape=[near_out((count, 2, height, width), BF16), near_out((2, height, lanes), F32)],
        in_specs=[VMEM] * len(args),
        out_specs=[VMEM] * 2,
        scratch_shapes=pass_scratch(count, height, width) + [pltpu.VMEM((4, 2 * height, width), F32)],
        compiler_params=kernel_params(),
        interpret=INTERPRET,
    )(*[near(x) for x in args])


def run_cascades(place, planes, first, normal, coil_planes, mask, weights, datas, cuts):
    per, _, height, width = datas[0].shape
    lanes = per * width
    count = coil_planes.shape[0]
    args = [planes, first, normal, coil_planes, mask] + pass_tables(height, width)
    args += list(weights) + list(datas)
    return pl.pallas_call(
        functools.partial(cascades_kernel, place, len(weights), len(datas)),
        out_shape=jax.ShapeDtypeStruct((len(weights) * cuts, per, 2 * height // cuts, width), BF16),
        in_specs=[VMEM] * len(args),
        out_specs=VMEM,
        scratch_shapes=refine_scratch(height, per, width, weights[0].shape[-1])
        + [pltpu.VMEM((2, height, lanes), F32)] * 4
        + pass_scratch(count, height, width)
        + [
            pltpu.VMEM((per, 2 * height, width), F32),
            pltpu.VMEM((len(weights),) + weights[0].shape, BF16),
        ],
        compiler_params=kernel_params(),
        interpret=INTERPRET,
    )(*[near(x) for x in args])


def split_kernel(place, sens, *refs):
    outs, sems = refs[:-1], refs[-1]
    start = place.half_block() * place.run
    copies = []
    for k, (_, target, _) in enumerate(own_and_peers("coil")):
        source = sens.at[place.slab(), 0, pl.ds(target * place.owned + start, place.run)]
        copies.append(pltpu.make_async_copy(source, outs[k], sems.at[k]))
    for copy in copies:
        copy.start()
    for copy in copies:
        copy.wait()


def split(place, sens):
    coils = lax.axis_size("coil")
    return pl.pallas_call(
        functools.partial(split_kernel, place),
        out_shape=[near_out((place.run,) + sens.shape[-2:], BF16)] * coils,
        in_specs=[ANY],
        out_specs=[VMEM] * coils,
        scratch_shapes=[pltpu.SemaphoreType.DMA((coils,))],
        compiler_params=kernel_params(),
        interpret=INTERPRET,
    )(away(sens))


def partners_kernel(place, *refs):
    coils = lax.axis_size("coil")
    senses, outs = refs[:coils], refs[coils:]
    for k, (_, target, _) in enumerate(peers("cuts")):
        for q in range(coils):
            outs[k][q] = senses[q][pl.ds(place.cut_block(target) * place.per, place.per)]


def for_partners(place, senses):
    coils, cuts = lax.axis_size("coil"), lax.axis_size("cuts")
    outs = [near_out((coils, place.per) + senses[0].shape[-2:], BF16)] * (cuts - 1)
    return pl.pallas_call(
        functools.partial(partners_kernel, place),
        out_shape=outs,
        in_specs=[VMEM] * coils,
        out_specs=[VMEM] * len(outs),
        compiler_params=kernel_params(),
        interpret=INTERPRET,
    )(*[near(x) for x in senses])


CHUNKS = 4


def adjoint_kernel(place, n_small, kspace, sens, initial, mask, tables_x, back_y, back_z, *refs):
    coils, cuts = lax.axis_size("coil"), lax.axis_size("cuts")
    small, step, refs = refs[:n_small], refs[n_small], refs[n_small + 1 :]
    outs, packed, refs = refs[:cuts], refs[cuts], refs[cuts + 1 :]
    held, refs = refs[:n_small], refs[n_small:]
    data, own_sens, table_x, planes, rows_z, stage, sems = refs
    size_x, rows, width = data.shape
    height = rows // 2
    kept = coils * place.run
    slab, block = place.slab(), place.half_block()
    chunk = size_x // CHUNKS
    first_small = 1 + CHUNKS + coils + cuts * place.per
    packing = [
        pltpu.make_async_copy(source, target, sems.at[first_small + k])
        for k, (source, target) in enumerate(zip(small, held))
    ]
    copies = [pltpu.make_async_copy(tables_x.at[block], table_x, sems.at[0])]
    for i in range(CHUNKS):
        at = pl.ds(i * chunk, chunk)
        copies.append(pltpu.make_async_copy(kspace.at[slab, 0, at], data.at[at], sems.at[1 + i]))
    first_sens = len(copies)
    for q in range(coils):
        source = sens.at[slab, 0, pl.ds(q * place.owned + block * place.run, place.run)]
        target = own_sens.at[pl.ds(q * place.run, place.run)]
        copies.append(pltpu.make_async_copy(source, target, sems.at[first_sens + q]))
    for k, (_, target, _) in enumerate(own_and_peers("cuts")):
        for s in range(place.per):
            n = block * place.run + place.cut_block(target) * place.per + s
            sem = sems.at[first_sens + coils + k * place.per + s]
            copies.append(pltpu.make_async_copy(initial.at[slab, n], outs[k].at[coils, s, 0], sem))
    for copy in packing + copies:
        copy.start()
    for copy in packing:
        copy.wait()
    pack_into(packed, *held, step)
    for copy in copies[:first_sens]:
        copy.wait()
    weight_mask = mask[slab].astype(F32)
    groups = rows // (2 * TILE)
    for g in range(0, groups, 2):
        both = [
            data[:, (g + i) * 2 * TILE : (g + i + 1) * 2 * TILE, :].reshape(size_x * 2 * TILE, width)
            for i in range(2)
        ]
        w = jnp.dot(table_x[...], jnp.concatenate(both, axis=1), preferred_element_type=F32)
        for i in range(2):
            at = slice((g + i) * TILE, (g + i + 1) * TILE)
            part = w[:, i * width : (i + 1) * width].reshape(2 * kept, TILE, width)
            planes[:, at, :] = part * weight_mask[at][None]
    for n in range(0, kept, 2):
        pair = [
            jnp.concatenate([planes[2 * (n + i)], planes[2 * (n + i) + 1]], axis=0).astype(BF16)
            for i in range(2)
        ]
        w = jnp.dot(back_y[...], jnp.concatenate(pair, axis=1), preferred_element_type=F32).astype(BF16)
        for i in range(2):
            lanes = slice(i * width, (i + 1) * width)
            rows_z[n + i] = jnp.concatenate([w[:height, lanes], w[height:, lanes]], axis=1)
    for copy in copies[first_sens:]:
        copy.wait()
    for k, (_, target, _) in enumerate(own_and_peers("cuts")):
        outs[k][coils, :, 1] = jnp.zeros((place.per, height, width), BF16)
        for q in range(coils):
            for s in range(place.per):
                n = q * place.run + place.cut_block(target) * place.per + s
                w = jnp.dot(rows_z[n], back_z[...], preferred_element_type=F32)
                br, bi = w[:, :width], w[:, width:]
                slot = stage.at[(q * place.per + s) % stage.shape[0]]
                slot[...] = own_sens[n].astype(F32)
                sr, si = (slot[pl.ds(part, height, stride=2), :] for part in range(2))
                outs[k][q, s, 0] = (sr * br + si * bi).astype(BF16)
                outs[k][q, s, 1] = (sr * bi - si * br).astype(BF16)


def adjoint(place, kspace, sens, initial, mask, conv_in, bias, conv_out, step):
    coils, cuts = lax.axis_size("coil"), lax.axis_size("cuts")
    size_x, rows, width = kspace.shape[-3:]
    height = rows // 2
    kept = coils * place.run
    assert initial.shape[-2] == height
    chosen = jnp.asarray(selections())
    small = [chosen, conv_in.T, bias, conv_out]
    table = dft_table(size_x, -1.0).reshape(2, size_x, 2, coils, place.by_half, place.run)
    table = np.einsum("cxdqbr,uv->bqrduxvc", table.astype(np.float32), np.eye(TILE, dtype=np.float32))
    table = table.reshape(place.by_half, 2 * kept * TILE, 2 * size_x * TILE).astype(ml_dtypes.bfloat16)
    tables = [jnp.asarray(t) for t in (table, dft_table(height, -1.0).T.copy(), dft_table(width, -1.0))]
    return pl.pallas_call(
        functools.partial(adjoint_kernel, place, len(small)),
        out_shape=[near_out((coils + 1, place.per, 2, height, width), BF16)] * cuts
        + [near_out((chosen.shape[0], bias.shape[1]), BF16)],
        in_specs=[ANY, ANY, ANY, VMEM, ANY, VMEM, VMEM] + [ANY] * len(small) + [SMEM],
        out_specs=[VMEM] * (cuts + 1),
        scratch_shapes=[pltpu.VMEM(x.shape, x.dtype) for x in small]
        + [
            pltpu.VMEM((size_x, rows, width), BF16),
            pltpu.VMEM((kept, rows, width), BF16),
            pltpu.VMEM(table.shape[1:], BF16),
            pltpu.VMEM((2 * kept, height, width), F32),
            pltpu.VMEM((kept, height, 2 * width), BF16),
            pltpu.VMEM((4, rows, width), F32),
            pltpu.SemaphoreType.DMA((1 + CHUNKS + coils + cuts * place.per + len(small),)),
        ],
        compiler_params=kernel_params(),
        interpret=INTERPRET,
    )(
        *[away(x) for x in (kspace, sens, initial)],
        near(mask),
        away(tables[0]),
        near(tables[1]),
        near(tables[2]),
        *[away(x) for x in small],
        step,
    )


def halve_kernel(n_in, bit, *refs):
    terms, (kept, given) = refs[:n_in], refs[n_in:]
    mine = lax.axis_index("coil") // (1 << bit) % 2
    for j in range(kept.shape[0]):
        for out, target in ((kept, 2 * j + mine), (given, 2 * j + 1 - mine)):
            out[j] = sum(t[target].astype(F32) for t in terms).astype(BF16)


def halve(terms, bit):
    count = terms[0].shape[0] // 2 * 2
    return pl.pallas_call(
        functools.partial(halve_kernel, len(terms), bit),
        out_shape=[near_out((count // 2,) + terms[0].shape[1:], BF16)] * 2,
        in_specs=[VMEM] * len(terms),
        out_specs=[VMEM] * 2,
        compiler_params=kernel_params(),
        interpret=INTERPRET,
    )(*[near(t) for t in terms])


def sum_over_coils(terms):
    coils = lax.axis_size("coil")
    assert coils & (coils - 1) == 0
    for bit in range(coils.bit_length() - 1):
        kept, given = halve(terms, bit)
        route = [(j, j ^ (1 << bit)) for j in range(coils)]
        terms = [kept, lax.ppermute(given, "coil", route)]
    return [t[0] for t in terms]


class Place:
    def __init__(self, slabs, size_x):
        sections, coils, cuts = (lax.axis_size(a) for a in ("section", "coil", "cuts"))
        self.slabs, self.cuts, self.halves = slabs, cuts, sections // slabs
        self.owned = size_x // coils
        self.by_half = math.gcd(self.owned, self.halves)
        self.by_cut = math.gcd(self.owned // self.by_half, cuts)
        self.per = self.owned // (self.by_half * self.by_cut)
        self.run = self.by_cut * self.per

    def slab(self):
        return lax.axis_index("section") // self.halves

    def half_block(self):
        return lax.axis_index("section") % self.halves * self.by_half // self.halves

    def cut_block(self, cut):
        return cut * self.by_cut // self.cuts


def sent(pieces, axis):
    arrived = [pieces[0]]
    for k, (route, _, _) in enumerate(peers(axis)):
        arrived.append(lax.ppermute(pieces[k + 1], axis, route))
    return arrived


def body(initial, sens, kspace, mask, step_sizes, conv_in, bias_in, conv_out):
    slabs, _, size_x, size_y, _, size_z = sens.shape
    sections, cuts = lax.axis_size("section"), lax.axis_size("cuts")
    place = Place(slabs, size_x)
    rows = size_y // cuts

    def joined(array):
        return array.reshape(array.shape[:-3] + (array.shape[-3] * 2, size_z))

    initial, sens, kspace = joined(initial), joined(sens), joined(kspace)
    sens_pieces = split(place, sens)
    senses = sent(sens_pieces, "coil")
    *terms, packed = adjoint(
        place, kspace, sens, initial, mask, conv_in[0], bias_in, conv_out[0], step_sizes
    )
    weights = sent([packed] * sections, "section")
    terms = sent(terms, "cuts")
    datas = sum_over_coils(terms)
    given = for_partners(place, senses)
    more = sent([None] + list(given), "cuts")[1:]
    first, planes = first_refine(terms, weights)
    coil_planes, normal = first_normal(place, planes, mask, senses, more)
    out = run_cascades(place, planes, first, normal, coil_planes, mask, weights, datas, cuts)
    out = lax.all_to_all(out, ("section", "cuts"), 0, 0, tiled=True)
    out = out.reshape(slabs, place.halves, cuts, place.per, rows, 2, size_z)
    out = out[:, :: place.halves // place.by_half, :: cuts // place.by_cut]
    return out.reshape(1, slabs, place.owned, rows, 2, size_z)


def solution(mesh):
    return jax.shard_map(
        body,
        mesh=mesh,
        in_specs=(
            P(None, "coil", "cuts", None, None),
            P(None, ("coil", "cuts"), None, None, None, None),
            P(None, ("coil", "cuts"), None, None, None, None),
            P(),
            P("section"),
            P("section", None, None),
            P("section", None),
            P("section", None, None),
        ),
        out_specs=P("section", None, "coil", "cuts", None, None),
        check_vma=False,
    )
```

```python
import functools
import math

import jax
import jax.numpy as jnp
import ml_dtypes
import numpy as np
from jax import lax
from jax.experimental import pallas as pl
from jax.experimental.pallas import tpu as pltpu
from jax.sharding import PartitionSpec as P


INTERPRET = False
BF16, F32 = jnp.bfloat16, jnp.float32
ACT = F32
GROUP = 4
TILE = 8


def dft_table(length, sign):
    ramp = np.arange(length)
    angle = (ramp[:, None] * ramp[None, :] % length) * (2.0 * math.pi / length)
    cosine = np.cos(angle) / math.sqrt(length)
    sine = sign * np.sin(angle) / math.sqrt(length)
    return np.block([[cosine, -sine], [sine, cosine]]).astype(ml_dtypes.bfloat16)


def peers(axis):
    count = lax.axis_size(axis)
    me = lax.axis_index(axis)
    for k in range(1, count):
        if count & (count - 1) == 0:
            yield [(j, j ^ k) for j in range(count)], jnp.bitwise_xor(me, k), jnp.bitwise_xor(me, k)
        else:
            route = [(j, (j + k) % count) for j in range(count)]
            yield route, (me + k) % count, (me - k) % count


def own_and_peers(axis):
    me = lax.axis_index(axis)
    yield None, me, me
    yield from peers(axis)


def step_to(index, axis):
    count = lax.axis_size(axis)
    me = lax.axis_index(axis)
    if count & (count - 1) == 0:
        return jnp.bitwise_xor(me, index)
    return (me - index) % count


SMEM = pl.BlockSpec(memory_space=pltpu.SMEM)
VMEM = pl.BlockSpec(memory_space=pltpu.VMEM)
ANY = pl.BlockSpec(memory_space=pl.ANY)


def far():
    return INTERPRET or lax.axis_size("coil") > 8


def near(x):
    return x if far() else pltpu.with_memory_space_constraint(x, pltpu.VMEM)


def away(x):
    return x if INTERPRET else pltpu.with_memory_space_constraint(x, pltpu.HBM)


def near_out(shape, dtype):
    return jax.ShapeDtypeStruct(shape, dtype) if far() else pltpu.VMEM(shape, dtype)


def kernel_params():
    return None if far() else pltpu.CompilerParams(vmem_limit_bytes=20 << 20)


def selections():
    chosen = np.zeros((4 * 4 * TILE + TILE, 42), np.float32)
    for dy in range(3):
        for dz in range(3):
            for part in range(2):
                tap = (3 * dy + dz) * 2 + part
                for row in range(2):
                    chosen[row * 32 + (row + dy) * TILE + dz * 2 + part, tap] = 0.5
                    chosen[64 + row * 32 + (row + 2 - dy) * TILE + dz * 2 + part, 21 + tap] = 1.0
    for row in range(2):
        for piece, at in enumerate((TILE + 6, TILE + 7, 2 * TILE + 6)):
            chosen[row * 32 + at, 18 + piece] = 0.5
    for piece in range(3):
        chosen[128 + piece, 39 + piece] = 1.0
    return chosen.astype(ml_dtypes.bfloat16)


def in_three(x):
    high = x.astype(BF16)
    rest = x - high.astype(F32)
    mid = rest.astype(BF16)
    return [high, mid, (rest - mid.astype(F32)).astype(BF16)]


def pack_into(packed, chosen, conv_in, bias, conv_out, step):
    def picked(rows, lanes):
        return jnp.dot(chosen[:, lanes], rows, preferred_element_type=F32)

    total = picked(conv_in[...], slice(0, 18)) + picked(conv_out[...], slice(21, 39))
    steps = jnp.full(bias.shape, step[0], F32)
    for at, split in ((18, in_three(bias[...])), (39, in_three(steps))):
        for piece, row in enumerate(split):
            column = chosen[:, at + piece : at + piece + 1].astype(F32)
            total += column * row.astype(F32)
    packed[...] = total.astype(BF16)


def shifted(plane, by, width):
    lane = lax.broadcasted_iota(jnp.int32, (plane.shape[0], width), 1)
    parts = []
    for at in range(0, plane.shape[1], width):
        moved = pltpu.roll(plane[:, at : at + width], (-by) % width, 1)
        parts.append(jnp.where((lane + by >= 0) & (lane + by < width), moved, 0.0))
    return jnp.concatenate(parts, axis=1)


def refine_into(planes, weights, scratch, result, width):
    rows, lanes = planes[0].shape
    taps_f32, taps, products, halves, hidden = scratch
    for dz in range(3):
        for part in range(2):
            plane = planes[part] if dz == 1 else shifted(planes[part], dz - 1, width)
            for s in range(lanes // width):
                place = pl.ds(TILE + dz * 2 + part, rows, stride=TILE)
                taps_f32.at[s][place, :] = plane[:, s * width : (s + 1) * width]
    for s in range(lanes // width):
        taps[:, s * width : (s + 1) * width] = taps_f32[s].astype(BF16)
    packed = weights.astype(F32)
    first = jnp.concatenate([packed[0:32].T, packed[32:64].T], axis=0).astype(BF16)
    second = jnp.concatenate([weights[64:96], weights[96:128]], axis=1)

    def start_of(j, g):
        start = (j * GROUP + g) * 2 * TILE
        return start if isinstance(start, int) else pl.multiple_of(start, 2 * TILE)

    def before(j, slot, g):
        window = taps[pl.ds(start_of(j, g), 4 * TILE), :]
        halves[slot, g] = jnp.dot(first, window, preferred_element_type=F32).astype(halves.dtype)

    def activate(slot, g):
        half = halves[slot, g]
        hidden[slot, g] = (half + half * jnp.tanh(half)).astype(BF16)

    def after(j, slot, g, carry):
        out = jnp.dot(second, hidden[slot, g], preferred_element_type=F32)
        done = out[: 2 * TILE] + carry
        for s in range(lanes // width):
            products.at[s][pl.ds(start_of(j, g), 2 * TILE), :] = done[:, s * width : (s + 1) * width]
        return out[2 * TILE :]

    blocks = rows // (2 * GROUP)
    for g in range(GROUP):
        before(0, 0, g)
    for g in range(GROUP):
        activate(0, g)
        before(1, 1, g)

    carry = jnp.zeros((2 * TILE, lanes), F32)
    for j in range(1, blocks + 1):
        for g in range(GROUP):
            carry = after(j - 1, (j - 1) % 2, g, carry)
            if j < blocks:
                activate(j % 2, g)
            if j + 1 < blocks:
                before(j + 1, (j + 1) % 2, g)
    last = carry
    for s in range(lanes // width):
        own = slice(s * width, (s + 1) * width)
        products.at[s][rows * TILE : (rows + 2) * TILE, :] = last[:, own]
        for part in range(2):
            total = products.at[s][pl.ds(TILE + 2 + part, rows, stride=TILE), :]
            for dz in (0, 2):
                total += shifted(products.at[s][pl.ds(TILE + dz * 2 + part, rows, stride=TILE), :], dz - 1, width)
            result[part, :, own] = total


def fill_ones(taps_f32):
    taps_f32[...] = jnp.zeros(taps_f32.shape, F32)
    slices, rows, width = taps_f32.shape
    for s in range(slices):
        for at in (6, 7):
            taps_f32.at[s][pl.ds(at, rows // TILE, stride=TILE), :] = jnp.ones((rows // TILE, width), F32)


def first_refine_kernel(n_rows, n_weights, *refs):
    pieces, weights = refs[:n_rows], refs[n_rows : n_rows + n_weights]
    refined, planes, stage = refs[n_rows + n_weights : n_rows + n_weights + 3]
    scratch = refs[n_rows + n_weights + 3 :]
    last, (per, _, block, width) = pieces[0].shape[0] - 1, pieces[0].shape[1:]
    fill_ones(scratch[0])
    for k, (_, _, source) in enumerate(own_and_peers("cuts")):
        for s in range(per):
            rows = pl.ds(pl.multiple_of(source * block, 16), block)
            stage.at[s][rows, :] = pieces[k][last, s, 0].astype(F32)
    height = stage.shape[1] // 2
    for s in range(per):
        for part in range(2):
            planes[part, :, s * width : (s + 1) * width] = stage.at[s][pl.ds(part, height, stride=2), :]
    refine_into([planes[0], planes[1]], of_cascade(weights, 0), scratch, refined, width)


def of_cascade(weights, cascade):
    at = step_to(cascade, "section")
    chosen = weights[0][...]
    for k in range(1, len(weights)):
        chosen = jnp.where(at == k, weights[k][...], chosen)
    return chosen


def subtract_normal(planes, coil_planes, weight_mask, tables, gradient, rows_y, rows_z):
    forward_z, back_z, forward_y, back_y = tables
    count, _, height, width = coil_planes.shape
    per = planes.shape[2] // width
    assert per <= 2
    pairs = count // 2

    def each_pair(step):
        lax.fori_loop(0, pairs, lambda m, _: step(m), None)

    def sens_and_lanes(m, i):
        n, s = 2 * m + i, i % per
        sens = coil_planes[n, 0].astype(F32), coil_planes[n, 1].astype(F32)
        return *sens, slice(s * width, (s + 1) * width)

    def product(m):
        coils = []
        for i in range(2):
            sr, si, lanes = sens_and_lanes(m, i)
            ir, ii = planes[0, :, lanes], planes[1, :, lanes]
            coils.append(jnp.concatenate([sr * ir - si * ii, sr * ii + si * ir], axis=1).astype(BF16))
        w = jnp.dot(jnp.concatenate(coils, axis=0), forward_z[...], preferred_element_type=F32)
        w = w.astype(BF16)
        for i in range(2):
            for part in range(2):
                block = w[i * height : (i + 1) * height, part * width : (part + 1) * width]
                rows_y[m, part * height : (part + 1) * height, i * width : (i + 1) * width] = block

    def forward(m):
        w = jnp.dot(forward_y[...], rows_y[m], preferred_element_type=F32)
        for i in range(2):
            lanes = slice(i * width, (i + 1) * width)
            rows_y[m, :, lanes] = (w[:, lanes] * weight_mask).astype(BF16)

    def back(m):
        w = jnp.dot(back_y[...], rows_y[m], preferred_element_type=F32).astype(BF16)
        for i in range(2):
            for part in range(2):
                block = w[part * height : (part + 1) * height, i * width : (i + 1) * width]
                rows_z[m, i * height : (i + 1) * height, part * width : (part + 1) * width] = block

    def gather(m):
        w = jnp.dot(rows_z[m], back_z[...], preferred_element_type=F32)
        for i in range(2):
            sr, si, lanes = sens_and_lanes(m, i)
            br = w[i * height : (i + 1) * height, :width]
            bi = w[i * height : (i + 1) * height, width:]
            gradient[0, :, lanes] -= sr * br + si * bi
            gradient[1, :, lanes] -= sr * bi - si * br

    if pairs > 8:
        return [functools.partial(each_pair, stage) for stage in (product, forward, back, gather)]
    return [functools.partial(stage, m) for stage in (product, forward, back, gather) for m in range(pairs)]


def mask_of(place, mask):
    weight_mask = mask[place.slab()].astype(F32)
    return jnp.concatenate([weight_mask] * 2, axis=0)


def first_normal_kernel(place, n_sens, planes, mask, *refs):
    tables, senses, more = refs[:4], refs[4 : 4 + n_sens], refs[4 + n_sens : -5]
    coil_planes, normal, rows_y, rows_z, stage = refs[-5:]
    height = coil_planes.shape[2]

    def keep(n, rows):
        slot = stage.at[n % stage.shape[0]]
        slot[...] = rows.astype(F32)
        for part in range(2):
            coil_planes[n, part] = slot[pl.ds(part, height, stride=2), :].astype(BF16)

    start = place.cut_block(lax.axis_index("cuts")) * place.per
    n = 0
    for ref in senses:
        for s in range(place.per):
            keep(n, ref[start + s])
            n += 1
    for ref in more:
        for q in range(ref.shape[0]):
            for s in range(place.per):
                keep(n, ref[q, s])
                n += 1
    normal[...] = jnp.zeros(normal.shape, F32)
    for step in subtract_normal(planes, coil_planes, mask_of(place, mask), tables, normal, rows_y, rows_z):
        step()


def cascades_kernel(place, n_weights, n_data, *refs):
    planes_in, first, normal, coil_planes, mask = refs[:5]
    tables, at = refs[5:9], 9
    weights, at = refs[at : at + n_weights], at + n_weights
    datas, at = refs[at : at + n_data], at + n_data
    cuts = lax.axis_size("cuts")
    outs = refs[at : at + cuts]
    scratch = refs[at + cuts : -8]
    refined, planes, data, gradient, rows_y, rows_z, stage, all_weights = refs[-8:]
    per, _, height, width = datas[0].shape
    cascades = len(weights)
    fill_ones(scratch[0])
    refined[...] = first[...]
    planes[...] = planes_in[...]
    for k in range(cascades):
        all_weights[k] = weights[k][...]
    for s in range(per):
        for part in range(2):
            data[part, :, s * width : (s + 1) * width] = sum(d[s, part].astype(F32) for d in datas)
    gradient[...] = data[...] + normal[...]
    weight_mask = mask_of(place, mask)

    def cascade(c, _):
        now = all_weights.at[step_to(c, "section")]
        step = sum(now[128 + piece : 129 + piece, 0:1].astype(F32) for piece in range(3))
        for part in range(2):
            new = (planes[part] - step * gradient[part] + refined[part]).astype(BF16).astype(F32)
            planes[part] = new
            for s in range(per):
                stage.at[s][pl.ds(part, height, stride=2), :] = new[:, s * width : (s + 1) * width]
        block = 2 * height // cuts
        for k, (_, target, _) in enumerate(own_and_peers("cuts")):
            for s in range(per):
                rows = stage.at[s][pl.ds(pl.multiple_of(target * block, 16), block), :]
                outs[k][step_to(c, "section"), s] = rows.astype(BF16)

        @pl.when(c + 1 < cascades)
        def _():
            following = all_weights[step_to(c + 1, "section")]
            refine_into([planes[0], planes[1]], following, scratch, refined, width)
            gradient[...] = data[...]
            for take in subtract_normal(
                planes, coil_planes, weight_mask, tables, gradient, rows_y, rows_z
            ):
                take()

    lax.fori_loop(0, cascades, cascade, None)


def refine_scratch(height, per, width, hid):
    rows, lanes = (height + 2) * TILE, per * width
    assert height % (4 * GROUP) == 0
    return [
        pltpu.VMEM((per, rows, width), F32),
        pltpu.VMEM((rows, lanes), BF16),
        pltpu.VMEM((per, rows, width), F32),
        pltpu.VMEM((2, GROUP, 2 * hid, lanes), ACT),
        pltpu.VMEM((2, GROUP, 2 * hid, lanes), BF16),
    ]


def first_refine(pieces, weights):
    per, _, block, width = pieces[0].shape[1:]
    rows = block * len(pieces)
    plane = near_out((2, rows // 2, per * width), F32)
    return pl.pallas_call(
        functools.partial(first_refine_kernel, len(pieces), len(weights)),
        out_shape=(plane, plane),
        in_specs=[VMEM] * (len(pieces) + len(weights)),
        out_specs=(VMEM, VMEM),
        scratch_shapes=[pltpu.VMEM((per, rows, width), F32)]
        + refine_scratch(rows // 2, per, width, weights[0].shape[-1]),
        compiler_params=kernel_params(),
        interpret=INTERPRET,
    )(*[near(x) for x in [*pieces, *weights]])


def pass_tables(height, width):
    tables = [
        dft_table(width, 1.0),
        dft_table(width, -1.0),
        dft_table(height, 1.0).T.copy(),
        dft_table(height, -1.0).T.copy(),
    ]
    return [near(jnp.asarray(t)) for t in tables]


def pass_scratch(count, height, width):
    return [
        pltpu.VMEM((count // 2, 2 * height, 2 * width), BF16),
        pltpu.VMEM((count // 2, 2 * height, 2 * width), BF16),
    ]


def first_normal(place, planes, mask, senses, more):
    _, height, lanes = planes.shape
    width = senses[0].shape[-1]
    count = place.per * (len(senses) + sum(m.shape[0] for m in more))
    args = [planes, mask] + pass_tables(height, width) + list(senses) + list(more)
    return pl.pallas_call(
        functools.partial(first_normal_kernel, place, len(senses)),
        out_shape=[near_out((count, 2, height, width), BF16), near_out((2, height, lanes), F32)],
        in_specs=[VMEM] * len(args),
        out_specs=[VMEM] * 2,
        scratch_shapes=pass_scratch(count, height, width) + [pltpu.VMEM((4, 2 * height, width), F32)],
        compiler_params=kernel_params(),
        interpret=INTERPRET,
    )(*[near(x) for x in args])


def run_cascades(place, planes, first, normal, coil_planes, mask, weights, datas, cuts):
    per, _, height, width = datas[0].shape
    lanes = per * width
    count = coil_planes.shape[0]
    args = [planes, first, normal, coil_planes, mask] + pass_tables(height, width)
    args += list(weights) + list(datas)
    return pl.pallas_call(
        functools.partial(cascades_kernel, place, len(weights), len(datas)),
        out_shape=[near_out((len(weights), per, 2 * height // cuts, width), BF16)] * cuts,
        in_specs=[VMEM] * len(args),
        out_specs=[VMEM] * cuts,
        scratch_shapes=refine_scratch(height, per, width, weights[0].shape[-1])
        + [pltpu.VMEM((2, height, lanes), F32)] * 4
        + pass_scratch(count, height, width)
        + [
            pltpu.VMEM((per, 2 * height, width), F32),
            pltpu.VMEM((len(weights),) + weights[0].shape, BF16),
        ],
        compiler_params=kernel_params(),
        interpret=INTERPRET,
    )(*[near(x) for x in args])


def split_kernel(place, sens, *refs):
    outs, sems = refs[:-1], refs[-1]
    start = place.half_block() * place.run
    copies = []
    for k, (_, target, _) in enumerate(own_and_peers("coil")):
        source = sens.at[place.slab(), 0, pl.ds(target * place.owned + start, place.run)]
        copies.append(pltpu.make_async_copy(source, outs[k], sems.at[k]))
    for copy in copies:
        copy.start()
    for copy in copies:
        copy.wait()


def split(place, sens):
    coils = lax.axis_size("coil")
    return pl.pallas_call(
        functools.partial(split_kernel, place),
        out_shape=[near_out((place.run,) + sens.shape[-2:], BF16)] * coils,
        in_specs=[ANY],
        out_specs=[VMEM] * coils,
        scratch_shapes=[pltpu.SemaphoreType.DMA((coils,))],
        compiler_params=kernel_params(),
        interpret=INTERPRET,
    )(away(sens))


def partners_kernel(place, *refs):
    coils = lax.axis_size("coil")
    senses, outs = refs[:coils], refs[coils:]
    for k, (_, target, _) in enumerate(peers("cuts")):
        for q in range(coils):
            outs[k][q] = senses[q][pl.ds(place.cut_block(target) * place.per, place.per)]


def for_partners(place, senses):
    coils, cuts = lax.axis_size("coil"), lax.axis_size("cuts")
    outs = [near_out((coils, place.per) + senses[0].shape[-2:], BF16)] * (cuts - 1)
    return pl.pallas_call(
        functools.partial(partners_kernel, place),
        out_shape=outs,
        in_specs=[VMEM] * coils,
        out_specs=[VMEM] * len(outs),
        compiler_params=kernel_params(),
        interpret=INTERPRET,
    )(*[near(x) for x in senses])


CHUNKS = 4


def adjoint_kernel(place, n_small, kspace, sens, initial, mask, tables_x, back_y, back_z, *refs):
    coils, cuts = lax.axis_size("coil"), lax.axis_size("cuts")
    small, step, refs = refs[:n_small], refs[n_small], refs[n_small + 1 :]
    outs, packed, refs = refs[:cuts], refs[cuts], refs[cuts + 1 :]
    held, refs = refs[:n_small], refs[n_small:]
    data, own_sens, table_x, planes, rows_z, stage, sems = refs
    size_x, rows, width = data.shape
    height = rows // 2
    kept = coils * place.run
    slab, block = place.slab(), place.half_block()
    chunk = size_x // CHUNKS
    first_small = 1 + CHUNKS + coils + cuts * place.per
    packing = [
        pltpu.make_async_copy(source, target, sems.at[first_small + k])
        for k, (source, target) in enumerate(zip(small, held))
    ]
    copies = [pltpu.make_async_copy(tables_x.at[block], table_x, sems.at[0])]
    for i in range(CHUNKS):
        at = pl.ds(i * chunk, chunk)
        copies.append(pltpu.make_async_copy(kspace.at[slab, 0, at], data.at[at], sems.at[1 + i]))
    first_sens = len(copies)
    for q in range(coils):
        source = sens.at[slab, 0, pl.ds(q * place.owned + block * place.run, place.run)]
        target = own_sens.at[pl.ds(q * place.run, place.run)]
        copies.append(pltpu.make_async_copy(source, target, sems.at[first_sens + q]))
    for k, (_, target, _) in enumerate(own_and_peers("cuts")):
        for s in range(place.per):
            n = block * place.run + place.cut_block(target) * place.per + s
            sem = sems.at[first_sens + coils + k * place.per + s]
            copies.append(pltpu.make_async_copy(initial.at[slab, n], outs[k].at[coils, s, 0], sem))
    for copy in packing + copies:
        copy.start()
    for copy in packing:
        copy.wait()
    pack_into(packed, *held, step)
    for copy in copies[:first_sens]:
        copy.wait()
    weight_mask = mask[slab].astype(F32)
    groups = rows // (2 * TILE)
    for g in range(0, groups, 2):
        both = [
            data[:, (g + i) * 2 * TILE : (g + i + 1) * 2 * TILE, :].reshape(size_x * 2 * TILE, width)
            for i in range(2)
        ]
        w = jnp.dot(table_x[...], jnp.concatenate(both, axis=1), preferred_element_type=F32)
        for i in range(2):
            at = slice((g + i) * TILE, (g + i + 1) * TILE)
            part = w[:, i * width : (i + 1) * width].reshape(2 * kept, TILE, width)
            planes[:, at, :] = part * weight_mask[at][None]
    for n in range(0, kept, 2):
        pair = [
            jnp.concatenate([planes[2 * (n + i)], planes[2 * (n + i) + 1]], axis=0).astype(BF16)
            for i in range(2)
        ]
        w = jnp.dot(back_y[...], jnp.concatenate(pair, axis=1), preferred_element_type=F32).astype(BF16)
        for i in range(2):
            lanes = slice(i * width, (i + 1) * width)
            rows_z[n + i] = jnp.concatenate([w[:height, lanes], w[height:, lanes]], axis=1)
    for copy in copies[first_sens:]:
        copy.wait()
    for k, (_, target, _) in enumerate(own_and_peers("cuts")):
        outs[k][coils, :, 1] = jnp.zeros((place.per, height, width), BF16)
        for q in range(coils):
            for s in range(place.per):
                n = q * place.run + place.cut_block(target) * place.per + s
                w = jnp.dot(rows_z[n], back_z[...], preferred_element_type=F32)
                br, bi = w[:, :width], w[:, width:]
                slot = stage.at[(q * place.per + s) % stage.shape[0]]
                slot[...] = own_sens[n].astype(F32)
                sr, si = (slot[pl.ds(part, height, stride=2), :] for part in range(2))
                outs[k][q, s, 0] = (sr * br + si * bi).astype(BF16)
                outs[k][q, s, 1] = (sr * bi - si * br).astype(BF16)


def adjoint(place, kspace, sens, initial, mask, conv_in, bias, conv_out, step):
    coils, cuts = lax.axis_size("coil"), lax.axis_size("cuts")
    size_x, rows, width = kspace.shape[-3:]
    height = rows // 2
    kept = coils * place.run
    assert initial.shape[-2] == height
    chosen = jnp.asarray(selections())
    small = [chosen, conv_in.T, bias, conv_out]
    table = dft_table(size_x, -1.0).reshape(2, size_x, 2, coils, place.by_half, place.run)
    table = np.einsum("cxdqbr,uv->bqrduxvc", table.astype(np.float32), np.eye(TILE, dtype=np.float32))
    table = table.reshape(place.by_half, 2 * kept * TILE, 2 * size_x * TILE).astype(ml_dtypes.bfloat16)
    tables = [jnp.asarray(t) for t in (table, dft_table(height, -1.0).T.copy(), dft_table(width, -1.0))]
    return pl.pallas_call(
        functools.partial(adjoint_kernel, place, len(small)),
        out_shape=[near_out((coils + 1, place.per, 2, height, width), BF16)] * cuts
        + [near_out((chosen.shape[0], bias.shape[1]), BF16)],
        in_specs=[ANY, ANY, ANY, VMEM, ANY, VMEM, VMEM] + [ANY] * len(small) + [SMEM],
        out_specs=[VMEM] * (cuts + 1),
        scratch_shapes=[pltpu.VMEM(x.shape, x.dtype) for x in small]
        + [
            pltpu.VMEM((size_x, rows, width), BF16),
            pltpu.VMEM((kept, rows, width), BF16),
            pltpu.VMEM(table.shape[1:], BF16),
            pltpu.VMEM((2 * kept, height, width), F32),
            pltpu.VMEM((kept, height, 2 * width), BF16),
            pltpu.VMEM((4, rows, width), F32),
            pltpu.SemaphoreType.DMA((1 + CHUNKS + coils + cuts * place.per + len(small),)),
        ],
        compiler_params=kernel_params(),
        interpret=INTERPRET,
    )(
        *[away(x) for x in (kspace, sens, initial)],
        near(mask),
        away(tables[0]),
        near(tables[1]),
        near(tables[2]),
        *[away(x) for x in small],
        step,
    )


def halve_kernel(n_in, bit, *refs):
    terms, (kept, given) = refs[:n_in], refs[n_in:]
    mine = lax.axis_index("coil") // (1 << bit) % 2
    for j in range(kept.shape[0]):
        for out, target in ((kept, 2 * j + mine), (given, 2 * j + 1 - mine)):
            out[j] = sum(t[target].astype(F32) for t in terms).astype(BF16)


def halve(terms, bit):
    count = terms[0].shape[0] // 2 * 2
    return pl.pallas_call(
        functools.partial(halve_kernel, len(terms), bit),
        out_shape=[near_out((count // 2,) + terms[0].shape[1:], BF16)] * 2,
        in_specs=[VMEM] * len(terms),
        out_specs=[VMEM] * 2,
        compiler_params=kernel_params(),
        interpret=INTERPRET,
    )(*[near(t) for t in terms])


def sum_over_coils(terms):
    coils = lax.axis_size("coil")
    assert coils & (coils - 1) == 0
    for bit in range(coils.bit_length() - 1):
        kept, given = halve(terms, bit)
        route = [(j, j ^ (1 << bit)) for j in range(coils)]
        terms = [kept, lax.ppermute(given, "coil", route)]
    return [t[0] for t in terms]


def by_section_kernel(n_in, *refs):
    images, outs = refs[:n_in], refs[n_in:]
    for k, (_, _, source) in enumerate(own_and_peers("cuts")):
        for section, out in enumerate(outs):
            out[source] = images[k][section]


def by_section(images):
    sections = images[0].shape[0]
    return pl.pallas_call(
        functools.partial(by_section_kernel, len(images)),
        out_shape=[near_out((len(images),) + images[0].shape[1:], BF16)] * sections,
        in_specs=[VMEM] * len(images),
        out_specs=[VMEM] * sections,
        compiler_params=kernel_params(),
        interpret=INTERPRET,
    )(*[near(x) for x in images])


def arrange_kernel(place, *refs):
    pieces, out = refs[:-1], refs[-1]
    for k, (_, _, source) in enumerate(own_and_peers("section")):
        slab = source // place.halves
        start = source % place.halves * place.by_half // place.halves * place.run
        for cut in range(place.cuts):
            at = start + place.cut_block(cut) * place.per
            out[slab, pl.ds(at, place.per)] = pieces[k][cut]


def arrange(place, pieces):
    return pl.pallas_call(
        functools.partial(arrange_kernel, place),
        out_shape=jax.ShapeDtypeStruct((place.slabs, place.owned) + pieces[0].shape[2:], BF16),
        in_specs=[VMEM] * len(pieces),
        out_specs=VMEM,
        compiler_params=kernel_params(),
        interpret=INTERPRET,
    )(*[near(x) for x in pieces])


class Place:
    def __init__(self, slabs, size_x):
        sections, coils, cuts = (lax.axis_size(a) for a in ("section", "coil", "cuts"))
        self.slabs, self.cuts, self.halves = slabs, cuts, sections // slabs
        self.owned = size_x // coils
        self.by_half = math.gcd(self.owned, self.halves)
        self.by_cut = math.gcd(self.owned // self.by_half, cuts)
        self.per = self.owned // (self.by_half * self.by_cut)
        self.run = self.by_cut * self.per

    def slab(self):
        return lax.axis_index("section") // self.halves

    def half_block(self):
        return lax.axis_index("section") % self.halves * self.by_half // self.halves

    def cut_block(self, cut):
        return cut * self.by_cut // self.cuts


def sent(pieces, axis):
    arrived = [pieces[0]]
    for k, (route, _, _) in enumerate(peers(axis)):
        arrived.append(lax.ppermute(pieces[k + 1], axis, route))
    return arrived


def body(initial, sens, kspace, mask, step_sizes, conv_in, bias_in, conv_out):
    slabs, _, size_x, size_y, _, size_z = sens.shape
    sections, cuts = lax.axis_size("section"), lax.axis_size("cuts")
    place = Place(slabs, size_x)
    rows = size_y // cuts

    def joined(array):
        return array.reshape(array.shape[:-3] + (array.shape[-3] * 2, size_z))

    initial, sens, kspace = joined(initial), joined(sens), joined(kspace)
    sens_pieces = split(place, sens)
    senses = sent(sens_pieces, "coil")
    *terms, packed = adjoint(
        place, kspace, sens, initial, mask, conv_in[0], bias_in, conv_out[0], step_sizes
    )
    weights = sent([packed] * sections, "section")
    terms = sent(terms, "cuts")
    datas = sum_over_coils(terms)
    given = for_partners(place, senses)
    more = sent([None] + list(given), "cuts")[1:]
    first, planes = first_refine(terms, weights)
    coil_planes, normal = first_normal(place, planes, mask, senses, more)
    images = run_cascades(place, planes, first, normal, coil_planes, mask, weights, datas, cuts)
    images = sent(images, "cuts")
    pieces = by_section(images)
    pieces = sent(pieces, "section")
    out = arrange(place, pieces)
    return out.reshape(1, slabs, place.owned, rows, 2, size_z)


def solution(mesh):
    return jax.shard_map(
        body,
        mesh=mesh,
        in_specs=(
            P(None, "coil", "cuts", None, None),
            P(None, ("coil", "cuts"), None, None, None, None),
            P(None, ("coil", "cuts"), None, None, None, None),
            P(),
            P("section"),
            P("section", None, None),
            P("section", None),
            P("section", None, None),
        ),
        out_specs=P("section", None, "coil", "cuts", None, None),
        check_vma=False,
    )
```

```python
import functools
import math

import jax
import jax.numpy as jnp
import ml_dtypes
import numpy as np
from jax import lax
from jax.experimental import pallas as pl
from jax.experimental.pallas import tpu as pltpu
from jax.sharding import PartitionSpec as P


INTERPRET = False
BF16, F32 = jnp.bfloat16, jnp.float32
ACT = F32
GROUP = 4
TILE = 8


def dft_table(length, sign):
    ramp = np.arange(length)
    angle = (ramp[:, None] * ramp[None, :] % length) * (2.0 * math.pi / length)
    cosine = np.cos(angle) / math.sqrt(length)
    sine = sign * np.sin(angle) / math.sqrt(length)
    return np.block([[cosine, -sine], [sine, cosine]]).astype(ml_dtypes.bfloat16)


def peers(axis):
    count = lax.axis_size(axis)
    me = lax.axis_index(axis)
    for k in range(1, count):
        if count & (count - 1) == 0:
            yield [(j, j ^ k) for j in range(count)], jnp.bitwise_xor(me, k), jnp.bitwise_xor(me, k)
        else:
            route = [(j, (j + k) % count) for j in range(count)]
            yield route, (me + k) % count, (me - k) % count


def own_and_peers(axis):
    me = lax.axis_index(axis)
    yield None, me, me
    yield from peers(axis)


def step_to(index, axis):
    count = lax.axis_size(axis)
    me = lax.axis_index(axis)
    if count & (count - 1) == 0:
        return jnp.bitwise_xor(me, index)
    return (me - index) % count


SMEM = pl.BlockSpec(memory_space=pltpu.SMEM)
VMEM = pl.BlockSpec(memory_space=pltpu.VMEM)
ANY = pl.BlockSpec(memory_space=pl.ANY)


def far():
    return INTERPRET or lax.axis_size("coil") > 8


def near(x):
    return x if far() else pltpu.with_memory_space_constraint(x, pltpu.VMEM)


def away(x):
    return x if INTERPRET else pltpu.with_memory_space_constraint(x, pltpu.HBM)


def near_out(shape, dtype):
    return jax.ShapeDtypeStruct(shape, dtype) if far() else pltpu.VMEM(shape, dtype)


def kernel_params():
    return None if far() else pltpu.CompilerParams(vmem_limit_bytes=20 << 20)


def selections():
    chosen = np.zeros((4 * 4 * TILE + TILE, 42), np.float32)
    for dy in range(3):
        for dz in range(3):
            for part in range(2):
                tap = (3 * dy + dz) * 2 + part
                for row in range(2):
                    chosen[row * 32 + (row + dy) * TILE + dz * 2 + part, tap] = 0.5
                    chosen[64 + row * 32 + (row + 2 - dy) * TILE + dz * 2 + part, 21 + tap] = 1.0
    for row in range(2):
        for piece, at in enumerate((TILE + 6, TILE + 7, 2 * TILE + 6)):
            chosen[row * 32 + at, 18 + piece] = 0.5
    for piece in range(3):
        chosen[128 + piece, 39 + piece] = 1.0
    return chosen.astype(ml_dtypes.bfloat16)


def in_three(x):
    high = x.astype(BF16)
    rest = x - high.astype(F32)
    mid = rest.astype(BF16)
    return [high, mid, (rest - mid.astype(F32)).astype(BF16)]


def pack_into(packed, chosen, conv_in, bias, conv_out, step):
    def picked(rows, lanes):
        return jnp.dot(chosen[:, lanes], rows, preferred_element_type=F32)

    total = picked(conv_in[...], slice(0, 18)) + picked(conv_out[...], slice(21, 39))
    steps = jnp.full(bias.shape, step[0], F32)
    for at, split in ((18, in_three(bias[...])), (39, in_three(steps))):
        for piece, row in enumerate(split):
            column = chosen[:, at + piece : at + piece + 1].astype(F32)
            total += column * row.astype(F32)
    packed[...] = total.astype(BF16)


def shifted(plane, by, width):
    lane = lax.broadcasted_iota(jnp.int32, (plane.shape[0], width), 1)
    parts = []
    for at in range(0, plane.shape[1], width):
        moved = pltpu.roll(plane[:, at : at + width], (-by) % width, 1)
        parts.append(jnp.where((lane + by >= 0) & (lane + by < width), moved, 0.0))
    return jnp.concatenate(parts, axis=1)


def refine_into(planes, weights, scratch, result, width):
    rows, lanes = planes[0].shape
    taps_f32, taps, products, halves, hidden = scratch
    for dz in range(3):
        for part in range(2):
            plane = planes[part] if dz == 1 else shifted(planes[part], dz - 1, width)
            for s in range(lanes // width):
                place = pl.ds(TILE + dz * 2 + part, rows, stride=TILE)
                taps_f32.at[s][place, :] = plane[:, s * width : (s + 1) * width]
    for s in range(lanes // width):
        taps[:, s * width : (s + 1) * width] = taps_f32[s].astype(BF16)
    packed = weights.astype(F32)
    first = jnp.concatenate([packed[0:32].T, packed[32:64].T], axis=0).astype(BF16)
    second = jnp.concatenate([weights[64:96], weights[96:128]], axis=1)

    def start_of(j, g):
        start = (j * GROUP + g) * 2 * TILE
        return start if isinstance(start, int) else pl.multiple_of(start, 2 * TILE)

    def before(j, slot, g):
        window = taps[pl.ds(start_of(j, g), 4 * TILE), :]
        halves[slot, g] = jnp.dot(first, window, preferred_element_type=F32).astype(halves.dtype)

    def activate(slot, g):
        half = halves[slot, g]
        hidden[slot, g] = (half + half * jnp.tanh(half)).astype(BF16)

    def after(j, slot, g, carry):
        out = jnp.dot(second, hidden[slot, g], preferred_element_type=F32)
        done = out[: 2 * TILE] + carry
        for s in range(lanes // width):
            products.at[s][pl.ds(start_of(j, g), 2 * TILE), :] = done[:, s * width : (s + 1) * width]
        return out[2 * TILE :]

    blocks = rows // (2 * GROUP)
    for g in range(GROUP):
        before(0, 0, g)
    for g in range(GROUP):
        activate(0, g)
        before(1, 1, g)

    carry = jnp.zeros((2 * TILE, lanes), F32)
    for j in range(1, blocks + 1):
        for g in range(GROUP):
            carry = after(j - 1, (j - 1) % 2, g, carry)
            if j < blocks:
                activate(j % 2, g)
            if j + 1 < blocks:
                before(j + 1, (j + 1) % 2, g)
    last = carry
    for s in range(lanes // width):
        own = slice(s * width, (s + 1) * width)
        products.at[s][rows * TILE : (rows + 2) * TILE, :] = last[:, own]
        for part in range(2):
            total = products.at[s][pl.ds(TILE + 2 + part, rows, stride=TILE), :]
            for dz in (0, 2):
                total += shifted(products.at[s][pl.ds(TILE + dz * 2 + part, rows, stride=TILE), :], dz - 1, width)
            result[part, :, own] = total


def fill_ones(taps_f32):
    taps_f32[...] = jnp.zeros(taps_f32.shape, F32)
    slices, rows, width = taps_f32.shape
    for s in range(slices):
        for at in (6, 7):
            taps_f32.at[s][pl.ds(at, rows // TILE, stride=TILE), :] = jnp.ones((rows // TILE, width), F32)


def first_refine_kernel(n_rows, n_weights, *refs):
    pieces, weights = refs[:n_rows], refs[n_rows : n_rows + n_weights]
    refined, planes, stage = refs[n_rows + n_weights : n_rows + n_weights + 3]
    scratch = refs[n_rows + n_weights + 3 :]
    last, (per, _, block, width) = pieces[0].shape[0] - 1, pieces[0].shape[1:]
    fill_ones(scratch[0])
    for k, (_, _, source) in enumerate(own_and_peers("cuts")):
        for s in range(per):
            rows = pl.ds(pl.multiple_of(source * block, 16), block)
            stage.at[s][rows, :] = pieces[k][last, s, 0].astype(F32)
    height = stage.shape[1] // 2
    for s in range(per):
        for part in range(2):
            planes[part, :, s * width : (s + 1) * width] = stage.at[s][pl.ds(part, height, stride=2), :]
    refine_into([planes[0], planes[1]], of_cascade(weights, 0), scratch, refined, width)


def of_cascade(weights, cascade):
    at = step_to(cascade, "section")
    chosen = weights[0][...]
    for k in range(1, len(weights)):
        chosen = jnp.where(at == k, weights[k][...], chosen)
    return chosen


def subtract_normal(planes, coil_planes, weight_mask, tables, gradient, rows_y, rows_z):
    forward_z, back_z, forward_y, back_y = tables
    count, _, height, width = coil_planes.shape
    per = planes.shape[2] // width
    assert per <= 2
    pairs = count // 2

    def each_pair(step):
        lax.fori_loop(0, pairs, lambda m, _: step(m), None)

    def sens_and_lanes(m, i):
        n, s = 2 * m + i, i % per
        sens = coil_planes[n, 0], coil_planes[n, 1]
        return *sens, slice(s * width, (s + 1) * width)

    def product(m):
        coils = []
        for i in range(2):
            sr, si, lanes = sens_and_lanes(m, i)
            ir, ii = planes[0, :, lanes], planes[1, :, lanes]
            coils.append(jnp.concatenate([sr * ir - si * ii, sr * ii + si * ir], axis=1).astype(BF16))
        w = jnp.dot(jnp.concatenate(coils, axis=0), forward_z[...], preferred_element_type=F32)
        w = w.astype(BF16)
        for i in range(2):
            for part in range(2):
                block = w[i * height : (i + 1) * height, part * width : (part + 1) * width]
                rows_y[m, part * height : (part + 1) * height, i * width : (i + 1) * width] = block

    def forward(m):
        w = jnp.dot(forward_y[...], rows_y[m], preferred_element_type=F32)
        for i in range(2):
            lanes = slice(i * width, (i + 1) * width)
            rows_y[m, :, lanes] = (w[:, lanes] * weight_mask).astype(BF16)

    def back(m):
        w = jnp.dot(back_y[...], rows_y[m], preferred_element_type=F32).astype(BF16)
        for i in range(2):
            for part in range(2):
                block = w[part * height : (part + 1) * height, i * width : (i + 1) * width]
                rows_z[m, i * height : (i + 1) * height, part * width : (part + 1) * width] = block

    def gather(m):
        w = jnp.dot(rows_z[m], back_z[...], preferred_element_type=F32)
        for i in range(2):
            sr, si, lanes = sens_and_lanes(m, i)
            br = w[i * height : (i + 1) * height, :width]
            bi = w[i * height : (i + 1) * height, width:]
            gradient[0, :, lanes] -= sr * br + si * bi
            gradient[1, :, lanes] -= sr * bi - si * br

    if pairs > 8:
        return [functools.partial(each_pair, stage) for stage in (product, forward, back, gather)]
    return [functools.partial(stage, m) for stage in (product, forward, back, gather) for m in range(pairs)]


def mask_of(place, mask):
    weight_mask = mask[place.slab()].astype(F32)
    return jnp.concatenate([weight_mask] * 2, axis=0)


def first_normal_kernel(place, n_sens, planes, mask, *refs):
    tables, senses, more = refs[:4], refs[4 : 4 + n_sens], refs[4 + n_sens : -5]
    coil_planes, normal, rows_y, rows_z, stage = refs[-5:]
    height = coil_planes.shape[2]

    def keep(n, rows):
        slot = stage.at[n % stage.shape[0]]
        slot[...] = rows.astype(F32)
        for part in range(2):
            coil_planes[n, part] = slot[pl.ds(part, height, stride=2), :]

    start = place.cut_block(lax.axis_index("cuts")) * place.per
    n = 0
    for ref in senses:
        for s in range(place.per):
            keep(n, ref[start + s])
            n += 1
    for ref in more:
        for q in range(ref.shape[0]):
            for s in range(place.per):
                keep(n, ref[q, s])
                n += 1
    normal[...] = jnp.zeros(normal.shape, F32)
    for step in subtract_normal(planes, coil_planes, mask_of(place, mask), tables, normal, rows_y, rows_z):
        step()


def cascades_kernel(place, n_weights, n_data, *refs):
    planes_in, first, normal, coil_planes, mask = refs[:5]
    tables, at = refs[5:9], 9
    weights, at = refs[at : at + n_weights], at + n_weights
    datas, at = refs[at : at + n_data], at + n_data
    cuts = lax.axis_size("cuts")
    outs = refs[at : at + cuts]
    scratch = refs[at + cuts : -8]
    refined, planes, data, gradient, rows_y, rows_z, stage, all_weights = refs[-8:]
    per, _, height, width = datas[0].shape
    cascades = len(weights)
    fill_ones(scratch[0])
    refined[...] = first[...]
    planes[...] = planes_in[...]
    for k in range(cascades):
        all_weights[k] = weights[k][...]
    for s in range(per):
        for part in range(2):
            data[part, :, s * width : (s + 1) * width] = sum(d[s, part].astype(F32) for d in datas)
    gradient[...] = data[...] + normal[...]
    weight_mask = mask_of(place, mask)

    def cascade(c, _):
        now = all_weights.at[step_to(c, "section")]
        step = sum(now[128 + piece : 129 + piece, 0:1].astype(F32) for piece in range(3))
        for part in range(2):
            new = (planes[part] - step * gradient[part] + refined[part]).astype(BF16).astype(F32)
            planes[part] = new
            for s in range(per):
                stage.at[s][pl.ds(part, height, stride=2), :] = new[:, s * width : (s + 1) * width]
        block = 2 * height // cuts
        for k, (_, target, _) in enumerate(own_and_peers("cuts")):
            for s in range(per):
                rows = stage.at[s][pl.ds(pl.multiple_of(target * block, 16), block), :]
                outs[k][step_to(c, "section"), s] = rows.astype(BF16)

        @pl.when(c + 1 < cascades)
        def _():
            following = all_weights[step_to(c + 1, "section")]
            refine_into([planes[0], planes[1]], following, scratch, refined, width)
            gradient[...] = data[...]
            for take in subtract_normal(
                planes, coil_planes, weight_mask, tables, gradient, rows_y, rows_z
            ):
                take()

    lax.fori_loop(0, cascades, cascade, None)


def refine_scratch(height, per, width, hid):
    rows, lanes = (height + 2) * TILE, per * width
    assert height % (4 * GROUP) == 0
    return [
        pltpu.VMEM((per, rows, width), F32),
        pltpu.VMEM((rows, lanes), BF16),
        pltpu.VMEM((per, rows, width), F32),
        pltpu.VMEM((2, GROUP, 2 * hid, lanes), ACT),
        pltpu.VMEM((2, GROUP, 2 * hid, lanes), BF16),
    ]


def first_refine(pieces, weights):
    per, _, block, width = pieces[0].shape[1:]
    rows = block * len(pieces)
    plane = near_out((2, rows // 2, per * width), F32)
    return pl.pallas_call(
        functools.partial(first_refine_kernel, len(pieces), len(weights)),
        out_shape=(plane, plane),
        in_specs=[VMEM] * (len(pieces) + len(weights)),
        out_specs=(VMEM, VMEM),
        scratch_shapes=[pltpu.VMEM((per, rows, width), F32)]
        + refine_scratch(rows // 2, per, width, weights[0].shape[-1]),
        compiler_params=kernel_params(),
        interpret=INTERPRET,
    )(*[near(x) for x in [*pieces, *weights]])


def pass_tables(height, width):
    tables = [
        dft_table(width, 1.0),
        dft_table(width, -1.0),
        dft_table(height, 1.0).T.copy(),
        dft_table(height, -1.0).T.copy(),
    ]
    return [near(jnp.asarray(t)) for t in tables]


def pass_scratch(count, height, width):
    return [
        pltpu.VMEM((count // 2, 2 * height, 2 * width), BF16),
        pltpu.VMEM((count // 2, 2 * height, 2 * width), BF16),
    ]


def first_normal(place, planes, mask, senses, more):
    _, height, lanes = planes.shape
    width = senses[0].shape[-1]
    count = place.per * (len(senses) + sum(m.shape[0] for m in more))
    args = [planes, mask] + pass_tables(height, width) + list(senses) + list(more)
    return pl.pallas_call(
        functools.partial(first_normal_kernel, place, len(senses)),
        out_shape=[near_out((count, 2, height, width), F32), near_out((2, height, lanes), F32)],
        in_specs=[VMEM] * len(args),
        out_specs=[VMEM] * 2,
        scratch_shapes=pass_scratch(count, height, width) + [pltpu.VMEM((4, 2 * height, width), F32)],
        compiler_params=kernel_params(),
        interpret=INTERPRET,
    )(*[near(x) for x in args])


def run_cascades(place, planes, first, normal, coil_planes, mask, weights, datas, cuts):
    per, _, height, width = datas[0].shape
    lanes = per * width
    count = coil_planes.shape[0]
    args = [planes, first, normal, coil_planes, mask] + pass_tables(height, width)
    args += list(weights) + list(datas)
    return pl.pallas_call(
        functools.partial(cascades_kernel, place, len(weights), len(datas)),
        out_shape=[near_out((len(weights), per, 2 * height // cuts, width), BF16)] * cuts,
        in_specs=[VMEM] * len(args),
        out_specs=[VMEM] * cuts,
        scratch_shapes=refine_scratch(height, per, width, weights[0].shape[-1])
        + [pltpu.VMEM((2, height, lanes), F32)] * 4
        + pass_scratch(count, height, width)
        + [
            pltpu.VMEM((per, 2 * height, width), F32),
            pltpu.VMEM((len(weights),) + weights[0].shape, BF16),
        ],
        compiler_params=kernel_params(),
        interpret=INTERPRET,
    )(*[near(x) for x in args])


def split_kernel(place, sens, *refs):
    outs, sems = refs[:-1], refs[-1]
    start = place.half_block() * place.run
    copies = []
    for k, (_, target, _) in enumerate(own_and_peers("coil")):
        source = sens.at[place.slab(), 0, pl.ds(target * place.owned + start, place.run)]
        copies.append(pltpu.make_async_copy(source, outs[k], sems.at[k]))
    for copy in copies:
        copy.start()
    for copy in copies:
        copy.wait()


def split(place, sens):
    coils = lax.axis_size("coil")
    return pl.pallas_call(
        functools.partial(split_kernel, place),
        out_shape=[near_out((place.run,) + sens.shape[-2:], BF16)] * coils,
        in_specs=[ANY],
        out_specs=[VMEM] * coils,
        scratch_shapes=[pltpu.SemaphoreType.DMA((coils,))],
        compiler_params=kernel_params(),
        interpret=INTERPRET,
    )(away(sens))


def partners_kernel(place, *refs):
    coils = lax.axis_size("coil")
    senses, outs = refs[:coils], refs[coils:]
    for k, (_, target, _) in enumerate(peers("cuts")):
        for q in range(coils):
            outs[k][q] = senses[q][pl.ds(place.cut_block(target) * place.per, place.per)]


def for_partners(place, senses):
    coils, cuts = lax.axis_size("coil"), lax.axis_size("cuts")
    outs = [near_out((coils, place.per) + senses[0].shape[-2:], BF16)] * (cuts - 1)
    return pl.pallas_call(
        functools.partial(partners_kernel, place),
        out_shape=outs,
        in_specs=[VMEM] * coils,
        out_specs=[VMEM] * len(outs),
        compiler_params=kernel_params(),
        interpret=INTERPRET,
    )(*[near(x) for x in senses])


CHUNKS = 4


def adjoint_kernel(place, n_small, kspace, sens, initial, mask, tables_x, back_y, back_z, *refs):
    coils, cuts = lax.axis_size("coil"), lax.axis_size("cuts")
    small, step, refs = refs[:n_small], refs[n_small], refs[n_small + 1 :]
    outs, packed, refs = refs[:cuts], refs[cuts], refs[cuts + 1 :]
    held, refs = refs[:n_small], refs[n_small:]
    data, own_sens, table_x, planes, rows_z, stage, sems = refs
    size_x, rows, width = data.shape
    height = rows // 2
    kept = coils * place.run
    slab, block = place.slab(), place.half_block()
    chunk = size_x // CHUNKS
    first_small = 1 + CHUNKS + coils + cuts * place.per
    packing = [
        pltpu.make_async_copy(source, target, sems.at[first_small + k])
        for k, (source, target) in enumerate(zip(small, held))
    ]
    copies = [pltpu.make_async_copy(tables_x.at[block], table_x, sems.at[0])]
    for i in range(CHUNKS):
        at = pl.ds(i * chunk, chunk)
        copies.append(pltpu.make_async_copy(kspace.at[slab, 0, at], data.at[at], sems.at[1 + i]))
    first_sens = len(copies)
    for q in range(coils):
        source = sens.at[slab, 0, pl.ds(q * place.owned + block * place.run, place.run)]
        target = own_sens.at[pl.ds(q * place.run, place.run)]
        copies.append(pltpu.make_async_copy(source, target, sems.at[first_sens + q]))
    for k, (_, target, _) in enumerate(own_and_peers("cuts")):
        for s in range(place.per):
            n = block * place.run + place.cut_block(target) * place.per + s
            sem = sems.at[first_sens + coils + k * place.per + s]
            copies.append(pltpu.make_async_copy(initial.at[slab, n], outs[k].at[coils, s, 0], sem))
    for copy in packing + copies:
        copy.start()
    for copy in packing:
        copy.wait()
    pack_into(packed, *held, step)
    for copy in copies[:first_sens]:
        copy.wait()
    weight_mask = mask[slab].astype(F32)
    groups = rows // (2 * TILE)
    for g in range(0, groups, 2):
        both = [
            data[:, (g + i) * 2 * TILE : (g + i + 1) * 2 * TILE, :].reshape(size_x * 2 * TILE, width)
            for i in range(2)
        ]
        w = jnp.dot(table_x[...], jnp.concatenate(both, axis=1), preferred_element_type=F32)
        for i in range(2):
            at = slice((g + i) * TILE, (g + i + 1) * TILE)
            part = w[:, i * width : (i + 1) * width].reshape(2 * kept, TILE, width)
            planes[:, at, :] = part * weight_mask[at][None]
    for n in range(0, kept, 2):
        pair = [
            jnp.concatenate([planes[2 * (n + i)], planes[2 * (n + i) + 1]], axis=0).astype(BF16)
            for i in range(2)
        ]
        w = jnp.dot(back_y[...], jnp.concatenate(pair, axis=1), preferred_element_type=F32).astype(BF16)
        for i in range(2):
            lanes = slice(i * width, (i + 1) * width)
            rows_z[n + i] = jnp.concatenate([w[:height, lanes], w[height:, lanes]], axis=1)
    for copy in copies[first_sens:]:
        copy.wait()
    for k, (_, target, _) in enumerate(own_and_peers("cuts")):
        outs[k][coils, :, 1] = jnp.zeros((place.per, height, width), BF16)
        for q in range(coils):
            for s in range(place.per):
                n = q * place.run + place.cut_block(target) * place.per + s
                w = jnp.dot(rows_z[n], back_z[...], preferred_element_type=F32)
                br, bi = w[:, :width], w[:, width:]
                slot = stage.at[(q * place.per + s) % stage.shape[0]]
                slot[...] = own_sens[n].astype(F32)
                sr, si = (slot[pl.ds(part, height, stride=2), :] for part in range(2))
                outs[k][q, s, 0] = (sr * br + si * bi).astype(BF16)
                outs[k][q, s, 1] = (sr * bi - si * br).astype(BF16)


def adjoint(place, kspace, sens, initial, mask, conv_in, bias, conv_out, step):
    coils, cuts = lax.axis_size("coil"), lax.axis_size("cuts")
    size_x, rows, width = kspace.shape[-3:]
    height = rows // 2
    kept = coils * place.run
    assert initial.shape[-2] == height
    chosen = jnp.asarray(selections())
    small = [chosen, conv_in.T, bias, conv_out]
    table = dft_table(size_x, -1.0).reshape(2, size_x, 2, coils, place.by_half, place.run)
    table = np.einsum("cxdqbr,uv->bqrduxvc", table.astype(np.float32), np.eye(TILE, dtype=np.float32))
    table = table.reshape(place.by_half, 2 * kept * TILE, 2 * size_x * TILE).astype(ml_dtypes.bfloat16)
    tables = [jnp.asarray(t) for t in (table, dft_table(height, -1.0).T.copy(), dft_table(width, -1.0))]
    return pl.pallas_call(
        functools.partial(adjoint_kernel, place, len(small)),
        out_shape=[near_out((coils + 1, place.per, 2, height, width), BF16)] * cuts
        + [near_out((chosen.shape[0], bias.shape[1]), BF16)],
        in_specs=[ANY, ANY, ANY, VMEM, ANY, VMEM, VMEM] + [ANY] * len(small) + [SMEM],
        out_specs=[VMEM] * (cuts + 1),
        scratch_shapes=[pltpu.VMEM(x.shape, x.dtype) for x in small]
        + [
            pltpu.VMEM((size_x, rows, width), BF16),
            pltpu.VMEM((kept, rows, width), BF16),
            pltpu.VMEM(table.shape[1:], BF16),
            pltpu.VMEM((2 * kept, height, width), F32),
            pltpu.VMEM((kept, height, 2 * width), BF16),
            pltpu.VMEM((4, rows, width), F32),
            pltpu.SemaphoreType.DMA((1 + CHUNKS + coils + cuts * place.per + len(small),)),
        ],
        compiler_params=kernel_params(),
        interpret=INTERPRET,
    )(
        *[away(x) for x in (kspace, sens, initial)],
        near(mask),
        away(tables[0]),
        near(tables[1]),
        near(tables[2]),
        *[away(x) for x in small],
        step,
    )


def halve_kernel(n_in, bit, *refs):
    terms, (kept, given) = refs[:n_in], refs[n_in:]
    mine = lax.axis_index("coil") // (1 << bit) % 2
    for j in range(kept.shape[0]):
        for out, target in ((kept, 2 * j + mine), (given, 2 * j + 1 - mine)):
            out[j] = sum(t[target].astype(F32) for t in terms).astype(BF16)


def halve(terms, bit):
    count = terms[0].shape[0] // 2 * 2
    return pl.pallas_call(
        functools.partial(halve_kernel, len(terms), bit),
        out_shape=[near_out((count // 2,) + terms[0].shape[1:], BF16)] * 2,
        in_specs=[VMEM] * len(terms),
        out_specs=[VMEM] * 2,
        compiler_params=kernel_params(),
        interpret=INTERPRET,
    )(*[near(t) for t in terms])


def sum_over_coils(terms):
    coils = lax.axis_size("coil")
    assert coils & (coils - 1) == 0
    for bit in range(coils.bit_length() - 1):
        kept, given = halve(terms, bit)
        route = [(j, j ^ (1 << bit)) for j in range(coils)]
        terms = [kept, lax.ppermute(given, "coil", route)]
    return [t[0] for t in terms]


def by_section_kernel(n_in, *refs):
    images, outs = refs[:n_in], refs[n_in:]
    for k, (_, _, source) in enumerate(own_and_peers("cuts")):
        for section, out in enumerate(outs):
            out[source] = images[k][section]


def by_section(images):
    sections = images[0].shape[0]
    return pl.pallas_call(
        functools.partial(by_section_kernel, len(images)),
        out_shape=[near_out((len(images),) + images[0].shape[1:], BF16)] * sections,
        in_specs=[VMEM] * len(images),
        out_specs=[VMEM] * sections,
        compiler_params=kernel_params(),
        interpret=INTERPRET,
    )(*[near(x) for x in images])


def arrange_kernel(place, *refs):
    pieces, out = refs[:-1], refs[-1]
    for k, (_, _, source) in enumerate(own_and_peers("section")):
        slab = source // place.halves
        start = source % place.halves * place.by_half // place.halves * place.run
        for cut in range(place.cuts):
            at = start + place.cut_block(cut) * place.per
            out[slab, pl.ds(at, place.per)] = pieces[k][cut]


def arrange(place, pieces):
    return pl.pallas_call(
        functools.partial(arrange_kernel, place),
        out_shape=jax.ShapeDtypeStruct((place.slabs, place.owned) + pieces[0].shape[2:], BF16),
        in_specs=[VMEM] * len(pieces),
        out_specs=VMEM,
        compiler_params=kernel_params(),
        interpret=INTERPRET,
    )(*[near(x) for x in pieces])


class Place:
    def __init__(self, slabs, size_x):
        sections, coils, cuts = (lax.axis_size(a) for a in ("section", "coil", "cuts"))
        self.slabs, self.cuts, self.halves = slabs, cuts, sections // slabs
        self.owned = size_x // coils
        self.by_half = math.gcd(self.owned, self.halves)
        self.by_cut = math.gcd(self.owned // self.by_half, cuts)
        self.per = self.owned // (self.by_half * self.by_cut)
        self.run = self.by_cut * self.per

    def slab(self):
        return lax.axis_index("section") // self.halves

    def half_block(self):
        return lax.axis_index("section") % self.halves * self.by_half // self.halves

    def cut_block(self, cut):
        return cut * self.by_cut // self.cuts


def sent(pieces, axis):
    arrived = [pieces[0]]
    for k, (route, _, _) in enumerate(peers(axis)):
        arrived.append(lax.ppermute(pieces[k + 1], axis, route))
    return arrived


def body(initial, sens, kspace, mask, step_sizes, conv_in, bias_in, conv_out):
    slabs, _, size_x, size_y, _, size_z = sens.shape
    sections, cuts = lax.axis_size("section"), lax.axis_size("cuts")
    place = Place(slabs, size_x)
    rows = size_y // cuts

    def joined(array):
        return array.reshape(array.shape[:-3] + (array.shape[-3] * 2, size_z))

    initial, sens, kspace = joined(initial), joined(sens), joined(kspace)
    sens_pieces = split(place, sens)
    senses = sent(sens_pieces, "coil")
    *terms, packed = adjoint(
        place, kspace, sens, initial, mask, conv_in[0], bias_in, conv_out[0], step_sizes
    )
    weights = sent([packed] * sections, "section")
    terms = sent(terms, "cuts")
    datas = sum_over_coils(terms)
    given = for_partners(place, senses)
    more = sent([None] + list(given), "cuts")[1:]
    first, planes = first_refine(terms, weights)
    coil_planes, normal = first_normal(place, planes, mask, senses, more)
    images = run_cascades(place, planes, first, normal, coil_planes, mask, weights, datas, cuts)
    images = sent(images, "cuts")
    pieces = by_section(images)
    pieces = sent(pieces, "section")
    out = arrange(place, pieces)
    return out.reshape(1, slabs, place.owned, rows, 2, size_z)


def solution(mesh):
    return jax.shard_map(
        body,
        mesh=mesh,
        in_specs=(
            P(None, "coil", "cuts", None, None),
            P(None, ("coil", "cuts"), None, None, None, None),
            P(None, ("coil", "cuts"), None, None, None, None),
            P(),
            P("section"),
            P("section", None, None),
            P("section", None),
            P("section", None, None),
        ),
        out_specs=P("section", None, "coil", "cuts", None, None),
        check_vma=False,
    )
```
